128 devices in a mesh: row: 16 (over z, x), col: 8 (over y, core).
Axes of the slice: x: 4, y: 4, z: 4, core: 2. Of those that a mesh axis runs over, the one named last changes fastest.
Arguments:
- measured: bfloat16 [512, 32, 16, 512], P('col', 'row'), may hold values from 0 to 2
- module_row: int32 [32], replicated, may hold values from 0 to 31, each once
- scan_offsets: int32 [16, 8, 4, 2], P('row', 'col'), may hold values from 0 to 511, as said below
- specimen: float32 [2, 4096, 4096], P(None, 'row', 'col'), may hold values from -9.3 to 9.3
- illumination: float32 [2, 512, 512], replicated, may hold values from -4 to 4
Outputs:
- specimen_step: float32 [2, 4096, 4096], P(None, 'row', 'col')
- illumination_step: float32 [2, 512, 512], replicated
The draws below stay inside these ranges and needn't reach their ends.
Inputs may be any that keep to these rules, and one draw needn't show every extreme that they name: `scan_offsets`: position s of a device's tile has row offset in [0, 256) and column offset in [s * 128, (s + 1) * 128).
All inputs are finite; a program needn't handle non-finite values.
Results may differ from the reference program's by a relative error of at most 0.002.
The reference program's roundings to bfloat16 on the way count: a program that leaves them out, or rounds other values in their place, can miss the bound.
Values may be sent and summed in bfloat16 or wider, within the bound.
No kernel may reach another device: no remote copies, remote signals or barrier semaphores. Data moves between devices by JAX's collectives and lax.ppermute only.
A program may use at most 128 MiB of HBM per device.

```python
import math
import jax
import jax.numpy as jnp
from jax import lax

FRAME = 512
MODULES = 32
SLOTS = 4
TY = 256
TX = 512
MROWS = 16
NOY = 4096
NOX = 4096
POSITIONS = 512
N_ROW = 16
N_COL = 8


def draw_scan_offsets(key, part):
    first, second = jax.random.split(key)
    rows_part = jax.random.randint(first, (N_ROW, N_COL, SLOTS), 0, TY, dtype=jnp.int32)
    width = TX // SLOTS
    cols_part = jax.random.randint(second, (N_ROW, N_COL, SLOTS), 0, width, dtype=jnp.int32)
    rows_part = rows_part.at[0, 0, 0].set(TY - 1)
    cols_part = cols_part.at[0, 0, 0].set(0)
    cols_part = cols_part.at[N_ROW - 1, N_COL - 1, SLOTS - 1].set(width - 1)
    cols_part = cols_part + jnp.arange(SLOTS, dtype=jnp.int32)[None, None, :] * width
    return jnp.stack([rows_part, cols_part], axis=-1)


def draw_specimen(key, part):
    first, second = jax.random.split(key)
    scale = jnp.exp(jax.random.uniform(first, (NOY, NOX), jnp.float32, -1.2, 1.2))
    values = 0.7 * jnp.clip(jax.random.normal(second, (2, NOY, NOX), jnp.float32), -4.0, 4.0)
    return values * scale[None]


def level_of(own_key, dims, cuts, least, top_value):
    def one(axis_at, blocks):
        steps = jax.random.uniform(jax.random.fold_in(jax.random.fold_in(own_key, 6), axis_at), (blocks,), jnp.float32, least / len(cuts), top_value / len(cuts))
        return jnp.repeat(jnp.exp(steps), dims[axis_at] // blocks).reshape((-1,) + (1,) * (len(dims) - axis_at - 1))

    level = one(*cuts[0])
    for cut in cuts[1:]:
        level = level * one(*cut)
    return level


def normal_values(stream_key, shape, spread, most, kind=jnp.bfloat16):
    drawn = jax.random.normal(stream_key, shape, jnp.float32) * spread
    return jnp.minimum(jnp.maximum(drawn, -most), most).astype(kind)


def setup_inputs(seed: int = 0) -> dict:
    key_list = jax.random.split(jax.random.key(seed), 6)
    measured = jnp.clip(2.0 * jax.random.uniform(key_list[0], (POSITIONS, MODULES, MROWS, FRAME), jnp.float32) ** level_of(key_list[0], (POSITIONS, MODULES, MROWS, FRAME), ((0, 8), (1, 16)), -0.2, 0.2), 0.0, 2.0).astype(jnp.bfloat16)
    module_row = jax.random.permutation(key_list[1], MODULES).astype(jnp.int32)
    scan_offsets = draw_scan_offsets(jax.random.fold_in(key_list[5], 71), 0)
    specimen = draw_specimen(jax.random.fold_in(key_list[5], 71), 0)
    illumination = normal_values(key_list[4], (2, FRAME, FRAME), 0.7, 4.0, jnp.float32)
    return {"measured": measured, "module_row": module_row, "scan_offsets": scan_offsets, "specimen": specimen, "illumination": illumination}


def dft_tables(size):
    index = jnp.arange(size, dtype=jnp.int32)
    wrapped = index[:, None] * index[None, :] % size
    angle = wrapped.astype(jnp.float32) * (2.0 * math.pi / size)
    norm = 1.0 / math.sqrt(size)
    return ((jnp.cos(angle) * norm).astype(jnp.bfloat16), (-jnp.sin(angle) * norm).astype(jnp.bfloat16))

def mdot(left, right):
    return jnp.dot(left, right, preferred_element_type=jnp.float32)

def reference(measured, module_row, scan_offsets, specimen, illumination):
    inverse = jnp.zeros((MODULES,), jnp.int32).at[module_row].set(jnp.arange(MODULES, dtype=jnp.int32))
    amplitude = jnp.take(measured, inverse, axis=1).reshape(POSITIONS, FRAME, FRAME)
    rows_index = jnp.arange(N_ROW, dtype=jnp.int32)
    cols_index = jnp.arange(N_COL, dtype=jnp.int32)
    offsets = jnp.transpose(scan_offsets, (1, 0, 2, 3))
    anchor_rows = (rows_index[None, :, None] * TY + offsets[..., 0]).reshape(POSITIONS).astype(jnp.int32)
    anchor_cols = (cols_index[:, None, None] * TX + offsets[..., 1]).reshape(POSITIONS).astype(jnp.int32)
    wide = jnp.concatenate([specimen, specimen[:, :, :FRAME]], axis=2)
    wide = jnp.concatenate([wide, wide[:, :FRAME]], axis=1)
    cos_table, sin_table = dft_tables(FRAME)
    ill_real = illumination[0]
    ill_imag = illumination[1]
    zero = jnp.zeros((), jnp.int32)

    def one_position(carry, inputs):
        accum, num_real, num_imag, density = carry
        amp, row_at, col_at = inputs
        patch = lax.dynamic_slice(wide, (zero, row_at, col_at), (2, FRAME, FRAME))
        spec_real = patch[0]
        spec_imag = patch[1]
        wave_real = (ill_real * spec_real - ill_imag * spec_imag).astype(jnp.bfloat16)
        wave_imag = (ill_real * spec_imag + ill_imag * spec_real).astype(jnp.bfloat16)
        half_real = (mdot(cos_table, wave_real) - mdot(sin_table, wave_imag)).astype(jnp.bfloat16)
        half_imag = (mdot(cos_table, wave_imag) + mdot(sin_table, wave_real)).astype(jnp.bfloat16)
        far_real = mdot(half_real, cos_table) - mdot(half_imag, sin_table)
        far_imag = mdot(half_real, sin_table) + mdot(half_imag, cos_table)
        magnitude = jnp.sqrt(far_real * far_real + far_imag * far_imag)
        factor = amp.astype(jnp.float32) / jnp.maximum(magnitude, 0.25) - 1.0
        corr_real = (factor * far_real).astype(jnp.bfloat16)
        corr_imag = (factor * far_imag).astype(jnp.bfloat16)
        back_real = (mdot(cos_table, corr_real) + mdot(sin_table, corr_imag)).astype(jnp.bfloat16)
        back_imag = (mdot(cos_table, corr_imag) - mdot(sin_table, corr_real)).astype(jnp.bfloat16)
        chg_real = mdot(back_real, cos_table) + mdot(back_imag, sin_table)
        chg_imag = mdot(back_imag, cos_table) - mdot(back_real, sin_table)
        grad = jnp.stack([ill_real * chg_real + ill_imag * chg_imag, ill_real * chg_imag - ill_imag * chg_real])
        current = lax.dynamic_slice(accum, (zero, row_at, col_at), (2, FRAME, FRAME))
        accum = lax.dynamic_update_slice(accum, current + grad, (zero, row_at, col_at))
        num_real = num_real + spec_real * chg_real + spec_imag * chg_imag
        num_imag = num_imag + spec_real * chg_imag - spec_imag * chg_real
        density = density + spec_real * spec_real + spec_imag * spec_imag
        return ((accum, num_real, num_imag, density), None)
    start = (jnp.zeros((2, NOY + FRAME, NOX + FRAME), jnp.float32), jnp.zeros((FRAME, FRAME), jnp.float32), jnp.zeros((FRAME, FRAME), jnp.float32), jnp.zeros((FRAME, FRAME), jnp.float32))
    (accum, num_real, num_imag, density), _ = lax.scan(one_position, start, (amplitude, anchor_rows, anchor_cols))
    specimen_step = accum[:, :NOY, :NOX]
    specimen_step = specimen_step.at[:, :FRAME, :].add(accum[:, NOY:, :NOX])
    specimen_step = specimen_step.at[:, :, :FRAME].add(accum[:, :NOY, NOX:])
    specimen_step = specimen_step.at[:, :FRAME, :FRAME].add(accum[:, NOY:, NOX:])
    root = jnp.sqrt(density + 1e-06)
    illumination_step = jnp.stack([num_real / root, num_imag / root])
    return (specimen_step, illumination_step)
```

```python
import functools
import math

import jax
import jax.numpy as jnp
from jax import lax
from jax.experimental import pallas as pl
from jax.experimental.pallas import tpu as pltpu
from jax.sharding import PartitionSpec as P

LANES = 128
SUBLANES = 8
CHUNK = 32
BLOCK = 256


def passed_along(value, axis, steps):
    count = lax.axis_size(axis)
    pairs = [(source, (source + steps) % count) for source in range(count)]
    return lax.ppermute(value, axis, pairs)


def passed_both(value, row_steps, col_steps):
    rows, cols = lax.axis_size("row"), lax.axis_size("col")
    pairs = [
        (row * cols + col, (row + row_steps) % rows * cols + (col + col_steps) % cols)
        for row in range(rows)
        for col in range(cols)
    ]
    return lax.ppermute(value, ("row", "col"), pairs)


def dft_tables(size):
    index = jnp.arange(size, dtype=jnp.int32)
    wrapped = index[:, None] * index[None, :] % size
    angle = wrapped.astype(jnp.float32) * (2.0 * math.pi / size)
    norm = 1.0 / math.sqrt(size)
    return (
        (jnp.cos(angle) * norm).astype(jnp.bfloat16),
        (-jnp.sin(angle) * norm).astype(jnp.bfloat16),
    )


def narrowed(value):
    peak = jnp.maximum(jnp.max(jnp.abs(value)), 1e-30)
    scaled = (value * (32768.0 / peak)).astype(jnp.float16)
    return scaled, (peak * (1.0 / 32768.0)).reshape(1, 1)


def widened(value, unit):
    return value.astype(jnp.float32) * unit[0, 0]


def gather_rows(ref, plane, start, rows, col, shift):
    tiles = rows // SUBLANES + 1
    block = ref[plane, pl.ds(start, tiles * SUBLANES), pl.ds(col, LANES)]
    block = block.reshape(tiles, SUBLANES, LANES)
    rolled = pltpu.roll(block, (SUBLANES - shift) % SUBLANES, axis=1)
    sub = lax.broadcasted_iota(jnp.int32, (tiles - 1, SUBLANES, LANES), 1)
    return jnp.where(sub < SUBLANES - shift, rolled[:-1], rolled[1:]).reshape(rows, LANES)


def forward_kernel(offs, region, ill, left, right, far, patch, density, wave, half):
    slot = pl.program_id(0)
    size = ill.shape[-1]
    row = offs[slot, 0]
    base = slot * LANES
    lane_shift = offs[slot, 1] % LANES
    row_shift = row % SUBLANES
    row_base = row - row_shift
    lane = lax.broadcasted_iota(jnp.int32, (CHUNK, LANES), 1)
    blocks = size // LANES

    @pl.when(slot == 0)
    def _():
        density[...] = jnp.zeros_like(density)

    def extract(step, carry):
        at = pl.multiple_of(step * CHUNK, CHUNK)
        start = pl.multiple_of(row_base + at, SUBLANES)
        last = [None, None]
        for block in range(blocks + 1):
            col = pl.multiple_of(base + block * LANES, LANES)
            now = [
                pltpu.roll(
                    gather_rows(region, plane, start, CHUNK, col, row_shift),
                    (LANES - lane_shift) % LANES,
                    axis=1,
                )
                for plane in range(2)
            ]
            if block > 0:
                to = slice((block - 1) * LANES, block * LANES)
                spec_real, spec_imag = (
                    jnp.where(lane < LANES - lane_shift, last[plane], now[plane])
                    for plane in range(2)
                )
                patch[0, 0, pl.ds(at, CHUNK), to] = spec_real
                patch[0, 1, pl.ds(at, CHUNK), to] = spec_imag
                ill_real = ill[0, pl.ds(at, CHUNK), to]
                ill_imag = ill[1, pl.ds(at, CHUNK), to]
                wave[pl.ds(at, CHUNK), to] = (
                    ill_real * spec_real - ill_imag * spec_imag
                ).astype(jnp.bfloat16)
                wave[pl.ds(size + at, CHUNK), to] = (
                    ill_real * spec_imag + ill_imag * spec_real
                ).astype(jnp.bfloat16)
                density[pl.ds(at, CHUNK), to] += spec_real * spec_real + spec_imag * spec_imag
            last = now
        return carry

    lax.fori_loop(0, size // CHUNK, extract, 0)
    for block in range(size // BLOCK):
        to = slice(block * BLOCK, (block + 1) * BLOCK)
        also = slice(size + block * BLOCK, size + (block + 1) * BLOCK)
        product = jnp.dot(left[...], wave[:, to], preferred_element_type=jnp.float32)
        half[:, to] = product[:size].astype(jnp.bfloat16)
        half[:, also] = product[size:].astype(jnp.bfloat16)
    for plane in range(2):
        for block in range(size // BLOCK):
            to = slice(block * BLOCK, (block + 1) * BLOCK)
            of = slice(plane * size + block * BLOCK, plane * size + (block + 1) * BLOCK)
            far[0, plane, :, to] = jnp.dot(
                half[...], right[:, of], preferred_element_type=jnp.float32
            )


def backward_kernel(
    offs, order, far, patch, amp, ill, left, right, accum, numer, corr, back, change, inverse
):
    slot = pl.program_id(0)
    size = ill.shape[-1]
    modules = size // amp.shape[3]
    senders = amp.shape[0]
    row = offs[slot, 0]
    base = slot * LANES
    lane_shift = offs[slot, 1] % LANES
    row_shift = row % SUBLANES
    row_base = row - row_shift
    blocks = size // LANES
    height = amp.shape[3]
    per = amp.shape[2]

    @pl.when(slot == 0)
    def _():
        numer[...] = jnp.zeros_like(numer)

        def clear(step, carry):
            at = pl.multiple_of(step * CHUNK, CHUNK)
            accum[:, pl.ds(at, CHUNK), :] = jnp.zeros((2, CHUNK, accum.shape[2]), jnp.float32)
            return carry

        lax.fori_loop(0, accum.shape[1] // CHUNK, clear, 0)

        def invert(module, carry):
            inverse[order[module]] = module
            return carry

        lax.fori_loop(0, modules, invert, 0)

    def correct(band, carry):
        at = pl.multiple_of(band * height, height)
        module = inverse[band]
        rows = pl.ds(at, height)
        far_real = far[0, 0, rows, :]
        far_imag = far[0, 1, rows, :]
        sender = (module // per + senders - 1) % senders
        level = amp[sender, 0, module % per].astype(jnp.float32)
        magnitude = jnp.sqrt(far_real * far_real + far_imag * far_imag)
        factor = level / jnp.maximum(magnitude, 0.25) - 1.0
        corr[rows, :] = (factor * far_real).astype(jnp.bfloat16)
        corr[pl.ds(size + at, height), :] = (factor * far_imag).astype(jnp.bfloat16)
        return carry

    lax.fori_loop(0, modules, correct, 0)
    for block in range(size // BLOCK):
        to = slice(block * BLOCK, (block + 1) * BLOCK)
        also = slice(size + block * BLOCK, size + (block + 1) * BLOCK)
        product = jnp.dot(right[...], corr[:, to], preferred_element_type=jnp.float32)
        back[:, to] = product[:size].astype(jnp.bfloat16)
        back[:, also] = product[size:].astype(jnp.bfloat16)
    for plane in range(2):
        for block in range(size // BLOCK):
            to = slice(block * BLOCK, (block + 1) * BLOCK)
            of = slice(plane * size + block * BLOCK, plane * size + (block + 1) * BLOCK)
            change[plane, :, to] = jnp.dot(
                back[...], left[:, of], preferred_element_type=jnp.float32
            )

    lane = lax.broadcasted_iota(jnp.int32, (CHUNK, LANES), 1)
    tiles = CHUNK // SUBLANES
    sub = lax.broadcasted_iota(jnp.int32, (tiles + 1, SUBLANES, LANES), 1)
    empty = jnp.zeros((1, SUBLANES, LANES), jnp.float32)

    def spread(step, carry):
        at = pl.multiple_of(step * CHUNK, CHUNK)
        rows = pl.ds(at, CHUNK)
        start = pl.multiple_of(row_base + at, SUBLANES)
        last = [jnp.zeros((CHUNK, LANES), jnp.float32)] * 2
        for block in range(blocks + 1):
            if block < blocks:
                to = slice(block * LANES, (block + 1) * LANES)
                chg_real = change[0, rows, to]
                chg_imag = change[1, rows, to]
                spec_real = patch[0, 0, rows, to]
                spec_imag = patch[0, 1, rows, to]
                ill_real = ill[0, rows, to]
                ill_imag = ill[1, rows, to]
                numer[0, rows, to] += spec_real * chg_real + spec_imag * chg_imag
                numer[1, rows, to] += spec_real * chg_imag - spec_imag * chg_real
                grads = (
                    ill_real * chg_real + ill_imag * chg_imag,
                    ill_real * chg_imag - ill_imag * chg_real,
                )
                now = [pltpu.roll(grad, lane_shift, axis=1) for grad in grads]
            else:
                now = [jnp.zeros((CHUNK, LANES), jnp.float32)] * 2
            col = pl.multiple_of(base + block * LANES, LANES)
            for plane in range(2):
                placed = jnp.where(lane < lane_shift, last[plane], now[plane])
                placed = pltpu.roll(placed.reshape(tiles, SUBLANES, LANES), row_shift, axis=1)
                placed = jnp.where(
                    sub < row_shift,
                    jnp.concatenate([empty, placed], axis=0),
                    jnp.concatenate([placed, empty], axis=0),
                ).reshape(CHUNK + SUBLANES, LANES)
                accum[plane, pl.ds(start, CHUNK + SUBLANES), pl.ds(col, LANES)] += placed
            last = now
        return carry

    lax.fori_loop(0, size // CHUNK, spread, 0)


def whole(shape):
    return pl.BlockSpec(shape, lambda slot, *refs: (0,) * len(shape))


def once(shape):
    return pl.BlockSpec(
        shape, lambda slot, *refs: (0,) * len(shape), pipeline_mode=pl.Buffered(1)
    )


def one_slot(shape):
    return pl.BlockSpec((1,) + shape, lambda slot, *refs: (slot,) + (0,) * len(shape))


def run_forward(offs, region, ill, left, right):
    slots = offs.shape[0]
    size = ill.shape[-1]
    planes = jax.ShapeDtypeStruct((slots, 2, size, size), jnp.float32)
    return pl.pallas_call(
        forward_kernel,
        grid_spec=pltpu.PrefetchScalarGridSpec(
            num_scalar_prefetch=1,
            grid=(slots,),
            in_specs=[once(region.shape), once(ill.shape), once(left.shape), once(right.shape)],
            out_specs=[
                one_slot((2, size, size)),
                one_slot((2, size, size)),
                whole((size, size)),
            ],
            scratch_shapes=[
                pltpu.VMEM((2 * size, size), jnp.bfloat16),
                pltpu.VMEM((size, 2 * size), jnp.bfloat16),
            ],
        ),
        out_shape=[planes, planes, jax.ShapeDtypeStruct((size, size), jnp.float32)],
        cost_estimate=pl.CostEstimate(
            flops=slots * 16 * size**3, bytes_accessed=30_000_000, transcendentals=0
        ),
        compiler_params=pltpu.CompilerParams(vmem_limit_bytes=48 * 1024 * 1024),
        name="forward",
    )(offs, region, ill, left, right)


def run_backward(offs, order, far, patch, amp, ill, left, right, region_shape):
    slots = offs.shape[0]
    size = ill.shape[-1]
    senders, _, per, height, _ = amp.shape
    return pl.pallas_call(
        backward_kernel,
        grid_spec=pltpu.PrefetchScalarGridSpec(
            num_scalar_prefetch=2,
            grid=(slots,),
            in_specs=[
                one_slot((2, size, size)),
                one_slot((2, size, size)),
                pl.BlockSpec(
                    (senders, 1, per, height, size), lambda slot, *refs: (0, slot, 0, 0, 0)
                ),
                once(ill.shape),
                once(left.shape),
                once(right.shape),
            ],
            out_specs=[whole(region_shape), whole((2, size, size))],
            scratch_shapes=[
                pltpu.VMEM((2 * size, size), jnp.bfloat16),
                pltpu.VMEM((size, 2 * size), jnp.bfloat16),
                pltpu.VMEM((2, size, size), jnp.float32),
                pltpu.SMEM((senders * per,), jnp.int32),
            ],
        ),
        out_shape=[
            jax.ShapeDtypeStruct(region_shape, jnp.float32),
            jax.ShapeDtypeStruct((2, size, size), jnp.float32),
        ],
        cost_estimate=pl.CostEstimate(
            flops=slots * 16 * size**3, bytes_accessed=30_000_000, transcendentals=0
        ),
        compiler_params=pltpu.CompilerParams(vmem_limit_bytes=56 * 1024 * 1024),
        name="backward",
    )(offs, order, far, patch, amp, ill, left, right)


def spread_out(value):
    return lax.all_to_all(value, ("row", "col"), split_axis=0, concat_axis=0, tiled=True)


def shards(measured, module_row, scan_offsets, specimen, illumination):
    slots = scan_offsets.shape[2]
    size = illumination.shape[-1]
    tile_rows = specimen.shape[1]
    tile_cols = specimen.shape[2]
    senders = lax.axis_size("row")
    devices = senders * lax.axis_size("col")
    per, height = measured.shape[1], measured.shape[2]
    late = slots // 2
    edge = tile_cols // 2
    grouped = measured.reshape(senders, slots, per, height, size)
    moved = passed_along(grouped[:, late:], "col", 1)
    upper = passed_along(specimen, "row", 1)
    lower = passed_along(specimen, "row", -1)
    west = passed_along(specimen[:, :, edge:], "col", 1)
    east = passed_along(specimen[:, :, :edge], "col", -1)
    early_offs = passed_along(scan_offsets[0, 0, :late], "row", 1)
    late_offs = passed_both(scan_offsets[0, 0, late:], 1, 1)
    offs = jnp.concatenate([late_offs, early_offs], axis=0)
    outer = jnp.concatenate([upper, lower], axis=1)
    outer_west = passed_along(outer[:, :, edge:], "col", 1)
    outer_east = passed_along(outer[:, :, :edge], "col", -1)
    arrived = lax.all_to_all(
        jnp.concatenate([moved, grouped[:, :late]], axis=1),
        "row",
        split_axis=0,
        concat_axis=0,
        tiled=True,
        axis_index_groups=[[(sender + 1) % senders for sender in range(senders)]],
    )
    region = jnp.concatenate(
        [
            jnp.concatenate(
                [outer_west[:, :tile_rows], upper, outer_east[:, :tile_rows]], axis=2
            ),
            jnp.concatenate([west, specimen, east], axis=2),
            jnp.concatenate(
                [outer_west[:, tile_rows:], lower, outer_east[:, tile_rows:]], axis=2
            ),
        ],
        axis=1,
    )
    cos_table, sin_table = dft_tables(size)
    left = jnp.concatenate(
        [
            jnp.concatenate([cos_table, -sin_table], axis=1),
            jnp.concatenate([sin_table, cos_table], axis=1),
        ],
        axis=0,
    )
    right = jnp.concatenate(
        [
            jnp.concatenate([cos_table, sin_table], axis=1),
            jnp.concatenate([-sin_table, cos_table], axis=1),
        ],
        axis=0,
    )
    far, patch, density = run_forward(offs, region, illumination, left, right)
    share = (devices, size * size // devices // LANES, LANES)
    density_parts = spread_out(density.reshape(share))
    root = jnp.sqrt(jnp.sum(density_parts.reshape(share), axis=0) + 1e-06)
    accum, numer = run_backward(
        offs, module_row, far, patch, arrived, illumination, left, right, region.shape
    )
    small, numer_unit = narrowed(numer)
    rows = share[1]
    small = small.reshape(2, devices, rows, LANES).swapaxes(0, 1).reshape(devices, 2 * rows, LANES)
    parts = spread_out(small)
    units = spread_out(jnp.broadcast_to(numer_unit.reshape(1, 1, 1), (devices, 1, LANES)))
    total = jnp.sum(
        parts.astype(jnp.float32).reshape(devices, 2, rows, LANES) * units[:, None, :, :1], axis=0
    )
    mine, mine_unit = narrowed(total / root[None])
    result = spread_out(jnp.broadcast_to(mine.reshape(1, 2 * rows, LANES), small.shape))
    result_units = spread_out(
        jnp.broadcast_to(mine_unit.reshape(1, 1, 1), (devices, 1, LANES))
    )
    result = (
        result.reshape(devices, 2, rows, LANES).astype(jnp.float32) * result_units[:, :, None, :1][:, :1]
    )
    illumination_step = result.swapaxes(0, 1).reshape(2, size, size)
    to_west, to_west_unit = narrowed(accum[:, :, :edge])
    to_east, to_east_unit = narrowed(accum[:, :, edge + tile_cols :])
    from_east = passed_along(to_west, "col", -1)
    from_west = passed_along(to_east, "col", 1)
    from_east_unit = passed_along(to_west_unit, "col", -1)
    from_west_unit = passed_along(to_east_unit, "col", 1)
    column = accum[:, :, edge : edge + tile_cols] + jnp.concatenate(
        [widened(from_west, from_west_unit), widened(from_east, from_east_unit)], axis=2
    )
    to_upper, to_upper_unit = narrowed(column[:, :tile_rows])
    to_lower, to_lower_unit = narrowed(column[:, 2 * tile_rows :])
    from_lower = passed_along(to_upper, "row", -1)
    from_upper = passed_along(to_lower, "row", 1)
    from_lower_unit = passed_along(to_upper_unit, "row", -1)
    from_upper_unit = passed_along(to_lower_unit, "row", 1)
    specimen_step = (
        column[:, tile_rows : 2 * tile_rows]
        + widened(from_lower, from_lower_unit)
        + widened(from_upper, from_upper_unit)
    )
    return (specimen_step, illumination_step)


def solution(mesh):
    return jax.shard_map(
        shards,
        mesh=mesh,
        in_specs=(
            P("col", "row", None, None),
            P(),
            P("row", "col", None, None),
            P(None, "row", "col"),
            P(),
        ),
        out_specs=(P(None, "row", "col"), P()),
        check_vma=False,
    )
```

```python
import math

import jax
import jax.numpy as jnp
from jax import lax
from jax.experimental import pallas as pl
from jax.experimental.pallas import tpu as pltpu
from jax.sharding import PartitionSpec as P


LANES = 128
SUBLANES = 8
CHUNK = 32
BLOCK = 256
PIECE = 16
HALF_TOP = 65504.0


def passed_along(value, axis, steps):
    count = lax.axis_size(axis)
    pairs = [(source, (source + steps) % count) for source in range(count)]
    return lax.ppermute(value, axis, pairs)


def passed_both(value, row_steps, col_steps):
    rows, cols = lax.axis_size("row"), lax.axis_size("col")
    pairs = [
        (row * cols + col, (row + row_steps) % rows * cols + (col + col_steps) % cols)
        for row in range(rows)
        for col in range(cols)
    ]
    return lax.ppermute(value, ("row", "col"), pairs)


def dft_tables(size):
    index = jnp.arange(size, dtype=jnp.int32)
    wrapped = index[:, None] * index[None, :] % size
    angle = wrapped.astype(jnp.float32) * (2.0 * math.pi / size)
    norm = 1.0 / math.sqrt(size)
    return (
        (jnp.cos(angle) * norm).astype(jnp.bfloat16),
        (-jnp.sin(angle) * norm).astype(jnp.bfloat16),
    )


def narrowed(value, bound):
    return (value * (HALF_TOP / bound)).astype(jnp.float16)


def widened(value, bound):
    return value.astype(jnp.float32) * (bound / HALF_TOP)


def gather_rows(ref, plane, start, rows, col, shift):
    tiles = rows // SUBLANES + 1
    block = ref[plane, pl.ds(start, tiles * SUBLANES), pl.ds(col, LANES)]
    block = block.reshape(tiles, SUBLANES, LANES)
    rolled = pltpu.roll(block, (SUBLANES - shift) % SUBLANES, axis=1)
    sub = lax.broadcasted_iota(jnp.int32, (tiles - 1, SUBLANES, LANES), 1)
    return jnp.where(sub < SUBLANES - shift, rolled[:-1], rolled[1:]).reshape(rows, LANES)


def forward_kernel(offs, region, ill, left, right, far, patch, wave, half):
    slot = pl.program_id(0)
    size = ill.shape[-1]
    row = offs[slot, 0]
    base = slot * LANES
    lane_shift = offs[slot, 1] % LANES
    row_shift = row % SUBLANES
    row_base = row - row_shift
    lane = lax.broadcasted_iota(jnp.int32, (CHUNK, LANES), 1)
    blocks = size // LANES

    def extract(step, carry):
        at = pl.multiple_of(step * CHUNK, CHUNK)
        start = pl.multiple_of(row_base + at, SUBLANES)
        last = [None, None]
        for block in range(blocks + 1):
            col = pl.multiple_of(base + block * LANES, LANES)
            now = [
                pltpu.roll(
                    gather_rows(region, plane, start, CHUNK, col, row_shift),
                    (LANES - lane_shift) % LANES,
                    axis=1,
                )
                for plane in range(2)
            ]
            if block > 0:
                to = slice((block - 1) * LANES, block * LANES)
                spec_real, spec_imag = (
                    jnp.where(lane < LANES - lane_shift, last[plane], now[plane])
                    for plane in range(2)
                )
                patch[0, 0, pl.ds(at, CHUNK), to] = spec_real
                patch[0, 1, pl.ds(at, CHUNK), to] = spec_imag
                ill_real = ill[0, pl.ds(at, CHUNK), to]
                ill_imag = ill[1, pl.ds(at, CHUNK), to]
                wave[pl.ds(at, CHUNK), to] = (
                    ill_real * spec_real - ill_imag * spec_imag
                ).astype(jnp.bfloat16)
                wave[pl.ds(size + at, CHUNK), to] = (
                    ill_real * spec_imag + ill_imag * spec_real
                ).astype(jnp.bfloat16)
            last = now
        return carry

    lax.fori_loop(0, size // CHUNK, extract, 0)
    for block in range(size // BLOCK):
        to = slice(block * BLOCK, (block + 1) * BLOCK)
        also = slice(size + block * BLOCK, size + (block + 1) * BLOCK)
        product = jnp.dot(left[...], wave[:, to], preferred_element_type=jnp.float32)
        half[:, to] = product[:size].astype(jnp.bfloat16)
        half[:, also] = product[size:].astype(jnp.bfloat16)
    for plane in range(2):
        for block in range(size // BLOCK):
            to = slice(block * BLOCK, (block + 1) * BLOCK)
            of = slice(plane * size + block * BLOCK, plane * size + (block + 1) * BLOCK)
            far[0, plane, :, to] = jnp.dot(
                half[...], right[:, of], preferred_element_type=jnp.float32
            )


def backward_kernel(
    offs, order, far, patch, amp, ill, left, right, accum, sums, corr, back, change, inverse
):
    slot = pl.program_id(0)
    size = ill.shape[-1]
    modules = size // amp.shape[3]
    senders = amp.shape[0]
    row = offs[slot, 0]
    base = slot * LANES
    lane_shift = offs[slot, 1] % LANES
    row_shift = row % SUBLANES
    row_base = row - row_shift
    blocks = size // LANES
    height = amp.shape[3]
    per = amp.shape[2]

    @pl.when(slot == 0)
    def _():
        sums[...] = jnp.zeros_like(sums)

        def clear(step, carry):
            at = pl.multiple_of(step * CHUNK, CHUNK)
            accum[:, pl.ds(at, CHUNK), :] = jnp.zeros((2, CHUNK, accum.shape[2]), jnp.float32)
            return carry

        lax.fori_loop(0, accum.shape[1] // CHUNK, clear, 0)

        def invert(module, carry):
            inverse[order[module]] = module
            return carry

        lax.fori_loop(0, modules, invert, 0)

    def correct(band, carry):
        at = pl.multiple_of(band * height, height)
        module = inverse[band]
        rows = pl.ds(at, height)
        far_real = far[0, 0, rows, :]
        far_imag = far[0, 1, rows, :]
        sender = (module // per + senders - 1) % senders
        level = amp[sender, 0, module % per].astype(jnp.float32)
        magnitude = jnp.sqrt(far_real * far_real + far_imag * far_imag)
        factor = level / jnp.maximum(magnitude, 0.25) - 1.0
        corr[rows, :] = (factor * far_real).astype(jnp.bfloat16)
        corr[pl.ds(size + at, height), :] = (factor * far_imag).astype(jnp.bfloat16)
        return carry

    lax.fori_loop(0, modules, correct, 0)
    for block in range(size // BLOCK):
        to = slice(block * BLOCK, (block + 1) * BLOCK)
        also = slice(size + block * BLOCK, size + (block + 1) * BLOCK)
        product = jnp.dot(right[...], corr[:, to], preferred_element_type=jnp.float32)
        back[:, to] = product[:size].astype(jnp.bfloat16)
        back[:, also] = product[size:].astype(jnp.bfloat16)
    for plane in range(2):
        for block in range(size // BLOCK):
            to = slice(block * BLOCK, (block + 1) * BLOCK)
            of = slice(plane * size + block * BLOCK, plane * size + (block + 1) * BLOCK)
            change[plane, :, to] = jnp.dot(
                back[...], left[:, of], preferred_element_type=jnp.float32
            )

    lane = lax.broadcasted_iota(jnp.int32, (CHUNK, LANES), 1)
    tiles = CHUNK // SUBLANES
    sub = lax.broadcasted_iota(jnp.int32, (tiles + 1, SUBLANES, LANES), 1)
    empty = jnp.zeros((1, SUBLANES, LANES), jnp.float32)

    def spread(step, carry):
        at = pl.multiple_of(step * CHUNK, CHUNK)
        rows = pl.ds(at, CHUNK)
        start = pl.multiple_of(row_base + at, SUBLANES)
        last = [jnp.zeros((CHUNK, LANES), jnp.float32)] * 2
        for block in range(blocks + 1):
            if block < blocks:
                to = slice(block * LANES, (block + 1) * LANES)
                chg_real = change[0, rows, to]
                chg_imag = change[1, rows, to]
                spec_real = patch[0, 0, rows, to]
                spec_imag = patch[0, 1, rows, to]
                ill_real = ill[0, rows, to]
                ill_imag = ill[1, rows, to]
                places = pl.ds(step * (CHUNK // PIECE), CHUNK // PIECE)
                pieces = (CHUNK // PIECE, PIECE, LANES)
                sums[block, places, 0] += (spec_real * chg_real + spec_imag * chg_imag).reshape(
                    pieces
                )
                sums[block, places, 1] += (spec_real * chg_imag - spec_imag * chg_real).reshape(
                    pieces
                )
                sums[block, places, 2] += (spec_real * spec_real + spec_imag * spec_imag).reshape(
                    pieces
                )
                grads = (
                    ill_real * chg_real + ill_imag * chg_imag,
                    ill_real * chg_imag - ill_imag * chg_real,
                )
                now = [pltpu.roll(grad, lane_shift, axis=1) for grad in grads]
            else:
                now = [jnp.zeros((CHUNK, LANES), jnp.float32)] * 2
            col = pl.multiple_of(base + block * LANES, LANES)
            for plane in range(2):
                placed = jnp.where(lane < lane_shift, last[plane], now[plane])
                placed = pltpu.roll(placed.reshape(tiles, SUBLANES, LANES), row_shift, axis=1)
                placed = jnp.where(
                    sub < row_shift,
                    jnp.concatenate([empty, placed], axis=0),
                    jnp.concatenate([placed, empty], axis=0),
                ).reshape(CHUNK + SUBLANES, LANES)
                accum[plane, pl.ds(start, CHUNK + SUBLANES), pl.ds(col, LANES)] += placed
            last = now
        return carry

    lax.fori_loop(0, size // CHUNK, spread, 0)


def whole(shape):
    return pl.BlockSpec(shape, lambda slot, *refs: (0,) * len(shape))


def once(shape):
    return pl.BlockSpec(
        shape, lambda slot, *refs: (0,) * len(shape), pipeline_mode=pl.Buffered(1)
    )


def one_slot(shape):
    return pl.BlockSpec((1,) + shape, lambda slot, *refs: (slot,) + (0,) * len(shape))


def run_forward(offs, region, ill, left, right):
    slots = offs.shape[0]
    size = ill.shape[-1]
    planes = jax.ShapeDtypeStruct((slots, 2, size, size), jnp.float32)
    return pl.pallas_call(
        forward_kernel,
        grid_spec=pltpu.PrefetchScalarGridSpec(
            num_scalar_prefetch=1,
            grid=(slots,),
            in_specs=[once(region.shape), once(ill.shape), once(left.shape), once(right.shape)],
            out_specs=[
                one_slot((2, size, size)),
                one_slot((2, size, size)),
            ],
            scratch_shapes=[
                pltpu.VMEM((2 * size, size), jnp.bfloat16),
                pltpu.VMEM((size, 2 * size), jnp.bfloat16),
            ],
        ),
        out_shape=[planes, planes],
        cost_estimate=pl.CostEstimate(
            flops=slots * 16 * size**3, bytes_accessed=30_000_000, transcendentals=0
        ),
        compiler_params=pltpu.CompilerParams(vmem_limit_bytes=48 * 1024 * 1024),
        name="forward",
    )(offs, region, ill, left, right)


def run_backward(offs, order, far, patch, amp, ill, left, right, region_shape):
    slots = offs.shape[0]
    size = ill.shape[-1]
    senders, _, per, height, _ = amp.shape
    sums_shape = (size // LANES, size // PIECE, 3, PIECE, LANES)
    return pl.pallas_call(
        backward_kernel,
        grid_spec=pltpu.PrefetchScalarGridSpec(
            num_scalar_prefetch=2,
            grid=(slots,),
            in_specs=[
                one_slot((2, size, size)),
                one_slot((2, size, size)),
                pl.BlockSpec(
                    (senders, 1, per, height, size), lambda slot, *refs: (0, slot, 0, 0, 0)
                ),
                once(ill.shape),
                once(left.shape),
                once(right.shape),
            ],
            out_specs=[whole(region_shape), whole(sums_shape)],
            scratch_shapes=[
                pltpu.VMEM((2 * size, size), jnp.bfloat16),
                pltpu.VMEM((size, 2 * size), jnp.bfloat16),
                pltpu.VMEM((2, size, size), jnp.float32),
                pltpu.SMEM((senders * per,), jnp.int32),
            ],
        ),
        out_shape=[
            jax.ShapeDtypeStruct(region_shape, jnp.float32),
            jax.ShapeDtypeStruct(sums_shape, jnp.float32),
        ],
        cost_estimate=pl.CostEstimate(
            flops=slots * 16 * size**3, bytes_accessed=30_000_000, transcendentals=0
        ),
        compiler_params=pltpu.CompilerParams(vmem_limit_bytes=56 * 1024 * 1024),
        name="backward",
    )(offs, order, far, patch, amp, ill, left, right)


def spread_out(value):
    return lax.all_to_all(value, ("row", "col"), split_axis=0, concat_axis=0, tiled=True)


def shards(measured, module_row, scan_offsets, specimen, illumination):
    slots = scan_offsets.shape[2]
    size = illumination.shape[-1]
    tile_rows = specimen.shape[1]
    tile_cols = specimen.shape[2]
    senders = lax.axis_size("row")
    devices = senders * lax.axis_size("col")
    per, height = measured.shape[1], measured.shape[2]
    late = slots // 2
    edge = tile_cols // 2
    grouped = measured.reshape(senders, slots, per, height, size)
    upper = passed_along(specimen, "row", 1)
    lower = passed_along(specimen, "row", -1)
    moved = passed_along(grouped[:, late:], "col", 1)
    west = passed_along(specimen[:, :, edge:], "col", 1)
    east = passed_along(specimen[:, :, :edge], "col", -1)
    early_offs = passed_along(scan_offsets[0, 0, :late], "row", 1)
    late_offs = passed_both(scan_offsets[0, 0, late:], 1, 1)
    offs = jnp.concatenate([late_offs, early_offs], axis=0)
    lane = lax.broadcasted_iota(jnp.int32, (devices, 1, LANES), 2)
    peak = jnp.max(jnp.abs(specimen))
    power = jnp.sum(specimen * specimen)
    peaks = spread_out(jnp.where(lane < LANES // 2, peak, power))
    peak = jnp.maximum(jnp.max(peaks[:, :, : LANES // 2]), 1e-12)
    power = jnp.max(peaks[:, :, LANES // 2 :])
    ill_power = jnp.sum(illumination * illumination)
    ill_peak = jnp.maximum(jnp.max(jnp.abs(illumination)), 1e-8)
    modulus = 1.5 * peak
    energy = jnp.minimum(
        modulus * jnp.sqrt(ill_power), 1.5 * ill_peak * jnp.sqrt(6.0 * power)
    )
    change_bound = 9.0 * jnp.maximum(energy, 1e-20)
    grad_bound = 24.0 * ill_peak * change_bound
    sum_bound = slots * modulus * change_bound
    density_bound = slots * modulus * modulus
    step_bound = math.sqrt(slots * devices) * change_bound
    cos_table, sin_table = dft_tables(size)
    left = jnp.concatenate(
        [
            jnp.concatenate([cos_table, -sin_table], axis=1),
            jnp.concatenate([sin_table, cos_table], axis=1),
        ],
        axis=0,
    )
    right = jnp.concatenate(
        [
            jnp.concatenate([cos_table, sin_table], axis=1),
            jnp.concatenate([-sin_table, cos_table], axis=1),
        ],
        axis=0,
    )
    bounds = (change_bound, grad_bound, sum_bound, density_bound, step_bound)
    upper, lower, moved, west, east, offs, left, right, bounds = lax.optimization_barrier(
        (upper, lower, moved, west, east, offs, left, right, bounds)
    )
    change_bound, grad_bound, sum_bound, density_bound, step_bound = bounds
    outer_west = passed_along(
        jnp.concatenate([upper[:, :, edge:], lower[:, :, edge:]], axis=1), "col", 1
    )
    outer_east = passed_along(
        jnp.concatenate([upper[:, :, :edge], lower[:, :, :edge]], axis=1), "col", -1
    )
    arrived = lax.all_to_all(
        jnp.concatenate([moved, grouped[:, :late]], axis=1),
        "row",
        split_axis=0,
        concat_axis=0,
        tiled=True,
        axis_index_groups=[[(sender + 1) % senders for sender in range(senders)]],
    )
    region = jnp.concatenate(
        [
            jnp.concatenate(
                [outer_west[:, :tile_rows], upper, outer_east[:, :tile_rows]], axis=2
            ),
            jnp.concatenate([west, specimen, east], axis=2),
            jnp.concatenate(
                [outer_west[:, tile_rows:], lower, outer_east[:, tile_rows:]], axis=2
            ),
        ],
        axis=1,
    )
    far, patch = run_forward(offs, region, illumination, left, right)
    accum, sums = run_backward(
        offs, module_row, far, patch, arrived, illumination, left, right, region.shape
    )
    to_west = narrowed(accum[:, :, :edge], grad_bound)
    to_east = narrowed(accum[:, :, edge + tile_cols :], grad_bound)
    from_east = passed_along(to_west, "col", -1)
    from_west = passed_along(to_east, "col", 1)
    sums = sums.reshape(devices, 3 * PIECE, LANES)
    line = lax.broadcasted_iota(jnp.int32, (1, 3 * PIECE, 1), 1)
    bounds = jnp.where(line < 2 * PIECE, sum_bound, density_bound)
    packed = narrowed(sums, bounds)
    parts = spread_out(packed)
    column = accum[:, :, edge : edge + tile_cols] + jnp.concatenate(
        [widened(from_west, grad_bound), widened(from_east, grad_bound)], axis=2
    )
    to_upper = narrowed(column[:, :tile_rows], grad_bound)
    to_lower = narrowed(column[:, 2 * tile_rows :], grad_bound)
    from_lower = passed_along(to_upper, "row", -1)
    from_upper = passed_along(to_lower, "row", 1)
    total = jnp.sum(widened(parts, bounds), axis=0)
    mine = total[: 2 * PIECE].reshape(2, PIECE, LANES) / jnp.sqrt(total[2 * PIECE :] + 1e-06)
    mine = narrowed(mine, step_bound).reshape(1, 2 * PIECE, LANES)
    copies = jnp.broadcast_to(mine, (devices, 2 * PIECE, LANES))
    result = spread_out(copies)
    result = widened(result, step_bound).reshape(
        size // LANES, size // PIECE, 2, PIECE, LANES
    )
    illumination_step = result.transpose(2, 1, 3, 0, 4).reshape(2, size, size)
    specimen_step = (
        column[:, tile_rows : 2 * tile_rows]
        + widened(from_lower, grad_bound)
        + widened(from_upper, grad_bound)
    )
    return (specimen_step, illumination_step)


def solution(mesh):
    return jax.shard_map(
        shards,
        mesh=mesh,
        in_specs=(
            P("col", "row", None, None),
            P(),
            P("row", "col", None, None),
            P(None, "row", "col"),
            P(),
        ),
        out_specs=(P(None, "row", "col"), P()),
        check_vma=False,
    )
```

```python
import math

import jax
import jax.numpy as jnp
import numpy as np
from jax import lax
from jax.experimental import pallas as pl
from jax.experimental.pallas import tpu as pltpu
from jax.sharding import PartitionSpec as P


LANES = 128
SUBLANES = 8
CHUNK = 32
BLOCK = 256
PIECE = 16
HALF_TOP = 65504.0


def passed_along(value, axis, steps):
    count = lax.axis_size(axis)
    pairs = [(source, (source + steps) % count) for source in range(count)]
    return lax.ppermute(value, axis, pairs)


def passed_both(value, row_steps, col_steps):
    rows, cols = lax.axis_size("row"), lax.axis_size("col")
    pairs = [
        (row * cols + col, (row + row_steps) % rows * cols + (col + col_steps) % cols)
        for row in range(rows)
        for col in range(cols)
    ]
    return lax.ppermute(value, ("row", "col"), pairs)


def dft_tables(size):
    index = np.arange(size, dtype=np.int64)
    wrapped = index[:, None] * index[None, :] % size
    angle = wrapped.astype(np.float32) * np.float32(2.0 * math.pi / size)
    norm = np.float32(1.0 / math.sqrt(size))
    cos_table = np.cos(angle.astype(np.float64)).astype(np.float32) * norm
    sin_table = -np.sin(angle.astype(np.float64)).astype(np.float32) * norm
    return jnp.asarray(cos_table, jnp.bfloat16), jnp.asarray(sin_table, jnp.bfloat16)


def narrowed(value, bound):
    return (value * (HALF_TOP / bound)).astype(jnp.float16)


def widened(value, bound):
    return value.astype(jnp.float32) * (bound / HALF_TOP)


def gather_rows(ref, plane, start, rows, col, shift):
    tiles = rows // SUBLANES + 1
    block = ref[plane, pl.ds(start, tiles * SUBLANES), pl.ds(col, LANES)]
    block = block.reshape(tiles, SUBLANES, LANES)
    rolled = pltpu.roll(block, (SUBLANES - shift) % SUBLANES, axis=1)
    sub = lax.broadcasted_iota(jnp.int32, (tiles - 1, SUBLANES, LANES), 1)
    return jnp.where(sub < SUBLANES - shift, rolled[:-1], rolled[1:]).reshape(rows, LANES)


def build_tables(cos_table, sin_table, left, right):
    size = cos_table.shape[-1]
    low, high = slice(0, size), slice(size, 2 * size)
    for table, sign in ((left, -1), (right, 1)):
        table[low, low] = cos_table[...]
        table[high, high] = cos_table[...]
        table[low, high] = sin_table[...] if sign > 0 else -sin_table[...]
        table[high, low] = -sin_table[...] if sign > 0 else sin_table[...]


def region_copies(pieces, region, sems):
    upper, lower, middle, west, east, outer_west, outer_east = pieces
    rows, cols, edge = middle.shape[1], middle.shape[2], west.shape[2]
    tops = [pl.ds(k * rows, rows) for k in range(3)]
    center, right = pl.ds(edge, cols), pl.ds(edge + cols, edge)
    first = pl.ds(0, edge)
    moves = [
        (upper, tops[0], center),
        (middle, tops[1], center),
        (lower, tops[2], center),
        (west, tops[1], first),
        (east, tops[1], right),
        (outer_west.at[:, pl.ds(0, rows)], tops[0], first),
        (outer_west.at[:, pl.ds(rows, rows)], tops[2], first),
        (outer_east.at[:, pl.ds(0, rows)], tops[0], right),
        (outer_east.at[:, pl.ds(rows, rows)], tops[2], right),
    ]
    return [
        pltpu.make_async_copy(source, region.at[:, place, columns], sems.at[index])
        for index, (source, place, columns) in enumerate(moves)
    ]


def forward_kernel(offs, *refs):
    pieces, refs = refs[:7], refs[7:]
    ill, cos_table, sin_table, far, patch, region, left, right, wave, half, sems = refs
    slot = pl.program_id(0)
    size = ill.shape[-1]
    row = offs[slot, 0]
    base = slot * LANES
    lane_shift = offs[slot, 1] % LANES
    row_shift = row % SUBLANES
    row_base = row - row_shift
    lane = lax.broadcasted_iota(jnp.int32, (CHUNK, LANES), 1)
    blocks = size // LANES

    @pl.when(slot == 0)
    def _():
        copies = region_copies(pieces, region, sems)
        for copy in copies:
            copy.start()
        build_tables(cos_table, sin_table, left, right)
        for copy in copies:
            copy.wait()

    def extract(step, carry):
        at = pl.multiple_of(step * CHUNK, CHUNK)
        start = pl.multiple_of(row_base + at, SUBLANES)
        last = [None, None]
        for block in range(blocks + 1):
            col = pl.multiple_of(base + block * LANES, LANES)
            now = [
                pltpu.roll(
                    gather_rows(region, plane, start, CHUNK, col, row_shift),
                    (LANES - lane_shift) % LANES,
                    axis=1,
                )
                for plane in range(2)
            ]
            if block > 0:
                to = slice((block - 1) * LANES, block * LANES)
                spec_real, spec_imag = (
                    jnp.where(lane < LANES - lane_shift, last[plane], now[plane])
                    for plane in range(2)
                )
                patch[0, 0, pl.ds(at, CHUNK), to] = spec_real
                patch[0, 1, pl.ds(at, CHUNK), to] = spec_imag
                ill_real = ill[0, pl.ds(at, CHUNK), to]
                ill_imag = ill[1, pl.ds(at, CHUNK), to]
                wave[pl.ds(at, CHUNK), to] = (
                    ill_real * spec_real - ill_imag * spec_imag
                ).astype(jnp.bfloat16)
                wave[pl.ds(size + at, CHUNK), to] = (
                    ill_real * spec_imag + ill_imag * spec_real
                ).astype(jnp.bfloat16)
            last = now
        return carry

    lax.fori_loop(0, size // CHUNK, extract, 0)
    for block in range(size // BLOCK):
        to = slice(block * BLOCK, (block + 1) * BLOCK)
        also = slice(size + block * BLOCK, size + (block + 1) * BLOCK)
        product = jnp.dot(left[...], wave[:, to], preferred_element_type=jnp.float32)
        half[:, to] = product[:size].astype(jnp.bfloat16)
        half[:, also] = product[size:].astype(jnp.bfloat16)
    for plane in range(2):
        for block in range(size // BLOCK):
            to = slice(block * BLOCK, (block + 1) * BLOCK)
            of = slice(plane * size + block * BLOCK, plane * size + (block + 1) * BLOCK)
            far[0, plane, :, to] = jnp.dot(
                half[...], right[:, of], preferred_element_type=jnp.float32
            )


def backward_kernel(
    offs,
    order,
    far,
    patch,
    amp,
    ill,
    cos_table,
    sin_table,
    accum,
    sums,
    corr,
    back,
    change,
    left,
    right,
    inverse,
):
    slot = pl.program_id(0)
    size = ill.shape[-1]
    modules = size // amp.shape[3]
    senders = amp.shape[0]
    row = offs[slot, 0]
    base = slot * LANES
    lane_shift = offs[slot, 1] % LANES
    row_shift = row % SUBLANES
    row_base = row - row_shift
    blocks = size // LANES
    height = amp.shape[3]
    per = amp.shape[2]

    @pl.when(slot == 0)
    def _():
        build_tables(cos_table, sin_table, left, right)
        sums[...] = jnp.zeros_like(sums)

        def clear(step, carry):
            at = pl.multiple_of(step * CHUNK, CHUNK)
            accum[:, pl.ds(at, CHUNK), :] = jnp.zeros((2, CHUNK, accum.shape[2]), jnp.float32)
            return carry

        lax.fori_loop(0, accum.shape[1] // CHUNK, clear, 0)

        def invert(module, carry):
            inverse[order[module]] = module
            return carry

        lax.fori_loop(0, modules, invert, 0)

    def correct(band, carry):
        at = pl.multiple_of(band * height, height)
        module = inverse[band]
        rows = pl.ds(at, height)
        far_real = far[0, 0, rows, :]
        far_imag = far[0, 1, rows, :]
        sender = (module // per + senders - 1) % senders
        level = amp[sender, 0, module % per].astype(jnp.float32)
        magnitude = jnp.sqrt(far_real * far_real + far_imag * far_imag)
        factor = level / jnp.maximum(magnitude, 0.25) - 1.0
        corr[rows, :] = (factor * far_real).astype(jnp.bfloat16)
        corr[pl.ds(size + at, height), :] = (factor * far_imag).astype(jnp.bfloat16)
        return carry

    lax.fori_loop(0, modules, correct, 0)
    for block in range(size // BLOCK):
        to = slice(block * BLOCK, (block + 1) * BLOCK)
        also = slice(size + block * BLOCK, size + (block + 1) * BLOCK)
        product = jnp.dot(right[...], corr[:, to], preferred_element_type=jnp.float32)
        back[:, to] = product[:size].astype(jnp.bfloat16)
        back[:, also] = product[size:].astype(jnp.bfloat16)
    for plane in range(2):
        for block in range(size // BLOCK):
            to = slice(block * BLOCK, (block + 1) * BLOCK)
            of = slice(plane * size + block * BLOCK, plane * size + (block + 1) * BLOCK)
            change[plane, :, to] = jnp.dot(
                back[...], left[:, of], preferred_element_type=jnp.float32
            )

    lane = lax.broadcasted_iota(jnp.int32, (CHUNK, LANES), 1)
    tiles = CHUNK // SUBLANES
    sub = lax.broadcasted_iota(jnp.int32, (tiles + 1, SUBLANES, LANES), 1)
    empty = jnp.zeros((1, SUBLANES, LANES), jnp.float32)

    def spread(step, carry):
        at = pl.multiple_of(step * CHUNK, CHUNK)
        rows = pl.ds(at, CHUNK)
        start = pl.multiple_of(row_base + at, SUBLANES)
        last = [jnp.zeros((CHUNK, LANES), jnp.float32)] * 2
        for block in range(blocks + 1):
            if block < blocks:
                to = slice(block * LANES, (block + 1) * LANES)
                chg_real = change[0, rows, to]
                chg_imag = change[1, rows, to]
                spec_real = patch[0, 0, rows, to]
                spec_imag = patch[0, 1, rows, to]
                ill_real = ill[0, rows, to]
                ill_imag = ill[1, rows, to]
                places = pl.ds(step * (CHUNK // PIECE), CHUNK // PIECE)
                pieces = (CHUNK // PIECE, PIECE, LANES)
                sums[block, places, 0] += (spec_real * chg_real + spec_imag * chg_imag).reshape(
                    pieces
                )
                sums[block, places, 1] += (spec_real * chg_imag - spec_imag * chg_real).reshape(
                    pieces
                )
                sums[block, places, 2] += (spec_real * spec_real + spec_imag * spec_imag).reshape(
                    pieces
                )
                grads = (
                    ill_real * chg_real + ill_imag * chg_imag,
                    ill_real * chg_imag - ill_imag * chg_real,
                )
                now = [pltpu.roll(grad, lane_shift, axis=1) for grad in grads]
            else:
                now = [jnp.zeros((CHUNK, LANES), jnp.float32)] * 2
            col = pl.multiple_of(base + block * LANES, LANES)
            for plane in range(2):
                placed = jnp.where(lane < lane_shift, last[plane], now[plane])
                placed = pltpu.roll(placed.reshape(tiles, SUBLANES, LANES), row_shift, axis=1)
                placed = jnp.where(
                    sub < row_shift,
                    jnp.concatenate([empty, placed], axis=0),
                    jnp.concatenate([placed, empty], axis=0),
                ).reshape(CHUNK + SUBLANES, LANES)
                accum[plane, pl.ds(start, CHUNK + SUBLANES), pl.ds(col, LANES)] += placed
            last = now
        return carry

    lax.fori_loop(0, size // CHUNK, spread, 0)


def whole(shape):
    return pl.BlockSpec(shape, lambda slot, *refs: (0,) * len(shape))


def once(shape):
    return pl.BlockSpec(
        shape, lambda slot, *refs: (0,) * len(shape), pipeline_mode=pl.Buffered(1)
    )


def one_slot(shape):
    return pl.BlockSpec((1,) + shape, lambda slot, *refs: (slot,) + (0,) * len(shape))


def run_forward(offs, pieces, ill, cos_table, sin_table):
    slots = offs.shape[0]
    size = ill.shape[-1]
    rows, cols, edge = pieces[2].shape[1], pieces[2].shape[2], pieces[3].shape[2]
    planes = jax.ShapeDtypeStruct((slots, 2, size, size), jnp.float32)
    return pl.pallas_call(
        forward_kernel,
        grid_spec=pltpu.PrefetchScalarGridSpec(
            num_scalar_prefetch=1,
            grid=(slots,),
            in_specs=[pl.BlockSpec(memory_space=pl.ANY)] * len(pieces)
            + [once(ill.shape), once(cos_table.shape), once(sin_table.shape)],
            out_specs=[
                one_slot((2, size, size)),
                one_slot((2, size, size)),
            ],
            scratch_shapes=[
                pltpu.VMEM((2, 3 * rows, cols + 2 * edge), jnp.float32),
                pltpu.VMEM((2 * size, 2 * size), jnp.bfloat16),
                pltpu.VMEM((2 * size, 2 * size), jnp.bfloat16),
                pltpu.VMEM((2 * size, size), jnp.bfloat16),
                pltpu.VMEM((size, 2 * size), jnp.bfloat16),
                pltpu.SemaphoreType.DMA((9,)),
            ],
        ),
        out_shape=[planes, planes],
        cost_estimate=pl.CostEstimate(
            flops=slots * 16 * size**3, bytes_accessed=30_000_000, transcendentals=0
        ),
        compiler_params=pltpu.CompilerParams(vmem_limit_bytes=48 * 1024 * 1024),
        name="forward",
    )(offs, *pieces, ill, cos_table, sin_table)


def run_backward(offs, order, far, patch, amp, ill, cos_table, sin_table, region_shape):
    slots = offs.shape[0]
    size = ill.shape[-1]
    senders, _, per, height, _ = amp.shape
    sums_shape = (size // LANES, size // PIECE, 3, PIECE, LANES)
    return pl.pallas_call(
        backward_kernel,
        grid_spec=pltpu.PrefetchScalarGridSpec(
            num_scalar_prefetch=2,
            grid=(slots,),
            in_specs=[
                one_slot((2, size, size)),
                one_slot((2, size, size)),
                pl.BlockSpec(
                    (senders, 1, per, height, size), lambda slot, *refs: (0, slot, 0, 0, 0)
                ),
                once(ill.shape),
                once(cos_table.shape),
                once(sin_table.shape),
            ],
            out_specs=[whole(region_shape), whole(sums_shape)],
            scratch_shapes=[
                pltpu.VMEM((2 * size, size), jnp.bfloat16),
                pltpu.VMEM((size, 2 * size), jnp.bfloat16),
                pltpu.VMEM((2, size, size), jnp.float32),
                pltpu.VMEM((2 * size, 2 * size), jnp.bfloat16),
                pltpu.VMEM((2 * size, 2 * size), jnp.bfloat16),
                pltpu.SMEM((senders * per,), jnp.int32),
            ],
        ),
        out_shape=[
            jax.ShapeDtypeStruct(region_shape, jnp.float32),
            jax.ShapeDtypeStruct(sums_shape, jnp.float32),
        ],
        cost_estimate=pl.CostEstimate(
            flops=slots * 16 * size**3, bytes_accessed=30_000_000, transcendentals=0
        ),
        compiler_params=pltpu.CompilerParams(vmem_limit_bytes=56 * 1024 * 1024),
        name="backward",
    )(offs, order, far, patch, amp, ill, cos_table, sin_table)


def unpack_kernel(packed, out):
    size = out.shape[1]
    for plane in range(2):
        out[plane] = packed[:, plane].reshape(size, LANES)


def unpacked(packed, size):
    packed = packed.reshape(size * size // (PIECE * LANES), 2, PIECE, LANES)
    return pl.pallas_call(
        unpack_kernel,
        grid=(size // LANES,),
        in_specs=[pl.BlockSpec((size // PIECE, 2, PIECE, LANES), lambda at: (at, 0, 0, 0))],
        out_specs=pl.BlockSpec((2, size, LANES), lambda at: (0, 0, at)),
        out_shape=jax.ShapeDtypeStruct((2, size, size), jnp.float32),
        name="unpack",
    )(packed)


def spread_out(value):
    return lax.all_to_all(value, ("row", "col"), split_axis=0, concat_axis=0, tiled=True)


def shards(measured, module_row, scan_offsets, specimen, illumination):
    slots = scan_offsets.shape[2]
    size = illumination.shape[-1]
    tile_rows = specimen.shape[1]
    tile_cols = specimen.shape[2]
    senders = lax.axis_size("row")
    devices = senders * lax.axis_size("col")
    per, height = measured.shape[1], measured.shape[2]
    late = slots // 2
    edge = tile_cols // 2
    grouped = measured.reshape(senders, slots, per, height, size)
    upper = passed_along(specimen, "row", 1)
    lower = passed_along(specimen, "row", -1)
    moved = passed_along(grouped[:, late:], "col", 1)
    west = passed_along(specimen[:, :, edge:], "col", 1)
    east = passed_along(specimen[:, :, :edge], "col", -1)
    early_offs = passed_along(scan_offsets[0, 0, :late], "row", 1)
    late_offs = passed_both(scan_offsets[0, 0, late:], 1, 1)
    offs = jnp.concatenate([late_offs, early_offs], axis=0)
    lane = lax.broadcasted_iota(jnp.int32, (devices, 1, LANES), 2)
    peak = jnp.max(jnp.abs(specimen))
    power = jnp.sum(specimen * specimen)
    peaks = spread_out(jnp.where(lane < LANES // 2, peak, power))
    peak = jnp.maximum(jnp.max(peaks[:, :, : LANES // 2]), 1e-12)
    power = jnp.max(peaks[:, :, LANES // 2 :])
    ill_power = jnp.sum(illumination * illumination)
    ill_peak = jnp.maximum(jnp.max(jnp.abs(illumination)), 1e-8)
    modulus = 1.5 * peak
    energy = jnp.minimum(
        modulus * jnp.sqrt(ill_power), 1.5 * ill_peak * jnp.sqrt(6.0 * power)
    )
    change_bound = 9.0 * jnp.maximum(energy, 1e-20)
    grad_bound = 24.0 * ill_peak * change_bound
    sum_bound = slots * modulus * change_bound
    density_bound = slots * modulus * modulus
    step_bound = math.sqrt(slots * devices) * change_bound
    cos_table, sin_table = dft_tables(size)
    bounds = (change_bound, grad_bound, sum_bound, density_bound, step_bound)
    upper, lower, moved, west, east, offs, bounds = lax.optimization_barrier(
        (upper, lower, moved, west, east, offs, bounds)
    )
    change_bound, grad_bound, sum_bound, density_bound, step_bound = bounds
    west_edges = jnp.concatenate([upper[:, :, edge:], lower[:, :, edge:]], axis=1)
    east_edges = jnp.concatenate([upper[:, :, :edge], lower[:, :, :edge]], axis=1)
    outer_west = passed_along(west_edges, "col", 1)
    outer_east = passed_along(east_edges, "col", -1)
    levels = jnp.concatenate([moved, grouped[:, :late]], axis=1)
    arrived = lax.all_to_all(
        levels,
        "row",
        split_axis=0,
        concat_axis=0,
        tiled=True,
        axis_index_groups=[[(sender + 1) % senders for sender in range(senders)]],
    )
    pieces = (upper, lower, specimen, west, east, outer_west, outer_east)
    far, patch = run_forward(offs, pieces, illumination, cos_table, sin_table)
    region_shape = (2, 3 * tile_rows, tile_cols + 2 * edge)
    accum, sums = run_backward(
        offs, module_row, far, patch, arrived, illumination, cos_table, sin_table, region_shape
    )
    to_west = narrowed(accum[:, :, :edge], grad_bound)
    to_east = narrowed(accum[:, :, edge + tile_cols :], grad_bound)
    from_east = passed_along(to_west, "col", -1)
    from_west = passed_along(to_east, "col", 1)
    sums = sums.reshape(devices, 3 * PIECE, LANES)
    line = lax.broadcasted_iota(jnp.int32, (1, 3 * PIECE, 1), 1)
    bounds = jnp.where(line < 2 * PIECE, sum_bound, density_bound)
    packed = narrowed(sums, bounds)
    parts = spread_out(packed)
    column = accum[:, :, edge : edge + tile_cols] + jnp.concatenate(
        [widened(from_west, grad_bound), widened(from_east, grad_bound)], axis=2
    )
    to_upper = narrowed(column[:, :tile_rows], grad_bound)
    to_lower = narrowed(column[:, 2 * tile_rows :], grad_bound)
    from_lower = passed_along(to_upper, "row", -1)
    from_upper = passed_along(to_lower, "row", 1)
    total = jnp.sum(widened(parts, bounds), axis=0)
    mine = total[: 2 * PIECE].reshape(2, PIECE, LANES) / jnp.sqrt(total[2 * PIECE :] + 1e-06)
    mine = narrowed(mine, step_bound).reshape(1, 2 * PIECE, LANES)
    copies = jnp.broadcast_to(mine, (devices, 2 * PIECE, LANES))
    result = spread_out(copies)
    illumination_step = unpacked(widened(result, step_bound), size)
    specimen_step = (
        column[:, tile_rows : 2 * tile_rows]
        + widened(from_lower, grad_bound)
        + widened(from_upper, grad_bound)
    )
    return (specimen_step, illumination_step)


def solution(mesh):
    return jax.shard_map(
        shards,
        mesh=mesh,
        in_specs=(
            P("col", "row", None, None),
            P(),
            P("row", "col", None, None),
            P(None, "row", "col"),
            P(),
        ),
        out_specs=(P(None, "row", "col"), P()),
        check_vma=False,
    )
```

```python
import math

import jax
import jax.numpy as jnp
import numpy as np
from jax import lax
from jax.experimental import pallas as pl
from jax.experimental.pallas import tpu as pltpu
from jax.sharding import PartitionSpec as P


LANES = 128
CHUNK = 32
BLOCK = 256
PIECE = 16
HALF_TOP = 65504.0


def passed_along(value, axis, steps):
    count = lax.axis_size(axis)
    pairs = [(source, (source + steps) % count) for source in range(count)]
    return lax.ppermute(value, axis, pairs)


def passed_both(value, row_steps, col_steps):
    rows, cols = lax.axis_size("row"), lax.axis_size("col")
    pairs = [
        (row * cols + col, (row + row_steps) % rows * cols + (col + col_steps) % cols)
        for row in range(rows)
        for col in range(cols)
    ]
    return lax.ppermute(value, ("row", "col"), pairs)


def dft_tables(size):
    index = np.arange(size, dtype=np.int64)
    wrapped = index[:, None] * index[None, :] % size
    angle = wrapped.astype(np.float32) * np.float32(2.0 * math.pi / size)
    norm = np.float32(1.0 / math.sqrt(size))
    cos_table = np.cos(angle.astype(np.float64)).astype(np.float32) * norm
    sin_table = -np.sin(angle.astype(np.float64)).astype(np.float32) * norm
    tables = (cos_table, sin_table, -sin_table)
    return tuple(jnp.asarray(table, jnp.bfloat16) for table in tables)


def narrowed(value, bound):
    return (value * (HALF_TOP / bound)).astype(jnp.float16)


def widened(value, bound):
    return value.astype(jnp.float32) * (bound / HALF_TOP)


def table_copies(tables, left, right, sems):
    cos_table, sin_table, negative = tables
    size = cos_table.shape[-1]
    low, high = pl.ds(0, size), pl.ds(size, size)
    moves = [
        (cos_table, left, low, low),
        (cos_table, left, high, high),
        (negative, left, low, high),
        (sin_table, left, high, low),
        (cos_table, right, low, low),
        (cos_table, right, high, high),
        (sin_table, right, low, high),
        (negative, right, high, low),
    ]
    return [
        pltpu.make_async_copy(source, table.at[rows, columns], sems.at[index])
        for index, (source, table, rows, columns) in enumerate(moves)
    ]


def region_copies(pieces, region, sems):
    upper, lower, middle, west, east, outer_west, outer_east = pieces
    rows, cols, edge = middle.shape[1], middle.shape[2], west.shape[2]
    center, right = edge // LANES, (edge + cols) // LANES
    moves = [
        (upper, 0, 0, center),
        (middle, 0, 1, center),
        (lower, 0, 2, center),
        (west, 0, 1, 0),
        (east, 0, 1, right),
        (outer_west, 0, 0, 0),
        (outer_west, 1, 2, 0),
        (outer_east, 0, 0, right),
        (outer_east, 1, 2, right),
    ]
    copies = []
    for piece, source, target, first in moves:
        for block in range(piece.shape[2] // LANES):
            copies.append(
                pltpu.make_async_copy(
                    piece.at[:, pl.ds(source * rows, rows), pl.ds(block * LANES, LANES)],
                    region.at[:, first + block, pl.ds(target * rows, rows)],
                    sems.at[len(copies)],
                )
            )
    return copies


def forward_kernel(offs, *refs):
    pieces, tables, refs = refs[:7], refs[7:10], refs[10:]
    ill, far, patch, region, left, right, wave, half, region_sems, table_sems = refs
    slot = pl.program_id(0)
    size = ill.shape[-1]
    row = offs[slot, 0]
    lane_shift = offs[slot, 1] % LANES
    lane = lax.broadcasted_iota(jnp.int32, (CHUNK, LANES), 1)
    blocks = size // LANES

    @pl.when(slot == 0)
    def _():
        region_moves = region_copies(pieces, region, region_sems)
        table_moves = table_copies(tables, left, right, table_sems)
        for move in region_moves + table_moves:
            move.start()
        for move in region_moves + table_moves:
            move.wait()

    def extract(step, carry):
        at = pl.multiple_of(step * CHUNK, CHUNK)
        last = [None, None]
        for block in range(blocks + 1):
            now = [
                pltpu.roll(
                    region[plane, slot + block, pl.ds(row + at, CHUNK), :],
                    (LANES - lane_shift) % LANES,
                    axis=1,
                )
                for plane in range(2)
            ]
            if block > 0:
                to = slice((block - 1) * LANES, block * LANES)
                spec_real, spec_imag = (
                    jnp.where(lane < LANES - lane_shift, last[plane], now[plane])
                    for plane in range(2)
                )
                patch[0, 0, pl.ds(at, CHUNK), to] = spec_real
                patch[0, 1, pl.ds(at, CHUNK), to] = spec_imag
                ill_real = ill[0, pl.ds(at, CHUNK), to]
                ill_imag = ill[1, pl.ds(at, CHUNK), to]
                wave[pl.ds(at, CHUNK), to] = (
                    ill_real * spec_real - ill_imag * spec_imag
                ).astype(jnp.bfloat16)
                wave[pl.ds(size + at, CHUNK), to] = (
                    ill_real * spec_imag + ill_imag * spec_real
                ).astype(jnp.bfloat16)
            last = now
        return carry

    lax.fori_loop(0, size // CHUNK, extract, 0, unroll=4)
    for block in range(size // BLOCK):
        to = slice(block * BLOCK, (block + 1) * BLOCK)
        also = slice(size + block * BLOCK, size + (block + 1) * BLOCK)
        product = jnp.dot(left[...], wave[:, to], preferred_element_type=jnp.float32)
        half[:, to] = product[:size].astype(jnp.bfloat16)
        half[:, also] = product[size:].astype(jnp.bfloat16)
    for plane in range(2):
        for block in range(size // BLOCK):
            to = slice(block * BLOCK, (block + 1) * BLOCK)
            of = slice(plane * size + block * BLOCK, plane * size + (block + 1) * BLOCK)
            far[0, plane, :, to] = jnp.dot(
                half[...], right[:, of], preferred_element_type=jnp.float32
            )


def backward_kernel(
    offs,
    order,
    far,
    patch,
    amp,
    ill,
    cos_table,
    sin_table,
    negative,
    accum,
    sums,
    corr,
    back,
    change,
    left,
    right,
    inverse,
    table_sems,
):
    slot = pl.program_id(0)
    size = ill.shape[-1]
    modules = size // amp.shape[3]
    senders = amp.shape[0]
    row = offs[slot, 0]
    lane_shift = offs[slot, 1] % LANES
    tables = (cos_table, sin_table, negative)
    blocks = size // LANES
    height = amp.shape[3]
    per = amp.shape[2]

    @pl.when(slot == 0)
    def _():
        for move in table_copies(tables, left, right, table_sems):
            move.start()
        sums[...] = jnp.zeros_like(sums)

        def clear(step, carry):
            at = pl.multiple_of(step * CHUNK, CHUNK)
            accum[:, :, pl.ds(at, CHUNK), :] = jnp.zeros(
                (2, accum.shape[1], CHUNK, LANES), jnp.float32
            )
            return carry

        lax.fori_loop(0, accum.shape[2] // CHUNK, clear, 0)

        def invert(module, carry):
            inverse[order[module]] = module
            return carry

        lax.fori_loop(0, modules, invert, 0)

    def correct(band, carry):
        at = pl.multiple_of(band * height, height)
        module = inverse[band]
        rows = pl.ds(at, height)
        far_real = far[0, 0, rows, :]
        far_imag = far[0, 1, rows, :]
        sender = (module // per + senders - 1) % senders
        level = amp[sender, 0, module % per].astype(jnp.float32)
        inverse_size = lax.rsqrt(far_real * far_real + far_imag * far_imag)
        factor = level * jnp.minimum(inverse_size, 4.0) - 1.0
        corr[rows, :] = (factor * far_real).astype(jnp.bfloat16)
        corr[pl.ds(size + at, height), :] = (factor * far_imag).astype(jnp.bfloat16)
        return carry

    lax.fori_loop(0, modules, correct, 0, unroll=4)

    @pl.when(slot == 0)
    def _():
        for move in table_copies(tables, left, right, table_sems):
            move.wait()

    for block in range(size // BLOCK):
        to = slice(block * BLOCK, (block + 1) * BLOCK)
        also = slice(size + block * BLOCK, size + (block + 1) * BLOCK)
        product = jnp.dot(right[...], corr[:, to], preferred_element_type=jnp.float32)
        back[:, to] = product[:size].astype(jnp.bfloat16)
        back[:, also] = product[size:].astype(jnp.bfloat16)
    for plane in range(2):
        for block in range(size // BLOCK):
            to = slice(block * BLOCK, (block + 1) * BLOCK)
            of = slice(plane * size + block * BLOCK, plane * size + (block + 1) * BLOCK)
            change[plane, :, to] = jnp.dot(
                back[...], left[:, of], preferred_element_type=jnp.float32
            )

    lane = lax.broadcasted_iota(jnp.int32, (CHUNK, LANES), 1)

    def spread(step, carry):
        at = pl.multiple_of(step * CHUNK, CHUNK)
        rows = pl.ds(at, CHUNK)
        last = [jnp.zeros((CHUNK, LANES), jnp.float32)] * 2
        for block in range(blocks + 1):
            if block < blocks:
                to = slice(block * LANES, (block + 1) * LANES)
                chg_real = change[0, rows, to]
                chg_imag = change[1, rows, to]
                spec_real = patch[0, 0, rows, to]
                spec_imag = patch[0, 1, rows, to]
                ill_real = ill[0, rows, to]
                ill_imag = ill[1, rows, to]
                places = pl.ds(step * (CHUNK // PIECE), CHUNK // PIECE)
                pieces = (CHUNK // PIECE, PIECE, LANES)
                sums[block, places, 0] += (spec_real * chg_real + spec_imag * chg_imag).reshape(
                    pieces
                )
                sums[block, places, 1] += (spec_real * chg_imag - spec_imag * chg_real).reshape(
                    pieces
                )
                sums[block, places, 2] += (spec_real * spec_real + spec_imag * spec_imag).reshape(
                    pieces
                )
                grads = (
                    ill_real * chg_real + ill_imag * chg_imag,
                    ill_real * chg_imag - ill_imag * chg_real,
                )
                now = [pltpu.roll(grad, lane_shift, axis=1) for grad in grads]
            else:
                now = [jnp.zeros((CHUNK, LANES), jnp.float32)] * 2
            for plane in range(2):
                placed = jnp.where(lane < lane_shift, last[plane], now[plane])
                accum[plane, slot + block, pl.ds(row + at, CHUNK), :] += placed
            last = now
        return carry

    lax.fori_loop(0, size // CHUNK, spread, 0, unroll=4)


def whole(shape):
    return pl.BlockSpec(shape, lambda slot, *refs: (0,) * len(shape))


def once(shape):
    return pl.BlockSpec(
        shape, lambda slot, *refs: (0,) * len(shape), pipeline_mode=pl.Buffered(1)
    )


def one_slot(shape):
    return pl.BlockSpec((1,) + shape, lambda slot, *refs: (slot,) + (0,) * len(shape))


def run_forward(offs, pieces, tables, ill):
    slots = offs.shape[0]
    size = ill.shape[-1]
    rows, cols, edge = pieces[2].shape[1], pieces[2].shape[2], pieces[3].shape[2]
    planes = jax.ShapeDtypeStruct((slots, 2, size, size), jnp.float32)
    return pl.pallas_call(
        forward_kernel,
        grid_spec=pltpu.PrefetchScalarGridSpec(
            num_scalar_prefetch=1,
            grid=(slots,),
            in_specs=[pl.BlockSpec(memory_space=pltpu.HBM)] * (len(pieces) + len(tables))
            + [once(ill.shape)],
            out_specs=[
                one_slot((2, size, size)),
                one_slot((2, size, size)),
            ],
            scratch_shapes=[
                pltpu.VMEM((2, (cols + 2 * edge) // LANES, 3 * rows, LANES), jnp.float32),
                pltpu.VMEM((2 * size, 2 * size), jnp.bfloat16),
                pltpu.VMEM((2 * size, 2 * size), jnp.bfloat16),
                pltpu.VMEM((2 * size, size), jnp.bfloat16),
                pltpu.VMEM((size, 2 * size), jnp.bfloat16),
                pltpu.SemaphoreType.DMA((24,)),
                pltpu.SemaphoreType.DMA((8,)),
            ],
        ),
        out_shape=[planes, planes],
        cost_estimate=pl.CostEstimate(
            flops=slots * 16 * size**3, bytes_accessed=30_000_000, transcendentals=0
        ),
        compiler_params=pltpu.CompilerParams(vmem_limit_bytes=67_000_000),
        name="forward",
    )(offs, *pieces, *tables, ill)


def run_backward(offs, order, far, patch, amp, ill, tables, region_shape):
    slots = offs.shape[0]
    size = ill.shape[-1]
    senders, _, per, height, _ = amp.shape
    sums_shape = (size // LANES, size // PIECE, 3, PIECE, LANES)
    return pl.pallas_call(
        backward_kernel,
        grid_spec=pltpu.PrefetchScalarGridSpec(
            num_scalar_prefetch=2,
            grid=(slots,),
            in_specs=[
                one_slot((2, size, size)),
                one_slot((2, size, size)),
                pl.BlockSpec(
                    (senders, 1, per, height, size), lambda slot, *refs: (0, slot, 0, 0, 0)
                ),
                once(ill.shape),
            ]
            + [pl.BlockSpec(memory_space=pltpu.HBM)] * len(tables),
            out_specs=[whole(region_shape), whole(sums_shape)],
            scratch_shapes=[
                pltpu.VMEM((2 * size, size), jnp.bfloat16),
                pltpu.VMEM((size, 2 * size), jnp.bfloat16),
                pltpu.VMEM((2, size, size), jnp.float32),
                pltpu.VMEM((2 * size, 2 * size), jnp.bfloat16),
                pltpu.VMEM((2 * size, 2 * size), jnp.bfloat16),
                pltpu.SMEM((senders * per,), jnp.int32),
                pltpu.SemaphoreType.DMA((8,)),
            ],
        ),
        out_shape=[
            jax.ShapeDtypeStruct(region_shape, jnp.float32),
            jax.ShapeDtypeStruct(sums_shape, jnp.float32),
        ],
        cost_estimate=pl.CostEstimate(
            flops=slots * 16 * size**3, bytes_accessed=30_000_000, transcendentals=0
        ),
        compiler_params=pltpu.CompilerParams(vmem_limit_bytes=67_000_000),
        name="backward",
    )(offs, order, far, patch, amp, ill, *tables)


def unpack_kernel(packed, out):
    size = out.shape[1]
    for plane in range(2):
        out[plane] = packed[:, plane].reshape(size, LANES)


def unpacked(packed, size):
    packed = packed.reshape(size * size // (PIECE * LANES), 2, PIECE, LANES)
    return pl.pallas_call(
        unpack_kernel,
        grid=(size // LANES,),
        in_specs=[pl.BlockSpec((size // PIECE, 2, PIECE, LANES), lambda at: (at, 0, 0, 0))],
        out_specs=pl.BlockSpec((2, size, LANES), lambda at: (0, 0, at)),
        out_shape=jax.ShapeDtypeStruct((2, size, size), jnp.float32),
        name="unpack",
    )(packed)


def spread_out(value):
    return lax.all_to_all(value, ("row", "col"), split_axis=0, concat_axis=0, tiled=True)


def shards(measured, module_row, scan_offsets, specimen, illumination):
    slots = scan_offsets.shape[2]
    size = illumination.shape[-1]
    tile_rows = specimen.shape[1]
    tile_cols = specimen.shape[2]
    senders = lax.axis_size("row")
    devices = senders * lax.axis_size("col")
    per, height = measured.shape[1], measured.shape[2]
    late = slots // 2
    edge = tile_cols // 2
    grouped = measured.reshape(senders, slots, per, height, size)
    upper = passed_along(specimen, "row", 1)
    lower = passed_along(specimen, "row", -1)
    early_offs = passed_along(scan_offsets[0, 0, :late], "row", 1)
    late_offs = passed_both(scan_offsets[0, 0, late:], 1, 1)
    offs = jnp.concatenate([late_offs, early_offs], axis=0)
    moved = passed_along(grouped[:, late:], "col", 1)
    west = passed_along(specimen[:, :, edge:], "col", 1)
    east = passed_along(specimen[:, :, :edge], "col", -1)
    levels = jnp.concatenate([moved, grouped[:, :late]], axis=1)
    lane = lax.broadcasted_iota(jnp.int32, (devices, 1, LANES), 2)
    peak = jnp.max(jnp.abs(specimen))
    power = jnp.sum(specimen * specimen)
    stats = jnp.where(lane < LANES // 2, peak, power)
    peaks = spread_out(stats)
    peak = jnp.maximum(jnp.max(peaks[:, :, : LANES // 2]), 1e-12)
    power = jnp.max(peaks[:, :, LANES // 2 :])
    tables = dft_tables(size)
    upper, lower, west, east, offs, levels, peak, power, probe = (
        lax.optimization_barrier(
            (upper, lower, west, east, offs, levels, peak, power, illumination)
        )
    )
    ill_power = jnp.sum(probe * probe)
    ill_peak = jnp.maximum(jnp.max(jnp.abs(probe)), 1e-8)
    modulus = 1.5 * peak
    energy = jnp.minimum(
        modulus * jnp.sqrt(ill_power), 1.5 * ill_peak * jnp.sqrt(6.0 * power)
    )
    change_bound = 9.0 * jnp.maximum(energy, 1e-20)
    grad_bound = 24.0 * ill_peak * change_bound
    sum_bound = slots * modulus * change_bound
    density_bound = slots * modulus * modulus
    step_bound = math.sqrt(slots * devices) * change_bound
    west_edges = jnp.concatenate([upper[:, :, edge:], lower[:, :, edge:]], axis=1)
    east_edges = jnp.concatenate([upper[:, :, :edge], lower[:, :, :edge]], axis=1)
    outer_west = passed_along(west_edges, "col", 1)
    outer_east = passed_along(east_edges, "col", -1)
    arrived = lax.all_to_all(
        levels,
        "row",
        split_axis=0,
        concat_axis=0,
        tiled=True,
        axis_index_groups=[[(sender + 1) % senders for sender in range(senders)]],
    )
    pieces = (upper, lower, specimen, west, east, outer_west, outer_east)
    far, patch = run_forward(offs, pieces, tables, illumination)
    region_shape = (2, (tile_cols + 2 * edge) // LANES, 3 * tile_rows, LANES)
    accum, sums = run_backward(
        offs, module_row, far, patch, arrived, illumination, tables, region_shape
    )
    side = edge // LANES
    to_west = narrowed(accum[:, :side], grad_bound)
    to_east = narrowed(accum[:, -side:], grad_bound)
    from_east = passed_along(to_west, "col", -1)
    from_west = passed_along(to_east, "col", 1)
    sums = sums.reshape(devices, 3 * PIECE, LANES)
    line = lax.broadcasted_iota(jnp.int32, (1, 3 * PIECE, 1), 1)
    bounds = jnp.where(line < 2 * PIECE, sum_bound, density_bound)
    packed = narrowed(sums, bounds)
    parts = spread_out(packed)
    column = accum[:, side:-side] + jnp.concatenate(
        [widened(from_west, grad_bound), widened(from_east, grad_bound)], axis=1
    )
    to_upper = narrowed(column[:, :, :tile_rows], grad_bound)
    to_lower = narrowed(column[:, :, 2 * tile_rows :], grad_bound)
    from_lower = passed_along(to_upper, "row", -1)
    from_upper = passed_along(to_lower, "row", 1)
    total = jnp.sum(widened(parts, bounds), axis=0)
    mine = total[: 2 * PIECE].reshape(2, PIECE, LANES) / jnp.sqrt(total[2 * PIECE :] + 1e-06)
    mine = narrowed(mine, step_bound).reshape(1, 2 * PIECE, LANES)
    copies = jnp.broadcast_to(mine, (devices, 2 * PIECE, LANES))
    result = spread_out(copies)
    illumination_step = unpacked(widened(result, step_bound), size)
    middle = (
        column[:, :, tile_rows : 2 * tile_rows]
        + widened(from_lower, grad_bound)
        + widened(from_upper, grad_bound)
    )
    specimen_step = middle.swapaxes(1, 2).reshape(2, tile_rows, tile_cols)
    return (specimen_step, illumination_step)


def solution(mesh):
    return jax.shard_map(
        shards,
        mesh=mesh,
        in_specs=(
            P("col", "row", None, None),
            P(),
            P("row", "col", None, None),
            P(None, "row", "col"),
            P(),
        ),
        out_specs=(P(None, "row", "col"), P()),
        check_vma=False,
    )
```

```python
import math

import jax
import jax.numpy as jnp
import numpy as np
from jax import lax
from jax.experimental import pallas as pl
from jax.experimental.pallas import tpu as pltpu
from jax.sharding import PartitionSpec as P


LANES = 128
SUBLANES = 8
CHUNK = 32
BLOCK = 256
PIECE = 16


def passed_along(value, axis, steps):
    count = lax.axis_size(axis)
    pairs = [(source, (source + steps) % count) for source in range(count)]
    return lax.ppermute(value, axis, pairs)


def passed_both(value, row_steps, col_steps):
    rows, cols = lax.axis_size("row"), lax.axis_size("col")
    pairs = [
        (row * cols + col, (row + row_steps) % rows * cols + (col + col_steps) % cols)
        for row in range(rows)
        for col in range(cols)
    ]
    return lax.ppermute(value, ("row", "col"), pairs)


def dft_tables(size):
    index = np.arange(size, dtype=np.int64)
    wrapped = index[:, None] * index[None, :] % size
    angle = wrapped.astype(np.float32) * np.float32(2.0 * math.pi / size)
    norm = np.float32(1.0 / math.sqrt(size))
    cos_table = np.cos(angle.astype(np.float64)).astype(np.float32) * norm
    sin_table = -np.sin(angle.astype(np.float64)).astype(np.float32) * norm
    tables = (cos_table, sin_table, -sin_table)
    return tuple(jnp.asarray(table, jnp.bfloat16) for table in tables)


def exponent(bound):
    return jnp.ceil(jnp.log2(jnp.maximum(bound, 1e-30))) + 1.0


def narrowed(value, power):
    return (value * jnp.exp2(15.0 - power)).astype(jnp.float16)


def widened(value, power):
    return value.astype(jnp.float32) * jnp.exp2(power - 15.0)


def relabelled(value, power):
    line = lax.broadcasted_iota(jnp.int32, (value.shape[-2], 1), 0)
    body = value.shape[-2] - SUBLANES
    return (value * jnp.where(line < body, jnp.exp2(15.0 - power), 1.0)).astype(jnp.float16)


def labelled(value, power):
    label = jnp.broadcast_to(power, value.shape[:-2] + (SUBLANES, value.shape[-1]))
    return jnp.concatenate([narrowed(value, power), label.astype(jnp.float16)], axis=-2)


def opened(value):
    power = value[(0,) * (value.ndim - 2) + (-1, 0)].astype(jnp.float32)
    return widened(value[..., :-SUBLANES, :], power), power


def table_copies(tables, left, right, sems):
    cos_table, sin_table, negative = tables
    size = cos_table.shape[-1]
    low, high = pl.ds(0, size), pl.ds(size, size)
    moves = [
        (cos_table, left, low, low),
        (cos_table, left, high, high),
        (negative, left, low, high),
        (sin_table, left, high, low),
        (cos_table, right, low, low),
        (cos_table, right, high, high),
        (sin_table, right, low, high),
        (negative, right, high, low),
    ]
    return [
        pltpu.make_async_copy(source, table.at[rows, columns], sems.at[index])
        for index, (source, table, rows, columns) in enumerate(moves)
    ]


def region_copies(pieces, region, sems):
    upper, lower, middle, west, east, outer_west, outer_east = pieces
    rows, cols, edge = middle.shape[1], middle.shape[2], west.shape[2]
    center, right = edge // LANES, (edge + cols) // LANES
    moves = [
        (upper, 0, 0, center),
        (middle, 0, 1, center),
        (lower, 0, 2, center),
        (west, 0, 1, 0),
        (east, 0, 1, right),
        (outer_west, 0, 0, 0),
        (outer_west, 1, 2, 0),
        (outer_east, 0, 0, right),
        (outer_east, 1, 2, right),
    ]
    copies = []
    for piece, source, target, first in moves:
        for block in range(piece.shape[2] // LANES):
            copies.append(
                pltpu.make_async_copy(
                    piece.at[:, pl.ds(source * rows, rows), pl.ds(block * LANES, LANES)],
                    region.at[:, first + block, pl.ds(target * rows, rows)],
                    sems.at[len(copies)],
                )
            )
    return copies


def folded(block, combine):
    parts = [block[at : at + SUBLANES] for at in range(0, block.shape[0], SUBLANES)]
    while len(parts) > 1:
        parts = [combine(*pair) for pair in zip(parts[::2], parts[1::2])]
    return parts[0]


def forward_kernel(offs, *refs):
    pieces, tables, refs = refs[:7], refs[7:10], refs[10:]
    ill, far, patch, stats, region, left, right, wave, half, region_sems, table_sems = refs
    slot = pl.program_id(0)
    size = ill.shape[-1]
    row = offs[slot, 0]
    lane_shift = offs[slot, 1] % LANES
    lane = lax.broadcasted_iota(jnp.int32, (CHUNK, LANES), 1)
    blocks = size // LANES

    @pl.when(slot == 0)
    def _():
        region_moves = region_copies(pieces, region, region_sems)
        table_moves = table_copies(tables, left, right, table_sems)
        for move in region_moves + table_moves:
            move.start()
        stats[...] = jnp.zeros_like(stats)
        for move in region_moves:
            move.wait()

    def extract(step, carry):
        peak, power = carry
        at = pl.multiple_of(step * CHUNK, CHUNK)
        last = [None, None]
        for block in range(blocks + 1):
            now = [
                pltpu.roll(
                    region[plane, slot + block, pl.ds(row + at, CHUNK), :],
                    (LANES - lane_shift) % LANES,
                    axis=1,
                )
                for plane in range(2)
            ]
            if block > 0:
                to = slice((block - 1) * LANES, block * LANES)
                spec_real, spec_imag = (
                    jnp.where(lane < LANES - lane_shift, last[plane], now[plane])
                    for plane in range(2)
                )
                patch[0, 0, pl.ds(at, CHUNK), to] = spec_real
                patch[0, 1, pl.ds(at, CHUNK), to] = spec_imag
                ill_real = ill[0, pl.ds(at, CHUNK), to]
                ill_imag = ill[1, pl.ds(at, CHUNK), to]
                wave_real = ill_real * spec_real - ill_imag * spec_imag
                wave_imag = ill_real * spec_imag + ill_imag * spec_real
                wave[pl.ds(at, CHUNK), to] = wave_real.astype(jnp.bfloat16)
                wave[pl.ds(size + at, CHUNK), to] = wave_imag.astype(jnp.bfloat16)
                most = jnp.maximum(jnp.abs(spec_real), jnp.abs(spec_imag))
                peak = jnp.maximum(peak, folded(most, jnp.maximum))
                power = power + folded(wave_real * wave_real + wave_imag * wave_imag, jnp.add)
            last = now
        return peak, power

    empty = jnp.zeros((SUBLANES, LANES), jnp.float32)
    peak, power = lax.fori_loop(0, size // CHUNK, extract, (empty, empty), unroll=4)
    stats[0] = jnp.maximum(stats[0], peak)
    stats[1] = stats[1] + power

    @pl.when(slot == 0)
    def _():
        for move in table_copies(tables, left, right, table_sems):
            move.wait()

    for block in range(size // BLOCK):
        to = slice(block * BLOCK, (block + 1) * BLOCK)
        also = slice(size + block * BLOCK, size + (block + 1) * BLOCK)
        product = jnp.dot(left[...], wave[:, to], preferred_element_type=jnp.float32)
        half[:, to] = product[:size].astype(jnp.bfloat16)
        half[:, also] = product[size:].astype(jnp.bfloat16)
    for plane in range(2):
        for block in range(size // BLOCK):
            to = slice(block * BLOCK, (block + 1) * BLOCK)
            of = slice(plane * size + block * BLOCK, plane * size + (block + 1) * BLOCK)
            far[0, plane, :, to] = jnp.dot(
                half[...], right[:, of], preferred_element_type=jnp.float32
            )


def backward_kernel(
    offs,
    order,
    powers,
    far,
    patch,
    amp,
    ill,
    cos_table,
    sin_table,
    negative,
    accum,
    sums,
    corr,
    back,
    change,
    left,
    right,
    inverse,
    table_sems,
):
    slot = pl.program_id(0)
    size = ill.shape[-1]
    modules = size // amp.shape[3]
    senders = amp.shape[0]
    row = offs[slot, 0]
    lane_shift = offs[slot, 1] % LANES
    tables = (cos_table, sin_table, negative)
    blocks = size // LANES
    height = amp.shape[3]
    per = amp.shape[2]

    @pl.when(slot == 0)
    def _():
        for move in table_copies(tables, left, right, table_sems):
            move.start()
        sums[...] = jnp.zeros_like(sums)
        label_line = lax.broadcasted_iota(jnp.int32, sums.shape[:2] + (SUBLANES, LANES), 2)
        sums[:, :, 3 * PIECE :, :] = jnp.where(label_line == 0, powers[0], powers[1])
        height_all = accum.shape[2] - SUBLANES
        accum[:, :, height_all:, :] = jnp.full(
            accum.shape[:2] + (SUBLANES, LANES), powers[2], jnp.float32
        )

        def clear(step, carry):
            at = pl.multiple_of(step * CHUNK, CHUNK)
            accum[:, :, pl.ds(at, CHUNK), :] = jnp.zeros(
                (2, accum.shape[1], CHUNK, LANES), jnp.float32
            )
            return carry

        lax.fori_loop(0, height_all // CHUNK, clear, 0)

        def invert(module, carry):
            inverse[order[module]] = module
            return carry

        lax.fori_loop(0, modules, invert, 0)

    def correct(band, carry):
        at = pl.multiple_of(band * height, height)
        module = inverse[band]
        rows = pl.ds(at, height)
        far_real = far[0, 0, rows, :]
        far_imag = far[0, 1, rows, :]
        sender = (module // per + senders - 1) % senders
        level = amp[sender, 0, module % per].astype(jnp.float32)
        inverse_size = lax.rsqrt(far_real * far_real + far_imag * far_imag)
        factor = level * jnp.minimum(inverse_size, 4.0) - 1.0
        corr[rows, :] = (factor * far_real).astype(jnp.bfloat16)
        corr[pl.ds(size + at, height), :] = (factor * far_imag).astype(jnp.bfloat16)
        return carry

    lax.fori_loop(0, modules, correct, 0, unroll=4)

    @pl.when(slot == 0)
    def _():
        for move in table_copies(tables, left, right, table_sems):
            move.wait()

    for block in range(size // BLOCK):
        to = slice(block * BLOCK, (block + 1) * BLOCK)
        also = slice(size + block * BLOCK, size + (block + 1) * BLOCK)
        product = jnp.dot(right[...], corr[:, to], preferred_element_type=jnp.float32)
        back[:, to] = product[:size].astype(jnp.bfloat16)
        back[:, also] = product[size:].astype(jnp.bfloat16)
    for plane in range(2):
        for block in range(size // BLOCK):
            to = slice(block * BLOCK, (block + 1) * BLOCK)
            of = slice(plane * size + block * BLOCK, plane * size + (block + 1) * BLOCK)
            change[plane, :, to] = jnp.dot(
                back[...], left[:, of], preferred_element_type=jnp.float32
            )

    lane = lax.broadcasted_iota(jnp.int32, (CHUNK, LANES), 1)

    def spread(step, carry):
        at = pl.multiple_of(step * CHUNK, CHUNK)
        rows = pl.ds(at, CHUNK)
        last = [jnp.zeros((CHUNK, LANES), jnp.float32)] * 2
        for block in range(blocks + 1):
            if block < blocks:
                to = slice(block * LANES, (block + 1) * LANES)
                chg_real = change[0, rows, to]
                chg_imag = change[1, rows, to]
                spec_real = patch[0, 0, rows, to]
                spec_imag = patch[0, 1, rows, to]
                ill_real = ill[0, rows, to]
                ill_imag = ill[1, rows, to]
                places = pl.ds(step * (CHUNK // PIECE), CHUNK // PIECE)
                pieces = (CHUNK // PIECE, PIECE, LANES)
                sums[block, places, :PIECE] += (spec_real * chg_real + spec_imag * chg_imag).reshape(
                    pieces
                )
                sums[block, places, PIECE : 2 * PIECE] += (spec_real * chg_imag - spec_imag * chg_real).reshape(
                    pieces
                )
                sums[block, places, 2 * PIECE : 3 * PIECE] += (spec_real * spec_real + spec_imag * spec_imag).reshape(
                    pieces
                )
                grads = (
                    ill_real * chg_real + ill_imag * chg_imag,
                    ill_real * chg_imag - ill_imag * chg_real,
                )
                now = [pltpu.roll(grad, lane_shift, axis=1) for grad in grads]
            else:
                now = [jnp.zeros((CHUNK, LANES), jnp.float32)] * 2
            for plane in range(2):
                placed = jnp.where(lane < lane_shift, last[plane], now[plane])
                accum[plane, slot + block, pl.ds(row + at, CHUNK), :] += placed
            last = now
        return carry

    lax.fori_loop(0, size // CHUNK, spread, 0, unroll=4)


def whole(shape):
    return pl.BlockSpec(shape, lambda slot, *refs: (0,) * len(shape))


def once(shape):
    return pl.BlockSpec(
        shape, lambda slot, *refs: (0,) * len(shape), pipeline_mode=pl.Buffered(1)
    )


def one_slot(shape):
    return pl.BlockSpec((1,) + shape, lambda slot, *refs: (slot,) + (0,) * len(shape))


def run_forward(offs, pieces, tables, ill):
    slots = offs.shape[0]
    size = ill.shape[-1]
    rows, cols, edge = pieces[2].shape[1], pieces[2].shape[2], pieces[3].shape[2]
    planes = jax.ShapeDtypeStruct((slots, 2, size, size), jnp.float32)
    return pl.pallas_call(
        forward_kernel,
        grid_spec=pltpu.PrefetchScalarGridSpec(
            num_scalar_prefetch=1,
            grid=(slots,),
            in_specs=[pl.BlockSpec(memory_space=pltpu.HBM)] * (len(pieces) + len(tables))
            + [once(ill.shape)],
            out_specs=[
                one_slot((2, size, size)),
                one_slot((2, size, size)),
                whole((2, SUBLANES, LANES)),
            ],
            scratch_shapes=[
                pltpu.VMEM((2, (cols + 2 * edge) // LANES, 3 * rows, LANES), jnp.float32),
                pltpu.VMEM((2 * size, 2 * size), jnp.bfloat16),
                pltpu.VMEM((2 * size, 2 * size), jnp.bfloat16),
                pltpu.VMEM((2 * size, size), jnp.bfloat16),
                pltpu.VMEM((size, 2 * size), jnp.bfloat16),
                pltpu.SemaphoreType.DMA((24,)),
                pltpu.SemaphoreType.DMA((8,)),
            ],
        ),
        out_shape=[planes, planes, jax.ShapeDtypeStruct((2, SUBLANES, LANES), jnp.float32)],
        cost_estimate=pl.CostEstimate(
            flops=slots * 16 * size**3, bytes_accessed=30_000_000, transcendentals=0
        ),
        compiler_params=pltpu.CompilerParams(vmem_limit_bytes=67_000_000),
        name="forward",
    )(offs, *pieces, *tables, ill)


def run_backward(offs, order, powers, far, patch, amp, ill, tables, region_shape):
    slots = offs.shape[0]
    size = ill.shape[-1]
    senders, _, per, height, _ = amp.shape
    sums_shape = (size // LANES, size // PIECE, 3 * PIECE + SUBLANES, LANES)
    return pl.pallas_call(
        backward_kernel,
        grid_spec=pltpu.PrefetchScalarGridSpec(
            num_scalar_prefetch=3,
            grid=(slots,),
            in_specs=[
                one_slot((2, size, size)),
                one_slot((2, size, size)),
                pl.BlockSpec(
                    (senders, 1, per, height, size), lambda slot, *refs: (0, slot, 0, 0, 0)
                ),
                once(ill.shape),
            ]
            + [pl.BlockSpec(memory_space=pltpu.HBM)] * len(tables),
            out_specs=[whole(region_shape), whole(sums_shape)],
            scratch_shapes=[
                pltpu.VMEM((2 * size, size), jnp.bfloat16),
                pltpu.VMEM((size, 2 * size), jnp.bfloat16),
                pltpu.VMEM((2, size, size), jnp.float32),
                pltpu.VMEM((2 * size, 2 * size), jnp.bfloat16),
                pltpu.VMEM((2 * size, 2 * size), jnp.bfloat16),
                pltpu.SMEM((senders * per,), jnp.int32),
                pltpu.SemaphoreType.DMA((8,)),
            ],
        ),
        out_shape=[
            jax.ShapeDtypeStruct(region_shape, jnp.float32),
            jax.ShapeDtypeStruct(sums_shape, jnp.float32),
        ],
        cost_estimate=pl.CostEstimate(
            flops=slots * 16 * size**3, bytes_accessed=30_000_000, transcendentals=0
        ),
        compiler_params=pltpu.CompilerParams(vmem_limit_bytes=67_000_000),
        name="backward",
    )(offs, order, powers, far, patch, amp, ill, *tables)


def unpack_kernel(packed, out):
    size = out.shape[1]
    for plane in range(2):
        out[plane] = packed[:, plane].reshape(size, LANES)


def unpacked(packed, size):
    packed = packed.reshape(size * size // (PIECE * LANES), 2, PIECE, LANES)
    return pl.pallas_call(
        unpack_kernel,
        grid=(size // LANES,),
        in_specs=[pl.BlockSpec((size // PIECE, 2, PIECE, LANES), lambda at: (at, 0, 0, 0))],
        out_specs=pl.BlockSpec((2, size, LANES), lambda at: (0, 0, at)),
        out_shape=jax.ShapeDtypeStruct((2, size, size), jnp.float32),
        name="unpack",
    )(packed)


def spread_out(value):
    return lax.all_to_all(value, ("row", "col"), split_axis=0, concat_axis=0, tiled=True)


def shards(measured, module_row, scan_offsets, specimen, illumination):
    slots = scan_offsets.shape[2]
    size = illumination.shape[-1]
    tile_rows = specimen.shape[1]
    tile_cols = specimen.shape[2]
    senders = lax.axis_size("row")
    devices = senders * lax.axis_size("col")
    per, height = measured.shape[1], measured.shape[2]
    late = slots // 2
    edge = tile_cols // 2
    grouped = measured.reshape(senders, slots, per, height, size)
    upper = passed_along(specimen, "row", 1)
    lower = passed_along(specimen, "row", -1)
    early_offs = passed_along(scan_offsets[0, 0, :late], "row", 1)
    late_offs = passed_both(scan_offsets[0, 0, late:], 1, 1)
    offs = jnp.concatenate([late_offs, early_offs], axis=0)
    moved = passed_along(grouped[:, late:], "col", 1)
    west = passed_along(specimen[:, :, edge:], "col", 1)
    east = passed_along(specimen[:, :, :edge], "col", -1)
    levels = jnp.concatenate([moved, grouped[:, :late]], axis=1)
    tables = dft_tables(size)
    upper, lower, west, east, offs, levels, probe = lax.optimization_barrier(
        (upper, lower, west, east, offs, levels, illumination)
    )
    ill_power = exponent(2.0 * jnp.max(jnp.abs(probe)))
    west_edges = jnp.concatenate([upper[:, :, edge:], lower[:, :, edge:]], axis=1)
    east_edges = jnp.concatenate([upper[:, :, :edge], lower[:, :, :edge]], axis=1)
    outer_west = passed_along(west_edges, "col", 1)
    outer_east = passed_along(east_edges, "col", -1)
    arrived = lax.all_to_all(
        levels,
        "row",
        split_axis=0,
        concat_axis=0,
        tiled=True,
        axis_index_groups=[[(sender + 1) % senders for sender in range(senders)]],
    )
    pieces = (upper, lower, specimen, west, east, outer_west, outer_east)
    far, patch, stats = run_forward(offs, pieces, tables, illumination)
    patch_power = exponent(1.5 * jnp.max(stats[0]))
    change_power = exponent(12.0 * jnp.sqrt(jnp.sum(stats[1])))
    home_power = ill_power + change_power + 1.0
    region_shape = (2, (tile_cols + 2 * edge) // LANES, 3 * tile_rows + SUBLANES, LANES)
    powers = jnp.stack([patch_power, change_power, home_power])
    accum, sums = run_backward(
        offs, module_row, powers, far, patch, arrived, illumination, tables, region_shape
    )
    side = edge // LANES
    to_west = relabelled(accum[:, :side], home_power)
    to_east = relabelled(accum[:, -side:], home_power)
    from_east = passed_along(to_west, "col", -1)
    from_west = passed_along(to_east, "col", 1)
    sums = sums.reshape(devices, 3 * PIECE + SUBLANES, LANES)
    line = lax.broadcasted_iota(jnp.int32, (1, 3 * PIECE + SUBLANES, 1), 1)
    scales = jnp.where(
        line < 2 * PIECE,
        jnp.exp2(14.0 - patch_power - change_power),
        jnp.where(line < 3 * PIECE, jnp.exp2(13.0 - 2.0 * patch_power), 1.0),
    )
    packed = (sums * scales).astype(jnp.float16)
    parts = spread_out(packed)
    body = 3 * tile_rows
    from_west, west_power = opened(from_west)
    from_east, east_power = opened(from_east)
    column = accum[:, side:-side, :body] + jnp.concatenate([from_west, from_east], axis=1)
    column_power = jnp.maximum(jnp.maximum(west_power, east_power), home_power) + 2.0
    to_upper = labelled(column[:, :, :tile_rows], column_power)
    to_lower = labelled(column[:, :, 2 * tile_rows : body], column_power)
    from_lower = passed_along(to_upper, "row", -1)
    from_upper = passed_along(to_lower, "row", 1)
    labels = parts[:, 3 * PIECE :].astype(jnp.float32)
    patch_powers, change_powers = labels[:, :1, :1], labels[:, 1:2, :1]
    line = line[:, : 3 * PIECE]
    powers = jnp.where(
        line < 2 * PIECE, patch_powers + change_powers + 1.0, 2.0 * patch_powers + 2.0
    )
    total = jnp.sum(widened(parts[:, : 3 * PIECE], powers), axis=0)
    mine = total[: 2 * PIECE].reshape(2, PIECE, LANES) / jnp.sqrt(total[2 * PIECE :] + 1e-06)
    step_power = jnp.max(change_powers) + math.ceil(0.5 * math.log2(slots * devices))
    mine = narrowed(mine, step_power).reshape(1, 2 * PIECE, LANES)
    copies = jnp.broadcast_to(mine, (devices, 2 * PIECE, LANES))
    result = spread_out(copies)
    illumination_step = unpacked(widened(result, step_power), size)
    middle = (
        column[:, :, tile_rows : 2 * tile_rows]
        + opened(from_lower)[0]
        + opened(from_upper)[0]
    )
    specimen_step = middle.swapaxes(1, 2).reshape(2, tile_rows, tile_cols)
    return (specimen_step, illumination_step)


def solution(mesh):
    return jax.shard_map(
        shards,
        mesh=mesh,
        in_specs=(
            P("col", "row", None, None),
            P(),
            P("row", "col", None, None),
            P(None, "row", "col"),
            P(),
        ),
        out_specs=(P(None, "row", "col"), P()),
        check_vma=False,
    )
```

```python
import math

import jax
import jax.numpy as jnp
import numpy as np
from jax import lax
from jax.experimental import pallas as pl
from jax.experimental.pallas import tpu as pltpu
from jax.sharding import PartitionSpec as P


LANES = 128
SUBLANES = 8
CHUNK = 32
BLOCK = 256
PIECE = 16


def passed_along(value, axis, steps):
    count = lax.axis_size(axis)
    pairs = [(source, (source + steps) % count) for source in range(count)]
    return lax.ppermute(value, axis, pairs)


def passed_both(value, row_steps, col_steps):
    rows, cols = lax.axis_size("row"), lax.axis_size("col")
    pairs = [
        (row * cols + col, (row + row_steps) % rows * cols + (col + col_steps) % cols)
        for row in range(rows)
        for col in range(cols)
    ]
    return lax.ppermute(value, ("row", "col"), pairs)


def dft_tables(size):
    index = np.arange(size, dtype=np.int64)
    wrapped = index[:, None] * index[None, :] % size
    angle = wrapped.astype(np.float32) * np.float32(2.0 * math.pi / size)
    norm = np.float32(1.0 / math.sqrt(size))
    cos_table = np.cos(angle.astype(np.float64)).astype(np.float32) * norm
    sin_table = -np.sin(angle.astype(np.float64)).astype(np.float32) * norm
    tables = (cos_table, sin_table, -sin_table)
    return tuple(jnp.asarray(table, jnp.bfloat16) for table in tables)


def exponent(bound):
    return jnp.ceil(jnp.log2(jnp.maximum(bound, 1e-30))) + 1.0


def narrowed(value, power):
    return (value * jnp.exp2(15.0 - power)).astype(jnp.float16)


def widened(value, power):
    return value.astype(jnp.float32) * jnp.exp2(power - 15.0)


def relabelled(value, power):
    line = lax.broadcasted_iota(jnp.int32, (value.shape[-2], 1), 0)
    body = value.shape[-2] - SUBLANES
    return (value * jnp.where(line < body, jnp.exp2(15.0 - power), 1.0)).astype(jnp.float16)


def labelled(value, power):
    label = jnp.broadcast_to(power, value.shape[:-2] + (SUBLANES, value.shape[-1]))
    return jnp.concatenate([narrowed(value, power), label.astype(jnp.float16)], axis=-2)


def opened(value):
    power = value[(0,) * (value.ndim - 2) + (-1, 0)].astype(jnp.float32)
    return widened(value[..., :-SUBLANES, :], power), power


def table_copies(tables, left, right, sems):
    cos_table, sin_table, negative = tables
    size = cos_table.shape[-1]
    low, high = pl.ds(0, size), pl.ds(size, size)
    moves = [
        (cos_table, left, low, low),
        (cos_table, left, high, high),
        (negative, left, low, high),
        (sin_table, left, high, low),
        (cos_table, right, low, low),
        (cos_table, right, high, high),
        (sin_table, right, low, high),
        (negative, right, high, low),
    ]
    return [
        pltpu.make_async_copy(source, table.at[rows, columns], sems.at[index])
        for index, (source, table, rows, columns) in enumerate(moves)
    ]


def region_copies(pieces, region, sems):
    middle, west, east = pieces[:3]
    rows, cols, edge = middle.shape[1], middle.shape[2], west.shape[2]
    center, right = edge // LANES, (edge + cols) // LANES
    both = pl.ds(0, 2)
    moves = [(middle, both, 0, 1, center), (west, both, 0, 1, 0), (east, both, 0, 1, right)]
    for plane in range(2):
        upper, lower, outer_west, outer_east = pieces[3 + 4 * plane : 7 + 4 * plane]
        one = pl.ds(plane, 1)
        moves += [
            (upper, one, 0, 0, center),
            (lower, one, 0, 2, center),
            (outer_west, one, 0, 0, 0),
            (outer_west, one, 1, 2, 0),
            (outer_east, one, 0, 0, right),
            (outer_east, one, 1, 2, right),
        ]
    copies = []
    for piece, planes, source, target, first in moves:
        for block in range(piece.shape[2] // LANES):
            copies.append(
                pltpu.make_async_copy(
                    piece.at[:, pl.ds(source * rows, rows), pl.ds(block * LANES, LANES)],
                    region.at[planes, first + block, pl.ds(target * rows, rows)],
                    sems.at[len(copies)],
                )
            )
    return copies


def folded(block, combine):
    parts = [block[at : at + SUBLANES] for at in range(0, block.shape[0], SUBLANES)]
    while len(parts) > 1:
        parts = [combine(*pair) for pair in zip(parts[::2], parts[1::2])]
    return parts[0]


def forward_kernel(offs, *refs):
    pieces, tables, refs = refs[:11], refs[11:14], refs[14:]
    ill, far, patch, stats, region, left, right, wave, half, region_sems, table_sems = refs
    slot = pl.program_id(0)
    size = ill.shape[-1]
    row = offs[slot, 0]
    lane_shift = offs[slot, 1] % LANES
    lane = lax.broadcasted_iota(jnp.int32, (CHUNK, LANES), 1)
    blocks = size // LANES

    @pl.when(slot == 0)
    def _():
        region_moves = region_copies(pieces, region, region_sems)
        table_moves = table_copies(tables, left, right, table_sems)
        for move in region_moves + table_moves:
            move.start()
        stats[...] = jnp.zeros_like(stats)
        for move in region_moves:
            move.wait()

    def extract(step, carry):
        peak, power = carry
        at = pl.multiple_of(step * CHUNK, CHUNK)
        last = [None, None]
        for block in range(blocks + 1):
            now = [
                pltpu.roll(
                    region[plane, slot + block, pl.ds(row + at, CHUNK), :],
                    (LANES - lane_shift) % LANES,
                    axis=1,
                )
                for plane in range(2)
            ]
            if block > 0:
                to = slice((block - 1) * LANES, block * LANES)
                spec_real, spec_imag = (
                    jnp.where(lane < LANES - lane_shift, last[plane], now[plane])
                    for plane in range(2)
                )
                patch[0, 0, pl.ds(at, CHUNK), to] = spec_real
                patch[0, 1, pl.ds(at, CHUNK), to] = spec_imag
                ill_real = ill[0, pl.ds(at, CHUNK), to]
                ill_imag = ill[1, pl.ds(at, CHUNK), to]
                wave_real = ill_real * spec_real - ill_imag * spec_imag
                wave_imag = ill_real * spec_imag + ill_imag * spec_real
                wave[pl.ds(at, CHUNK), to] = wave_real.astype(jnp.bfloat16)
                wave[pl.ds(size + at, CHUNK), to] = wave_imag.astype(jnp.bfloat16)
                most = jnp.maximum(jnp.abs(spec_real), jnp.abs(spec_imag))
                peak = jnp.maximum(peak, folded(most, jnp.maximum))
                power = power + folded(wave_real * wave_real + wave_imag * wave_imag, jnp.add)
            last = now
        return peak, power

    empty = jnp.zeros((SUBLANES, LANES), jnp.float32)
    peak, power = lax.fori_loop(0, size // CHUNK, extract, (empty, empty), unroll=4)
    stats[0] = jnp.maximum(stats[0], peak)
    stats[1] = stats[1] + power

    @pl.when(slot == 0)
    def _():
        for move in table_copies(tables, left, right, table_sems):
            move.wait()

    for block in range(size // BLOCK):
        to = slice(block * BLOCK, (block + 1) * BLOCK)
        also = slice(size + block * BLOCK, size + (block + 1) * BLOCK)
        product = jnp.dot(left[...], wave[:, to], preferred_element_type=jnp.float32)
        half[:, to] = product[:size].astype(jnp.bfloat16)
        half[:, also] = product[size:].astype(jnp.bfloat16)
    for plane in range(2):
        for block in range(size // BLOCK):
            to = slice(block * BLOCK, (block + 1) * BLOCK)
            of = slice(plane * size + block * BLOCK, plane * size + (block + 1) * BLOCK)
            far[0, plane, :, to] = jnp.dot(
                half[...], right[:, of], preferred_element_type=jnp.float32
            )


def backward_kernel(
    offs,
    order,
    powers,
    far,
    patch,
    amp,
    ill,
    cos_table,
    sin_table,
    negative,
    accum,
    sums,
    corr,
    back,
    change,
    left,
    right,
    inverse,
    table_sems,
):
    slot = pl.program_id(0)
    size = ill.shape[-1]
    modules = size // amp.shape[3]
    senders = amp.shape[0]
    row = offs[slot, 0]
    lane_shift = offs[slot, 1] % LANES
    tables = (cos_table, sin_table, negative)
    blocks = size // LANES
    height = amp.shape[3]
    per = amp.shape[2]

    @pl.when(slot == 0)
    def _():
        for move in table_copies(tables, left, right, table_sems):
            move.start()
        sums[...] = jnp.zeros_like(sums)
        label_line = lax.broadcasted_iota(jnp.int32, sums.shape[:2] + (SUBLANES, LANES), 2)
        sums[:, :, 3 * PIECE :, :] = jnp.where(label_line == 0, powers[0], powers[1])
        height_all = accum.shape[2] - SUBLANES
        accum[:, :, height_all:, :] = jnp.full(
            accum.shape[:2] + (SUBLANES, LANES), powers[2], jnp.float32
        )

        def clear(step, carry):
            at = pl.multiple_of(step * CHUNK, CHUNK)
            accum[:, :, pl.ds(at, CHUNK), :] = jnp.zeros(
                (2, accum.shape[1], CHUNK, LANES), jnp.float32
            )
            return carry

        lax.fori_loop(0, height_all // CHUNK, clear, 0)

        def invert(module, carry):
            inverse[order[module]] = module
            return carry

        lax.fori_loop(0, modules, invert, 0)

    def correct(band, carry):
        at = pl.multiple_of(band * height, height)
        module = inverse[band]
        rows = pl.ds(at, height)
        far_real = far[0, 0, rows, :]
        far_imag = far[0, 1, rows, :]
        sender = (module // per + senders - 1) % senders
        level = amp[sender, 0, module % per].astype(jnp.float32)
        inverse_size = lax.rsqrt(far_real * far_real + far_imag * far_imag)
        factor = level * jnp.minimum(inverse_size, 4.0) - 1.0
        corr[rows, :] = (factor * far_real).astype(jnp.bfloat16)
        corr[pl.ds(size + at, height), :] = (factor * far_imag).astype(jnp.bfloat16)
        return carry

    lax.fori_loop(0, modules, correct, 0, unroll=4)

    @pl.when(slot == 0)
    def _():
        for move in table_copies(tables, left, right, table_sems):
            move.wait()

    for block in range(size // BLOCK):
        to = slice(block * BLOCK, (block + 1) * BLOCK)
        also = slice(size + block * BLOCK, size + (block + 1) * BLOCK)
        product = jnp.dot(right[...], corr[:, to], preferred_element_type=jnp.float32)
        back[:, to] = product[:size].astype(jnp.bfloat16)
        back[:, also] = product[size:].astype(jnp.bfloat16)
    for plane in range(2):
        for block in range(size // BLOCK):
            to = slice(block * BLOCK, (block + 1) * BLOCK)
            of = slice(plane * size + block * BLOCK, plane * size + (block + 1) * BLOCK)
            change[plane, :, to] = jnp.dot(
                back[...], left[:, of], preferred_element_type=jnp.float32
            )

    lane = lax.broadcasted_iota(jnp.int32, (CHUNK, LANES), 1)

    def spread(step, carry):
        at = pl.multiple_of(step * CHUNK, CHUNK)
        rows = pl.ds(at, CHUNK)
        last = [jnp.zeros((CHUNK, LANES), jnp.float32)] * 2
        for block in range(blocks + 1):
            if block < blocks:
                to = slice(block * LANES, (block + 1) * LANES)
                chg_real = change[0, rows, to]
                chg_imag = change[1, rows, to]
                spec_real = patch[0, 0, rows, to]
                spec_imag = patch[0, 1, rows, to]
                ill_real = ill[0, rows, to]
                ill_imag = ill[1, rows, to]
                places = pl.ds(step * (CHUNK // PIECE), CHUNK // PIECE)
                pieces = (CHUNK // PIECE, PIECE, LANES)
                sums[block, places, :PIECE] += (spec_real * chg_real + spec_imag * chg_imag).reshape(
                    pieces
                )
                sums[block, places, PIECE : 2 * PIECE] += (spec_real * chg_imag - spec_imag * chg_real).reshape(
                    pieces
                )
                sums[block, places, 2 * PIECE : 3 * PIECE] += (spec_real * spec_real + spec_imag * spec_imag).reshape(
                    pieces
                )
                grads = (
                    ill_real * chg_real + ill_imag * chg_imag,
                    ill_real * chg_imag - ill_imag * chg_real,
                )
                now = [pltpu.roll(grad, lane_shift, axis=1) for grad in grads]
            else:
                now = [jnp.zeros((CHUNK, LANES), jnp.float32)] * 2
            for plane in range(2):
                placed = jnp.where(lane < lane_shift, last[plane], now[plane])
                accum[plane, slot + block, pl.ds(row + at, CHUNK), :] += placed
            last = now
        return carry

    lax.fori_loop(0, size // CHUNK, spread, 0, unroll=4)


def whole(shape):
    return pl.BlockSpec(shape, lambda slot, *refs: (0,) * len(shape))


def once(shape):
    return pl.BlockSpec(
        shape, lambda slot, *refs: (0,) * len(shape), pipeline_mode=pl.Buffered(1)
    )


def one_slot(shape):
    return pl.BlockSpec((1,) + shape, lambda slot, *refs: (slot,) + (0,) * len(shape))


def run_forward(offs, pieces, tables, ill):
    slots = offs.shape[0]
    size = ill.shape[-1]
    rows, cols, edge = pieces[0].shape[1], pieces[0].shape[2], pieces[1].shape[2]
    planes = jax.ShapeDtypeStruct((slots, 2, size, size), jnp.float32)
    return pl.pallas_call(
        forward_kernel,
        grid_spec=pltpu.PrefetchScalarGridSpec(
            num_scalar_prefetch=1,
            grid=(slots,),
            in_specs=[pl.BlockSpec(memory_space=pltpu.HBM)] * (len(pieces) + len(tables))
            + [once(ill.shape)],
            out_specs=[
                one_slot((2, size, size)),
                one_slot((2, size, size)),
                whole((2, SUBLANES, LANES)),
            ],
            scratch_shapes=[
                pltpu.VMEM((2, (cols + 2 * edge) // LANES, 3 * rows, LANES), jnp.float32),
                pltpu.VMEM((2 * size, 2 * size), jnp.bfloat16),
                pltpu.VMEM((2 * size, 2 * size), jnp.bfloat16),
                pltpu.VMEM((2 * size, size), jnp.bfloat16),
                pltpu.VMEM((size, 2 * size), jnp.bfloat16),
                pltpu.SemaphoreType.DMA((40,)),
                pltpu.SemaphoreType.DMA((8,)),
            ],
        ),
        out_shape=[planes, planes, jax.ShapeDtypeStruct((2, SUBLANES, LANES), jnp.float32)],
        cost_estimate=pl.CostEstimate(
            flops=slots * 16 * size**3, bytes_accessed=30_000_000, transcendentals=0
        ),
        compiler_params=pltpu.CompilerParams(vmem_limit_bytes=67_000_000),
        name="forward",
    )(offs, *pieces, *tables, ill)


def run_backward(offs, order, powers, far, patch, amp, ill, tables, region_shape):
    slots = offs.shape[0]
    size = ill.shape[-1]
    senders, _, per, height, _ = amp.shape
    sums_shape = (size // LANES, size // PIECE, 3 * PIECE + SUBLANES, LANES)
    return pl.pallas_call(
        backward_kernel,
        grid_spec=pltpu.PrefetchScalarGridSpec(
            num_scalar_prefetch=3,
            grid=(slots,),
            in_specs=[
                one_slot((2, size, size)),
                one_slot((2, size, size)),
                pl.BlockSpec(
                    (senders, 1, per, height, size), lambda slot, *refs: (0, slot, 0, 0, 0)
                ),
                once(ill.shape),
            ]
            + [pl.BlockSpec(memory_space=pltpu.HBM)] * len(tables),
            out_specs=[whole(region_shape), whole(sums_shape)],
            scratch_shapes=[
                pltpu.VMEM((2 * size, size), jnp.bfloat16),
                pltpu.VMEM((size, 2 * size), jnp.bfloat16),
                pltpu.VMEM((2, size, size), jnp.float32),
                pltpu.VMEM((2 * size, 2 * size), jnp.bfloat16),
                pltpu.VMEM((2 * size, 2 * size), jnp.bfloat16),
                pltpu.SMEM((senders * per,), jnp.int32),
                pltpu.SemaphoreType.DMA((8,)),
            ],
        ),
        out_shape=[
            jax.ShapeDtypeStruct(region_shape, jnp.float32),
            jax.ShapeDtypeStruct(sums_shape, jnp.float32),
        ],
        cost_estimate=pl.CostEstimate(
            flops=slots * 16 * size**3, bytes_accessed=30_000_000, transcendentals=0
        ),
        compiler_params=pltpu.CompilerParams(vmem_limit_bytes=67_000_000),
        name="backward",
    )(offs, order, powers, far, patch, amp, ill, *tables)


def spread_out(value):
    return lax.all_to_all(value, ("row", "col"), split_axis=0, concat_axis=0, tiled=True)


def shards(measured, module_row, scan_offsets, specimen, illumination):
    slots = scan_offsets.shape[2]
    size = illumination.shape[-1]
    tile_rows = specimen.shape[1]
    tile_cols = specimen.shape[2]
    senders = lax.axis_size("row")
    devices = senders * lax.axis_size("col")
    per, height = measured.shape[1], measured.shape[2]
    late = slots // 2
    edge = tile_cols // 2
    grouped = measured.reshape(senders, slots, per, height, size)
    uppers, lowers = [], []
    for plane in range(2):
        uppers.append(passed_along(specimen[plane : plane + 1], "row", 1))
        lowers.append(passed_along(specimen[plane : plane + 1], "row", -1))
    early_offs = passed_along(scan_offsets[0, 0, :late], "row", 1)
    late_offs = passed_both(scan_offsets[0, 0, late:], 1, 1)
    offs = jnp.concatenate([late_offs, early_offs], axis=0)
    moved = passed_along(grouped[:, late:], "col", 1)
    west = passed_along(specimen[:, :, edge:], "col", 1)
    east = passed_along(specimen[:, :, :edge], "col", -1)
    levels = jnp.concatenate([moved, grouped[:, :late]], axis=1)
    tables = dft_tables(size)
    outers = []
    for plane in range(2):
        upper, lower = uppers[plane], lowers[plane]
        west_edges = jnp.concatenate([upper[:, :, edge:], lower[:, :, edge:]], axis=1)
        east_edges = jnp.concatenate([upper[:, :, :edge], lower[:, :, :edge]], axis=1)
        if plane == 0:
            uppers[1], lowers[1], _, _ = lax.optimization_barrier(
                (uppers[1], lowers[1], west_edges, east_edges)
            )
        outer_west = passed_along(west_edges, "col", 1)
        outer_east = passed_along(east_edges, "col", -1)
        outers.append((upper, lower, outer_west, outer_east))
    levels, probe, _ = lax.optimization_barrier((levels, illumination, uppers[0]))
    ill_power = exponent(2.0 * jnp.max(jnp.abs(probe)))
    arrived = lax.all_to_all(
        levels,
        "row",
        split_axis=0,
        concat_axis=0,
        tiled=True,
        axis_index_groups=[[(sender + 1) % senders for sender in range(senders)]],
    )
    pieces = (specimen, west, east) + outers[0] + outers[1]
    far, patch, stats = run_forward(offs, pieces, tables, illumination)
    patch_power = exponent(1.5 * jnp.max(stats[0]))
    change_power = exponent(12.0 * jnp.sqrt(jnp.sum(stats[1])))
    home_power = ill_power + change_power + 1.0
    region_shape = (2, (tile_cols + 2 * edge) // LANES, 3 * tile_rows + SUBLANES, LANES)
    powers = jnp.stack([patch_power, change_power, home_power])
    accum, sums = run_backward(
        offs, module_row, powers, far, patch, arrived, illumination, tables, region_shape
    )
    side = edge // LANES
    to_west = relabelled(accum[:, :side], home_power)
    to_east = relabelled(accum[:, -side:], home_power)
    from_east = passed_along(to_west, "col", -1)
    from_west = passed_along(to_east, "col", 1)
    sums = sums.reshape(devices, 3 * PIECE + SUBLANES, LANES)
    line = lax.broadcasted_iota(jnp.int32, (1, 3 * PIECE + SUBLANES, 1), 1)
    scales = jnp.where(
        line < 2 * PIECE,
        jnp.exp2(14.0 - patch_power - change_power),
        jnp.where(line < 3 * PIECE, jnp.exp2(13.0 - 2.0 * patch_power), 1.0),
    )
    packed = (sums * scales).astype(jnp.float16)
    parts = spread_out(packed)
    body = 3 * tile_rows
    from_west, west_power = opened(from_west)
    from_east, east_power = opened(from_east)
    column = accum[:, side:-side, :body] + jnp.concatenate([from_west, from_east], axis=1)
    column_power = jnp.maximum(jnp.maximum(west_power, east_power), home_power) + 2.0
    to_upper = labelled(column[:, :, :tile_rows], column_power)
    to_lower = labelled(column[:, :, 2 * tile_rows : body], column_power)
    from_lower = passed_along(to_upper, "row", -1)
    from_upper = passed_along(to_lower, "row", 1)
    labels = parts[:, 3 * PIECE :].astype(jnp.float32)
    patch_powers, change_powers = labels[:, :1, :1], labels[:, 1:2, :1]
    line = line[:, : 3 * PIECE]
    powers = jnp.where(
        line < 2 * PIECE, patch_powers + change_powers + 1.0, 2.0 * patch_powers + 2.0
    )
    total = jnp.sum(widened(parts[:, : 3 * PIECE], powers), axis=0)
    mine = total[: 2 * PIECE].reshape(2, PIECE, LANES) / jnp.sqrt(total[2 * PIECE :] + 1e-06)
    step_power = jnp.max(change_powers) + math.ceil(0.5 * math.log2(slots * devices))
    mine = narrowed(mine, step_power).reshape(1, 2 * PIECE, LANES)
    copies = jnp.broadcast_to(mine, (devices, 2 * PIECE, LANES))
    result = spread_out(copies)
    result = result.reshape(size // LANES, size // PIECE, 2, PIECE, LANES)
    result = result.transpose(2, 1, 3, 0, 4).reshape(2, size, size)
    illumination_step = widened(result, step_power)
    middle = (
        column[:, :, tile_rows : 2 * tile_rows]
        + opened(from_lower)[0]
        + opened(from_upper)[0]
    )
    specimen_step = middle.swapaxes(1, 2).reshape(2, tile_rows, tile_cols)
    return (specimen_step, illumination_step)


def solution(mesh):
    return jax.shard_map(
        shards,
        mesh=mesh,
        in_specs=(
            P("col", "row", None, None),
            P(),
            P("row", "col", None, None),
            P(None, "row", "col"),
            P(),
        ),
        out_specs=(P(None, "row", "col"), P()),
        check_vma=False,
    )
```

```python
import math

import jax
import jax.numpy as jnp
import numpy as np
from jax import lax
from jax.experimental import pallas as pl
from jax.experimental.pallas import tpu as pltpu
from jax.sharding import PartitionSpec as P


LANES = 128
SUBLANES = 8
CHUNK = 32
BLOCK = 256
PIECE = 16


def passed_along(value, axis, steps):
    count = lax.axis_size(axis)
    pairs = [(source, (source + steps) % count) for source in range(count)]
    return lax.ppermute(value, axis, pairs)


def passed_both(value, row_steps, col_steps):
    rows, cols = lax.axis_size("row"), lax.axis_size("col")
    pairs = [
        (row * cols + col, (row + row_steps) % rows * cols + (col + col_steps) % cols)
        for row in range(rows)
        for col in range(cols)
    ]
    return lax.ppermute(value, ("row", "col"), pairs)


def dft_tables(size):
    index = np.arange(size, dtype=np.int64)
    wrapped = index[:, None] * index[None, :] % size
    angle = wrapped.astype(np.float32) * np.float32(2.0 * math.pi / size)
    norm = np.float32(1.0 / math.sqrt(size))
    cos_table = np.cos(angle.astype(np.float64)).astype(np.float32) * norm
    sin_table = -np.sin(angle.astype(np.float64)).astype(np.float32) * norm
    tables = (cos_table, sin_table, -sin_table)
    return tuple(jnp.asarray(table, jnp.bfloat16) for table in tables)


def exponent(bound):
    return jnp.ceil(jnp.log2(jnp.maximum(bound, 1e-30))) + 1.0


def narrowed(value, power):
    return (value * jnp.exp2(15.0 - power)).astype(jnp.float16)


def widened(value, power):
    return value.astype(jnp.float32) * jnp.exp2(power - 15.0)


def relabelled(value, power):
    line = lax.broadcasted_iota(jnp.int32, (value.shape[-2], 1), 0)
    body = value.shape[-2] - SUBLANES
    return (value * jnp.where(line < body, jnp.exp2(15.0 - power), 1.0)).astype(jnp.float16)


def labelled(value, power):
    label = jnp.broadcast_to(power, value.shape[:-2] + (SUBLANES, value.shape[-1]))
    return jnp.concatenate([narrowed(value, power), label.astype(jnp.float16)], axis=-2)


def opened(value):
    power = value[(0,) * (value.ndim - 2) + (-1, 0)].astype(jnp.float32)
    return widened(value[..., :-SUBLANES, :], power), power


def table_copies(tables, left, right, sems):
    cos_table, sin_table, negative = tables
    size = cos_table.shape[-1]
    low, high = pl.ds(0, size), pl.ds(size, size)
    moves = [
        (cos_table, left, low, low),
        (cos_table, left, high, high),
        (negative, left, low, high),
        (sin_table, left, high, low),
        (cos_table, right, low, low),
        (cos_table, right, high, high),
        (sin_table, right, low, high),
        (negative, right, high, low),
    ]
    return [
        pltpu.make_async_copy(source, table.at[rows, columns], sems.at[index])
        for index, (source, table, rows, columns) in enumerate(moves)
    ]


def region_copies(pieces, region, sems):
    middle, west, east = pieces[:3]
    rows, cols, edge = middle.shape[1], middle.shape[2], west.shape[2]
    center, right = edge // LANES, (edge + cols) // LANES
    both = pl.ds(0, 2)
    moves = [(middle, both, 0, 1, center), (west, both, 0, 1, 0), (east, both, 0, 1, right)]
    for plane in range(2):
        upper, lower, outer_west, outer_east = pieces[3 + 4 * plane : 7 + 4 * plane]
        one = pl.ds(plane, 1)
        moves += [
            (upper, one, 0, 0, center),
            (lower, one, 0, 2, center),
            (outer_west, one, 0, 0, 0),
            (outer_west, one, 1, 2, 0),
            (outer_east, one, 0, 0, right),
            (outer_east, one, 1, 2, right),
        ]
    copies = []
    for piece, planes, source, target, first in moves:
        for block in range(piece.shape[2] // LANES):
            copies.append(
                pltpu.make_async_copy(
                    piece.at[:, pl.ds(source * rows, rows), pl.ds(block * LANES, LANES)],
                    region.at[planes, first + block, pl.ds(target * rows, rows)],
                    sems.at[len(copies)],
                )
            )
    return copies


def folded(block, combine):
    parts = [block[at : at + SUBLANES] for at in range(0, block.shape[0], SUBLANES)]
    while len(parts) > 1:
        parts = [combine(*pair) for pair in zip(parts[::2], parts[1::2])]
    return parts[0]


def forward_kernel(offs, *refs):
    pieces, tables, refs = refs[:11], refs[11:14], refs[14:]
    ill, far, patch, stats, region, left, right, wave, half, region_sems, table_sems = refs
    slot = pl.program_id(0)
    size = ill.shape[-1]
    row = offs[slot, 0]
    lane_shift = offs[slot, 1] % LANES
    lane = lax.broadcasted_iota(jnp.int32, (CHUNK, LANES), 1)
    blocks = size // LANES

    @pl.when(slot == 0)
    def _():
        region_moves = region_copies(pieces, region, region_sems)
        table_moves = table_copies(tables, left, right, table_sems)
        for move in region_moves + table_moves:
            move.start()
        stats[...] = jnp.zeros_like(stats)
        for move in region_moves:
            move.wait()

    def extract(step, carry):
        peak, power = carry
        at = pl.multiple_of(step * CHUNK, CHUNK)
        last = [None, None]
        for block in range(blocks + 1):
            now = [
                pltpu.roll(
                    region[plane, slot + block, pl.ds(row + at, CHUNK), :],
                    (LANES - lane_shift) % LANES,
                    axis=1,
                )
                for plane in range(2)
            ]
            if block > 0:
                to = slice((block - 1) * LANES, block * LANES)
                spec_real, spec_imag = (
                    jnp.where(lane < LANES - lane_shift, last[plane], now[plane])
                    for plane in range(2)
                )
                patch[0, 0, pl.ds(at, CHUNK), to] = spec_real
                patch[0, 1, pl.ds(at, CHUNK), to] = spec_imag
                ill_real = ill[0, pl.ds(at, CHUNK), to]
                ill_imag = ill[1, pl.ds(at, CHUNK), to]
                wave_real = ill_real * spec_real - ill_imag * spec_imag
                wave_imag = ill_real * spec_imag + ill_imag * spec_real
                wave[pl.ds(at, CHUNK), to] = wave_real.astype(jnp.bfloat16)
                wave[pl.ds(size + at, CHUNK), to] = wave_imag.astype(jnp.bfloat16)
                most = jnp.maximum(jnp.abs(spec_real), jnp.abs(spec_imag))
                peak = jnp.maximum(peak, folded(most, jnp.maximum))
                power = power + folded(wave_real * wave_real + wave_imag * wave_imag, jnp.add)
            last = now
        return peak, power

    empty = jnp.zeros((SUBLANES, LANES), jnp.float32)
    peak, power = lax.fori_loop(0, size // CHUNK, extract, (empty, empty), unroll=8)
    stats[0] = jnp.maximum(stats[0], peak)
    stats[1] = stats[1] + power

    @pl.when(slot == 0)
    def _():
        for move in table_copies(tables, left, right, table_sems):
            move.wait()

    for block in range(size // BLOCK):
        to = slice(block * BLOCK, (block + 1) * BLOCK)
        also = slice(size + block * BLOCK, size + (block + 1) * BLOCK)
        product = jnp.dot(left[...], wave[:, to], preferred_element_type=jnp.float32)
        half[:, to] = product[:size].astype(jnp.bfloat16)
        half[:, also] = product[size:].astype(jnp.bfloat16)
    for plane in range(2):
        for block in range(size // BLOCK):
            to = slice(block * BLOCK, (block + 1) * BLOCK)
            of = slice(plane * size + block * BLOCK, plane * size + (block + 1) * BLOCK)
            far[0, plane, :, to] = jnp.dot(
                half[...], right[:, of], preferred_element_type=jnp.float32
            )


def backward_kernel(
    offs,
    order,
    powers,
    far,
    patch,
    amp,
    ill,
    cos_table,
    sin_table,
    negative,
    accum,
    sums,
    corr,
    back,
    change,
    left,
    right,
    inverse,
    table_sems,
):
    slot = pl.program_id(0)
    size = ill.shape[-1]
    modules = size // amp.shape[3]
    senders = amp.shape[0]
    row = offs[slot, 0]
    lane_shift = offs[slot, 1] % LANES
    tables = (cos_table, sin_table, negative)
    blocks = size // LANES
    height = amp.shape[3]
    per = amp.shape[2]

    @pl.when(slot == 0)
    def _():
        for move in table_copies(tables, left, right, table_sems):
            move.start()
        sums[...] = jnp.zeros_like(sums)
        label_line = lax.broadcasted_iota(jnp.int32, sums.shape[:2] + (SUBLANES, LANES), 2)
        sums[:, :, 3 * PIECE :, :] = jnp.where(label_line == 0, powers[0], powers[1])
        height_all = accum.shape[2] - SUBLANES
        accum[:, :, height_all:, :] = jnp.full(
            accum.shape[:2] + (SUBLANES, LANES), powers[2], jnp.float32
        )

        def clear(step, carry):
            at = pl.multiple_of(step * CHUNK, CHUNK)
            accum[:, :, pl.ds(at, CHUNK), :] = jnp.zeros(
                (2, accum.shape[1], CHUNK, LANES), jnp.float32
            )
            return carry

        lax.fori_loop(0, height_all // CHUNK, clear, 0)

        def invert(module, carry):
            inverse[order[module]] = module
            return carry

        lax.fori_loop(0, modules, invert, 0)

    def correct(band, carry):
        at = pl.multiple_of(band * height, height)
        module = inverse[band]
        rows = pl.ds(at, height)
        far_real = far[0, 0, rows, :]
        far_imag = far[0, 1, rows, :]
        sender = (module // per + senders - 1) % senders
        level = amp[sender, 0, module % per].astype(jnp.float32)
        inverse_size = lax.rsqrt(far_real * far_real + far_imag * far_imag)
        factor = level * jnp.minimum(inverse_size, 4.0) - 1.0
        corr[rows, :] = (factor * far_real).astype(jnp.bfloat16)
        corr[pl.ds(size + at, height), :] = (factor * far_imag).astype(jnp.bfloat16)
        return carry

    lax.fori_loop(0, modules, correct, 0, unroll=8)

    @pl.when(slot == 0)
    def _():
        for move in table_copies(tables, left, right, table_sems):
            move.wait()

    for block in range(size // BLOCK):
        to = slice(block * BLOCK, (block + 1) * BLOCK)
        also = slice(size + block * BLOCK, size + (block + 1) * BLOCK)
        product = jnp.dot(right[...], corr[:, to], preferred_element_type=jnp.float32)
        back[:, to] = product[:size].astype(jnp.bfloat16)
        back[:, also] = product[size:].astype(jnp.bfloat16)
    for plane in range(2):
        for block in range(size // BLOCK):
            to = slice(block * BLOCK, (block + 1) * BLOCK)
            of = slice(plane * size + block * BLOCK, plane * size + (block + 1) * BLOCK)
            change[plane, :, to] = jnp.dot(
                back[...], left[:, of], preferred_element_type=jnp.float32
            )

    lane = lax.broadcasted_iota(jnp.int32, (CHUNK, LANES), 1)

    def spread(step, carry):
        at = pl.multiple_of(step * CHUNK, CHUNK)
        rows = pl.ds(at, CHUNK)
        last = [jnp.zeros((CHUNK, LANES), jnp.float32)] * 2
        for block in range(blocks + 1):
            if block < blocks:
                to = slice(block * LANES, (block + 1) * LANES)
                chg_real = change[0, rows, to]
                chg_imag = change[1, rows, to]
                spec_real = patch[0, 0, rows, to]
                spec_imag = patch[0, 1, rows, to]
                ill_real = ill[0, rows, to]
                ill_imag = ill[1, rows, to]
                places = pl.ds(step * (CHUNK // PIECE), CHUNK // PIECE)
                pieces = (CHUNK // PIECE, PIECE, LANES)
                sums[block, places, :PIECE] += (spec_real * chg_real + spec_imag * chg_imag).reshape(
                    pieces
                )
                sums[block, places, PIECE : 2 * PIECE] += (spec_real * chg_imag - spec_imag * chg_real).reshape(
                    pieces
                )
                sums[block, places, 2 * PIECE : 3 * PIECE] += (spec_real * spec_real + spec_imag * spec_imag).reshape(
                    pieces
                )
                grads = (
                    ill_real * chg_real + ill_imag * chg_imag,
                    ill_real * chg_imag - ill_imag * chg_real,
                )
                now = [pltpu.roll(grad, lane_shift, axis=1) for grad in grads]
            else:
                now = [jnp.zeros((CHUNK, LANES), jnp.float32)] * 2
            for plane in range(2):
                placed = jnp.where(lane < lane_shift, last[plane], now[plane])
                accum[plane, slot + block, pl.ds(row + at, CHUNK), :] += placed
            last = now
        return carry

    lax.fori_loop(0, size // CHUNK, spread, 0, unroll=8)


def whole(shape):
    return pl.BlockSpec(shape, lambda slot, *refs: (0,) * len(shape))


def once(shape):
    return pl.BlockSpec(
        shape, lambda slot, *refs: (0,) * len(shape), pipeline_mode=pl.Buffered(1)
    )


def one_slot(shape):
    return pl.BlockSpec((1,) + shape, lambda slot, *refs: (slot,) + (0,) * len(shape))


def run_forward(offs, pieces, tables, ill):
    slots = offs.shape[0]
    size = ill.shape[-1]
    rows, cols, edge = pieces[0].shape[1], pieces[0].shape[2], pieces[1].shape[2]
    planes = jax.ShapeDtypeStruct((slots, 2, size, size), jnp.float32)
    return pl.pallas_call(
        forward_kernel,
        grid_spec=pltpu.PrefetchScalarGridSpec(
            num_scalar_prefetch=1,
            grid=(slots,),
            in_specs=[pl.BlockSpec(memory_space=pltpu.HBM)] * (len(pieces) + len(tables))
            + [once(ill.shape)],
            out_specs=[
                one_slot((2, size, size)),
                one_slot((2, size, size)),
                whole((2, SUBLANES, LANES)),
            ],
            scratch_shapes=[
                pltpu.VMEM((2, (cols + 2 * edge) // LANES, 3 * rows, LANES), jnp.float32),
                pltpu.VMEM((2 * size, 2 * size), jnp.bfloat16),
                pltpu.VMEM((2 * size, 2 * size), jnp.bfloat16),
                pltpu.VMEM((2 * size, size), jnp.bfloat16),
                pltpu.VMEM((size, 2 * size), jnp.bfloat16),
                pltpu.SemaphoreType.DMA((40,)),
                pltpu.SemaphoreType.DMA((8,)),
            ],
        ),
        out_shape=[planes, planes, jax.ShapeDtypeStruct((2, SUBLANES, LANES), jnp.float32)],
        cost_estimate=pl.CostEstimate(
            flops=slots * 16 * size**3, bytes_accessed=30_000_000, transcendentals=0
        ),
        compiler_params=pltpu.CompilerParams(vmem_limit_bytes=67_000_000),
        name="forward",
    )(offs, *pieces, *tables, ill)


def run_backward(offs, order, powers, far, patch, amp, ill, tables, region_shape):
    slots = offs.shape[0]
    size = ill.shape[-1]
    senders, _, per, height, _ = amp.shape
    sums_shape = (size // LANES, size // PIECE, 3 * PIECE + SUBLANES, LANES)
    return pl.pallas_call(
        backward_kernel,
        grid_spec=pltpu.PrefetchScalarGridSpec(
            num_scalar_prefetch=3,
            grid=(slots,),
            in_specs=[
                one_slot((2, size, size)),
                one_slot((2, size, size)),
                pl.BlockSpec(
                    (senders, 1, per, height, size), lambda slot, *refs: (0, slot, 0, 0, 0)
                ),
                once(ill.shape),
            ]
            + [pl.BlockSpec(memory_space=pltpu.HBM)] * len(tables),
            out_specs=[whole(region_shape), whole(sums_shape)],
            scratch_shapes=[
                pltpu.VMEM((2 * size, size), jnp.bfloat16),
                pltpu.VMEM((size, 2 * size), jnp.bfloat16),
                pltpu.VMEM((2, size, size), jnp.float32),
                pltpu.VMEM((2 * size, 2 * size), jnp.bfloat16),
                pltpu.VMEM((2 * size, 2 * size), jnp.bfloat16),
                pltpu.SMEM((senders * per,), jnp.int32),
                pltpu.SemaphoreType.DMA((8,)),
            ],
        ),
        out_shape=[
            jax.ShapeDtypeStruct(region_shape, jnp.float32),
            jax.ShapeDtypeStruct(sums_shape, jnp.float32),
        ],
        cost_estimate=pl.CostEstimate(
            flops=slots * 16 * size**3, bytes_accessed=30_000_000, transcendentals=0
        ),
        compiler_params=pltpu.CompilerParams(vmem_limit_bytes=67_000_000),
        name="backward",
    )(offs, order, powers, far, patch, amp, ill, *tables)


def unpack_kernel(packed, out):
    size = out.shape[1]
    per = size // PIECE
    for column in range(size // LANES):
        for plane in range(2):
            part = packed[column * per : (column + 1) * per, plane * PIECE : (plane + 1) * PIECE]
            out[plane, :, column * LANES : (column + 1) * LANES] = part.reshape(size, LANES)


def unpacked(packed, size):
    return pl.pallas_call(
        unpack_kernel,
        in_specs=[pl.BlockSpec(memory_space=pltpu.VMEM)],
        out_specs=pl.BlockSpec(memory_space=pltpu.VMEM),
        out_shape=jax.ShapeDtypeStruct((2, size, size), jnp.float32),
        compiler_params=pltpu.CompilerParams(vmem_limit_bytes=16 * 1024 * 1024),
        name="unpack",
    )(packed)


def spread_out(value):
    return lax.all_to_all(value, ("row", "col"), split_axis=0, concat_axis=0, tiled=True)


def shards(measured, module_row, scan_offsets, specimen, illumination):
    slots = scan_offsets.shape[2]
    size = illumination.shape[-1]
    tile_rows = specimen.shape[1]
    tile_cols = specimen.shape[2]
    senders = lax.axis_size("row")
    devices = senders * lax.axis_size("col")
    per, height = measured.shape[1], measured.shape[2]
    late = slots // 2
    edge = tile_cols // 2
    grouped = measured.reshape(senders, slots, per, height, size)
    uppers, lowers = [], []
    for plane in range(2):
        uppers.append(passed_along(specimen[plane : plane + 1], "row", 1))
        lowers.append(passed_along(specimen[plane : plane + 1], "row", -1))
    early_offs = passed_along(scan_offsets[0, 0, :late], "row", 1)
    late_offs = passed_both(scan_offsets[0, 0, late:], 1, 1)
    offs = jnp.concatenate([late_offs, early_offs], axis=0)
    moved = passed_along(grouped[:, late:], "col", 1)
    west = passed_along(specimen[:, :, edge:], "col", 1)
    east = passed_along(specimen[:, :, :edge], "col", -1)
    levels = jnp.concatenate([moved, grouped[:, :late]], axis=1)
    tables = dft_tables(size)
    outers = []
    for plane in range(2):
        upper, lower = uppers[plane], lowers[plane]
        west_edges = jnp.concatenate([upper[:, :, edge:], lower[:, :, edge:]], axis=1)
        east_edges = jnp.concatenate([upper[:, :, :edge], lower[:, :, :edge]], axis=1)
        if plane == 0:
            uppers[1], lowers[1], _, _ = lax.optimization_barrier(
                (uppers[1], lowers[1], west_edges, east_edges)
            )
        outer_west = passed_along(west_edges, "col", 1)
        outer_east = passed_along(east_edges, "col", -1)
        outers.append((upper, lower, outer_west, outer_east))
    levels, probe, _ = lax.optimization_barrier((levels, illumination, uppers[0]))
    ill_power = exponent(2.0 * jnp.max(jnp.abs(probe)))
    levels, ill_power = lax.optimization_barrier((levels, ill_power))
    arrived = lax.all_to_all(
        levels,
        "row",
        split_axis=0,
        concat_axis=0,
        tiled=True,
        axis_index_groups=[[(sender + 1) % senders for sender in range(senders)]],
    )
    pieces = (specimen, west, east) + outers[0] + outers[1]
    far, patch, stats = run_forward(offs, pieces, tables, illumination)
    patch_power = exponent(1.5 * jnp.max(stats[0]))
    change_power = exponent(12.0 * jnp.sqrt(jnp.sum(stats[1])))
    home_power = ill_power + change_power + 1.0
    region_shape = (2, (tile_cols + 2 * edge) // LANES, 3 * tile_rows + SUBLANES, LANES)
    powers = jnp.stack([patch_power, change_power, home_power])
    accum, sums = run_backward(
        offs, module_row, powers, far, patch, arrived, illumination, tables, region_shape
    )
    side = edge // LANES
    to_west = relabelled(accum[:, :side], home_power)
    to_east = relabelled(accum[:, -side:], home_power)
    from_east = passed_along(to_west, "col", -1)
    from_west = passed_along(to_east, "col", 1)
    sums = sums.reshape(devices, 3 * PIECE + SUBLANES, LANES)
    line = lax.broadcasted_iota(jnp.int32, (1, 3 * PIECE + SUBLANES, 1), 1)
    scales = jnp.where(
        line < 2 * PIECE,
        jnp.exp2(14.0 - patch_power - change_power),
        jnp.where(line < 3 * PIECE, jnp.exp2(13.0 - 2.0 * patch_power), 1.0),
    )
    packed = (sums * scales).astype(jnp.float16)
    parts = spread_out(packed)
    body = 3 * tile_rows
    from_west, west_power = opened(from_west)
    from_east, east_power = opened(from_east)
    column = accum[:, side:-side, :body] + jnp.concatenate([from_west, from_east], axis=1)
    column_power = jnp.maximum(jnp.maximum(west_power, east_power), home_power) + 2.0
    to_upper = labelled(column[:, :, :tile_rows], column_power)
    to_lower = labelled(column[:, :, 2 * tile_rows : body], column_power)
    from_lower = passed_along(to_upper, "row", -1)
    from_upper = passed_along(to_lower, "row", 1)
    labels = parts[:, 3 * PIECE :].astype(jnp.float32)
    patch_powers, change_powers = labels[:, :1, :1], labels[:, 1:2, :1]
    line = line[:, : 3 * PIECE]
    powers = jnp.where(
        line < 2 * PIECE, patch_powers + change_powers + 1.0, 2.0 * patch_powers + 2.0
    )
    total = jnp.sum(widened(parts[:, : 3 * PIECE], powers), axis=0)
    mine = total[: 2 * PIECE].reshape(2, PIECE, LANES) / jnp.sqrt(total[2 * PIECE :] + 1e-06)
    step_power = jnp.max(change_powers) + math.ceil(0.5 * math.log2(slots * devices))
    mine = narrowed(mine, step_power).reshape(1, 2 * PIECE, LANES)
    copies = jnp.broadcast_to(mine, (devices, 2 * PIECE, LANES))
    result = spread_out(copies)
    illumination_step = unpacked(widened(result, step_power), size)
    middle = (
        column[:, :, tile_rows : 2 * tile_rows]
        + opened(from_lower)[0]
        + opened(from_upper)[0]
    )
    specimen_step = middle.swapaxes(1, 2).reshape(2, tile_rows, tile_cols)
    return (specimen_step, illumination_step)


def solution(mesh):
    return jax.shard_map(
        shards,
        mesh=mesh,
        in_specs=(
            P("col", "row", None, None),
            P(),
            P("row", "col", None, None),
            P(None, "row", "col"),
            P(),
        ),
        out_specs=(P(None, "row", "col"), P()),
        check_vma=False,
    )
```

```python
import math

import jax
import jax.numpy as jnp
import numpy as np
from jax import lax
from jax.experimental import pallas as pl
from jax.experimental.pallas import tpu as pltpu
from jax.sharding import PartitionSpec as P


LANES = 128
CHUNK = 32
BLOCK = 256
PIECE = 16
HALF_TOP = 65504.0


def passed_along(value, axis, steps):
    count = lax.axis_size(axis)
    pairs = [(source, (source + steps) % count) for source in range(count)]
    return lax.ppermute(value, axis, pairs)


def passed_both(value, row_steps, col_steps):
    rows, cols = lax.axis_size("row"), lax.axis_size("col")
    pairs = [
        (row * cols + col, (row + row_steps) % rows * cols + (col + col_steps) % cols)
        for row in range(rows)
        for col in range(cols)
    ]
    return lax.ppermute(value, ("row", "col"), pairs)


def dft_tables(size):
    index = np.arange(size, dtype=np.int64)
    wrapped = index[:, None] * index[None, :] % size
    angle = wrapped.astype(np.float32) * np.float32(2.0 * math.pi / size)
    norm = np.float32(1.0 / math.sqrt(size))
    cos_table = np.cos(angle.astype(np.float64)).astype(np.float32) * norm
    sin_table = -np.sin(angle.astype(np.float64)).astype(np.float32) * norm
    tables = (cos_table, sin_table, -sin_table)
    return tuple(jnp.asarray(table, jnp.bfloat16) for table in tables)


def narrowed(value, bound):
    return (value * (HALF_TOP / bound)).astype(jnp.float16)


def widened(value, bound):
    return value.astype(jnp.float32) * (bound / HALF_TOP)


def table_copies(tables, left, right, sems):
    cos_table, sin_table, negative = tables
    size = cos_table.shape[-1]
    low, high = pl.ds(0, size), pl.ds(size, size)
    moves = [
        (cos_table, left, low, low),
        (cos_table, left, high, high),
        (negative, left, low, high),
        (sin_table, left, high, low),
        (cos_table, right, low, low),
        (cos_table, right, high, high),
        (sin_table, right, low, high),
        (negative, right, high, low),
    ]
    return [
        pltpu.make_async_copy(source, table.at[rows, columns], sems.at[index])
        for index, (source, table, rows, columns) in enumerate(moves)
    ]


def region_copies(pieces, region, sems):
    middle, west, east = pieces[:3]
    rows, cols, edge = middle.shape[1], middle.shape[2], west.shape[2]
    center, right = edge // LANES, (edge + cols) // LANES
    both = pl.ds(0, 2)
    moves = [(middle, both, 0, 1, center), (west, both, 0, 1, 0), (east, both, 0, 1, right)]
    for plane in range(2):
        upper, lower, outer_west, outer_east = pieces[3 + 4 * plane : 7 + 4 * plane]
        one = pl.ds(plane, 1)
        moves += [
            (upper, one, 0, 0, center),
            (lower, one, 0, 2, center),
            (outer_west, one, 0, 0, 0),
            (outer_west, one, 1, 2, 0),
            (outer_east, one, 0, 0, right),
            (outer_east, one, 1, 2, right),
        ]
    copies = []
    for piece, planes, source, target, first in moves:
        for block in range(piece.shape[2] // LANES):
            copies.append(
                pltpu.make_async_copy(
                    piece.at[:, pl.ds(source * rows, rows), pl.ds(block * LANES, LANES)],
                    region.at[planes, first + block, pl.ds(target * rows, rows)],
                    sems.at[len(copies)],
                )
            )
    return copies


def forward_kernel(offs, *refs):
    pieces, tables, refs = refs[:11], refs[11:14], refs[14:]
    ill, far, patch, region, left, right, wave, half, region_sems, table_sems = refs
    slot = pl.program_id(0)
    size = ill.shape[-1]
    row = offs[slot, 0]
    lane_shift = offs[slot, 1] % LANES
    lane = lax.broadcasted_iota(jnp.int32, (CHUNK, LANES), 1)
    blocks = size // LANES

    @pl.when(slot == 0)
    def _():
        region_moves = region_copies(pieces, region, region_sems)
        table_moves = table_copies(tables, left, right, table_sems)
        for move in region_moves:
            move.start()
        for move in region_moves:
            move.wait()
        for move in table_moves:
            move.start()

    def extract(step, carry):
        at = pl.multiple_of(step * CHUNK, CHUNK)
        last = [None, None]
        for block in range(blocks + 1):
            now = [
                pltpu.roll(
                    region[plane, slot + block, pl.ds(row + at, CHUNK), :],
                    (LANES - lane_shift) % LANES,
                    axis=1,
                )
                for plane in range(2)
            ]
            if block > 0:
                to = slice((block - 1) * LANES, block * LANES)
                spec_real, spec_imag = (
                    jnp.where(lane < LANES - lane_shift, last[plane], now[plane])
                    for plane in range(2)
                )
                patch[0, 0, pl.ds(at, CHUNK), to] = spec_real
                patch[0, 1, pl.ds(at, CHUNK), to] = spec_imag
                ill_real = ill[0, pl.ds(at, CHUNK), to]
                ill_imag = ill[1, pl.ds(at, CHUNK), to]
                wave[pl.ds(at, CHUNK), to] = (
                    ill_real * spec_real - ill_imag * spec_imag
                ).astype(jnp.bfloat16)
                wave[pl.ds(size + at, CHUNK), to] = (
                    ill_real * spec_imag + ill_imag * spec_real
                ).astype(jnp.bfloat16)
            last = now
        return carry

    lax.fori_loop(0, size // CHUNK, extract, 0, unroll=8)

    @pl.when(slot == 0)
    def _():
        for move in table_copies(tables, left, right, table_sems):
            move.wait()

    for block in range(size // BLOCK):
        to = slice(block * BLOCK, (block + 1) * BLOCK)
        also = slice(size + block * BLOCK, size + (block + 1) * BLOCK)
        product = jnp.dot(left[...], wave[:, to], preferred_element_type=jnp.float32)
        half[:, to] = product[:size].astype(jnp.bfloat16)
        half[:, also] = product[size:].astype(jnp.bfloat16)
    for plane in range(2):
        for block in range(size // BLOCK):
            to = slice(block * BLOCK, (block + 1) * BLOCK)
            of = slice(plane * size + block * BLOCK, plane * size + (block + 1) * BLOCK)
            far[0, plane, :, to] = jnp.dot(
                half[...], right[:, of], preferred_element_type=jnp.float32
            )


def backward_kernel(
    offs,
    order,
    far,
    patch,
    amp,
    ill,
    cos_table,
    sin_table,
    negative,
    accum,
    sums,
    corr,
    back,
    change,
    left,
    right,
    inverse,
    table_sems,
):
    slot = pl.program_id(0)
    size = ill.shape[-1]
    modules = size // amp.shape[3]
    senders = amp.shape[0]
    row = offs[slot, 0]
    lane_shift = offs[slot, 1] % LANES
    tables = (cos_table, sin_table, negative)
    blocks = size // LANES
    height = amp.shape[3]
    per = amp.shape[2]

    @pl.when(slot == 0)
    def _():
        for move in table_copies(tables, left, right, table_sems):
            move.start()
        sums[...] = jnp.zeros_like(sums)

        def clear(step, carry):
            at = pl.multiple_of(step * CHUNK, CHUNK)
            accum[:, :, pl.ds(at, CHUNK), :] = jnp.zeros(
                (2, accum.shape[1], CHUNK, LANES), jnp.float32
            )
            return carry

        lax.fori_loop(0, accum.shape[2] // CHUNK, clear, 0)

        def invert(module, carry):
            inverse[order[module]] = module
            return carry

        lax.fori_loop(0, modules, invert, 0)

    def correct(band, carry):
        at = pl.multiple_of(band * height, height)
        module = inverse[band]
        rows = pl.ds(at, height)
        far_real = far[0, 0, rows, :]
        far_imag = far[0, 1, rows, :]
        sender = (module // per + senders - 1) % senders
        level = amp[sender, 0, module % per].astype(jnp.float32)
        inverse_size = lax.rsqrt(far_real * far_real + far_imag * far_imag)
        factor = level * jnp.minimum(inverse_size, 4.0) - 1.0
        corr[rows, :] = (factor * far_real).astype(jnp.bfloat16)
        corr[pl.ds(size + at, height), :] = (factor * far_imag).astype(jnp.bfloat16)
        return carry

    lax.fori_loop(0, modules, correct, 0, unroll=8)

    @pl.when(slot == 0)
    def _():
        for move in table_copies(tables, left, right, table_sems):
            move.wait()

    for block in range(size // BLOCK):
        to = slice(block * BLOCK, (block + 1) * BLOCK)
        also = slice(size + block * BLOCK, size + (block + 1) * BLOCK)
        product = jnp.dot(right[...], corr[:, to], preferred_element_type=jnp.float32)
        back[:, to] = product[:size].astype(jnp.bfloat16)
        back[:, also] = product[size:].astype(jnp.bfloat16)
    for plane in range(2):
        for block in range(size // BLOCK):
            to = slice(block * BLOCK, (block + 1) * BLOCK)
            of = slice(plane * size + block * BLOCK, plane * size + (block + 1) * BLOCK)
            change[plane, :, to] = jnp.dot(
                back[...], left[:, of], preferred_element_type=jnp.float32
            )

    lane = lax.broadcasted_iota(jnp.int32, (CHUNK, LANES), 1)

    def spread(step, carry):
        at = pl.multiple_of(step * CHUNK, CHUNK)
        rows = pl.ds(at, CHUNK)
        last = [jnp.zeros((CHUNK, LANES), jnp.float32)] * 2
        for block in range(blocks + 1):
            if block < blocks:
                to = slice(block * LANES, (block + 1) * LANES)
                chg_real = change[0, rows, to]
                chg_imag = change[1, rows, to]
                spec_real = patch[0, 0, rows, to]
                spec_imag = patch[0, 1, rows, to]
                ill_real = ill[0, rows, to]
                ill_imag = ill[1, rows, to]
                places = pl.ds(step * (CHUNK // PIECE), CHUNK // PIECE)
                pieces = (CHUNK // PIECE, PIECE, LANES)
                sums[block, places, 0] += (spec_real * chg_real + spec_imag * chg_imag).reshape(
                    pieces
                )
                sums[block, places, 1] += (spec_real * chg_imag - spec_imag * chg_real).reshape(
                    pieces
                )
                sums[block, places, 2] += (spec_real * spec_real + spec_imag * spec_imag).reshape(
                    pieces
                )
                grads = (
                    ill_real * chg_real + ill_imag * chg_imag,
                    ill_real * chg_imag - ill_imag * chg_real,
                )
                now = [pltpu.roll(grad, lane_shift, axis=1) for grad in grads]
            else:
                now = [jnp.zeros((CHUNK, LANES), jnp.float32)] * 2
            for plane in range(2):
                placed = jnp.where(lane < lane_shift, last[plane], now[plane])
                accum[plane, slot + block, pl.ds(row + at, CHUNK), :] += placed
            last = now
        return carry

    lax.fori_loop(0, size // CHUNK, spread, 0, unroll=8)


def whole(shape):
    return pl.BlockSpec(shape, lambda slot, *refs: (0,) * len(shape))


def once(shape):
    return pl.BlockSpec(
        shape, lambda slot, *refs: (0,) * len(shape), pipeline_mode=pl.Buffered(1)
    )


def one_slot(shape):
    return pl.BlockSpec((1,) + shape, lambda slot, *refs: (slot,) + (0,) * len(shape))


def run_forward(offs, pieces, tables, ill):
    slots = offs.shape[0]
    size = ill.shape[-1]
    rows, cols, edge = pieces[0].shape[1], pieces[0].shape[2], pieces[1].shape[2]
    planes = jax.ShapeDtypeStruct((slots, 2, size, size), jnp.float32)
    return pl.pallas_call(
        forward_kernel,
        grid_spec=pltpu.PrefetchScalarGridSpec(
            num_scalar_prefetch=1,
            grid=(slots,),
            in_specs=[pl.BlockSpec(memory_space=pltpu.HBM)] * (len(pieces) + len(tables))
            + [once(ill.shape)],
            out_specs=[
                one_slot((2, size, size)),
                one_slot((2, size, size)),
            ],
            scratch_shapes=[
                pltpu.VMEM((2, (cols + 2 * edge) // LANES, 3 * rows, LANES), jnp.float32),
                pltpu.VMEM((2 * size, 2 * size), jnp.bfloat16),
                pltpu.VMEM((2 * size, 2 * size), jnp.bfloat16),
                pltpu.VMEM((2 * size, size), jnp.bfloat16),
                pltpu.VMEM((size, 2 * size), jnp.bfloat16),
                pltpu.SemaphoreType.DMA((40,)),
                pltpu.SemaphoreType.DMA((8,)),
            ],
        ),
        out_shape=[planes, planes],
        cost_estimate=pl.CostEstimate(
            flops=slots * 16 * size**3, bytes_accessed=30_000_000, transcendentals=0
        ),
        compiler_params=pltpu.CompilerParams(vmem_limit_bytes=67_000_000),
        name="forward",
    )(offs, *pieces, *tables, ill)


def run_backward(offs, order, far, patch, amp, ill, tables, region_shape):
    slots = offs.shape[0]
    size = ill.shape[-1]
    senders, _, per, height, _ = amp.shape
    sums_shape = (size // LANES, size // PIECE, 3, PIECE, LANES)
    return pl.pallas_call(
        backward_kernel,
        grid_spec=pltpu.PrefetchScalarGridSpec(
            num_scalar_prefetch=2,
            grid=(slots,),
            in_specs=[
                one_slot((2, size, size)),
                one_slot((2, size, size)),
                pl.BlockSpec(
                    (senders, 1, per, height, size), lambda slot, *refs: (0, slot, 0, 0, 0)
                ),
                once(ill.shape),
            ]
            + [pl.BlockSpec(memory_space=pltpu.HBM)] * len(tables),
            out_specs=[whole(region_shape), whole(sums_shape)],
            scratch_shapes=[
                pltpu.VMEM((2 * size, size), jnp.bfloat16),
                pltpu.VMEM((size, 2 * size), jnp.bfloat16),
                pltpu.VMEM((2, size, size), jnp.float32),
                pltpu.VMEM((2 * size, 2 * size), jnp.bfloat16),
                pltpu.VMEM((2 * size, 2 * size), jnp.bfloat16),
                pltpu.SMEM((senders * per,), jnp.int32),
                pltpu.SemaphoreType.DMA((8,)),
            ],
        ),
        out_shape=[
            jax.ShapeDtypeStruct(region_shape, jnp.float32),
            jax.ShapeDtypeStruct(sums_shape, jnp.float32),
        ],
        cost_estimate=pl.CostEstimate(
            flops=slots * 16 * size**3, bytes_accessed=30_000_000, transcendentals=0
        ),
        compiler_params=pltpu.CompilerParams(vmem_limit_bytes=67_000_000),
        name="backward",
    )(offs, order, far, patch, amp, ill, *tables)


def unpack_kernel(packed, out):
    size = out.shape[1]
    per = size // PIECE
    for column in range(size // LANES):
        for plane in range(2):
            part = packed[column * per : (column + 1) * per, plane * PIECE : (plane + 1) * PIECE]
            out[plane, :, column * LANES : (column + 1) * LANES] = part.reshape(size, LANES)


def unpacked(packed, size):
    return pl.pallas_call(
        unpack_kernel,
        in_specs=[pl.BlockSpec(memory_space=pltpu.VMEM)],
        out_specs=pl.BlockSpec(memory_space=pltpu.VMEM),
        out_shape=jax.ShapeDtypeStruct((2, size, size), jnp.float32),
        compiler_params=pltpu.CompilerParams(vmem_limit_bytes=16 * 1024 * 1024),
        name="unpack",
    )(packed)


def spread_out(value):
    return lax.all_to_all(value, ("row", "col"), split_axis=0, concat_axis=0, tiled=True)


def shards(measured, module_row, scan_offsets, specimen, illumination):
    slots = scan_offsets.shape[2]
    size = illumination.shape[-1]
    tile_rows = specimen.shape[1]
    tile_cols = specimen.shape[2]
    senders = lax.axis_size("row")
    devices = senders * lax.axis_size("col")
    per, height = measured.shape[1], measured.shape[2]
    late = slots // 2
    edge = tile_cols // 2
    grouped = measured.reshape(senders, slots, per, height, size)
    uppers, lowers = [], []
    for plane in range(2):
        uppers.append(passed_along(specimen[plane : plane + 1], "row", 1))
        lowers.append(passed_along(specimen[plane : plane + 1], "row", -1))
    early_offs = passed_along(scan_offsets[0, 0, :late], "row", 1)
    late_offs = passed_both(scan_offsets[0, 0, late:], 1, 1)
    offs = jnp.concatenate([late_offs, early_offs], axis=0)
    moved = passed_along(grouped[:, late:], "col", 1)
    west = passed_along(specimen[:, :, edge:], "col", 1)
    east = passed_along(specimen[:, :, :edge], "col", -1)
    levels = jnp.concatenate([moved, grouped[:, :late]], axis=1)
    tables = dft_tables(size)
    lane = lax.broadcasted_iota(jnp.int32, (devices, 1, LANES), 2)
    stats = jnp.where(
        lane < LANES // 2, jnp.max(jnp.abs(specimen)), jnp.sum(specimen * specimen)
    )
    peaks = spread_out(stats)
    peak = jnp.maximum(jnp.max(peaks[:, :, : LANES // 2]), 1e-12)
    power = jnp.max(peaks[:, :, LANES // 2 :])
    outers = []
    for plane in range(2):
        upper, lower = uppers[plane], lowers[plane]
        west_edges = jnp.concatenate([upper[:, :, edge:], lower[:, :, edge:]], axis=1)
        east_edges = jnp.concatenate([upper[:, :, :edge], lower[:, :, :edge]], axis=1)
        if plane == 0:
            uppers[1], lowers[1], _, _ = lax.optimization_barrier(
                (uppers[1], lowers[1], west_edges, east_edges)
            )
        outer_west = passed_along(west_edges, "col", 1)
        outer_east = passed_along(east_edges, "col", -1)
        outers.append((upper, lower, outer_west, outer_east))
    levels, probe, _ = lax.optimization_barrier((levels, illumination, uppers[0]))
    ill_power = jnp.sum(probe * probe)
    ill_peak = jnp.maximum(jnp.max(jnp.abs(probe)), 1e-8)
    levels, ill_power, ill_peak = lax.optimization_barrier((levels, ill_power, ill_peak))
    modulus = 1.5 * peak
    energy = jnp.minimum(
        modulus * jnp.sqrt(ill_power), 1.5 * ill_peak * jnp.sqrt(6.0 * power)
    )
    change_bound = 9.0 * jnp.maximum(energy, 1e-20)
    grad_bound = 24.0 * ill_peak * change_bound
    sum_bound = slots * modulus * change_bound
    density_bound = slots * modulus * modulus
    step_bound = math.sqrt(slots * devices) * change_bound
    arrived = lax.all_to_all(
        levels,
        "row",
        split_axis=0,
        concat_axis=0,
        tiled=True,
        axis_index_groups=[[(sender + 1) % senders for sender in range(senders)]],
    )
    pieces = (specimen, west, east) + outers[0] + outers[1]
    far, patch = run_forward(offs, pieces, tables, illumination)
    region_shape = (2, (tile_cols + 2 * edge) // LANES, 3 * tile_rows, LANES)
    accum, sums = run_backward(
        offs, module_row, far, patch, arrived, illumination, tables, region_shape
    )
    side = edge // LANES
    to_west = narrowed(accum[:, :side], grad_bound)
    to_east = narrowed(accum[:, -side:], grad_bound)
    from_east = passed_along(to_west, "col", -1)
    from_west = passed_along(to_east, "col", 1)
    sums = sums.reshape(devices, 3 * PIECE, LANES)
    line = lax.broadcasted_iota(jnp.int32, (1, 3 * PIECE, 1), 1)
    bounds = jnp.where(line < 2 * PIECE, sum_bound, density_bound)
    packed = narrowed(sums, bounds)
    parts = spread_out(packed)
    column = accum[:, side:-side] + jnp.concatenate(
        [widened(from_west, grad_bound), widened(from_east, grad_bound)], axis=1
    )
    to_upper = narrowed(column[:, :, :tile_rows], grad_bound)
    to_lower = narrowed(column[:, :, 2 * tile_rows :], grad_bound)
    from_lower = passed_along(to_upper, "row", -1)
    from_upper = passed_along(to_lower, "row", 1)
    total = jnp.sum(widened(parts, bounds), axis=0)
    mine = total[: 2 * PIECE].reshape(2, PIECE, LANES) / jnp.sqrt(total[2 * PIECE :] + 1e-06)
    mine = narrowed(mine, step_bound).reshape(1, 2 * PIECE, LANES)
    copies = jnp.broadcast_to(mine, (devices, 2 * PIECE, LANES))
    result = spread_out(copies)
    illumination_step = unpacked(widened(result, step_bound), size)
    middle = (
        column[:, :, tile_rows : 2 * tile_rows]
        + widened(from_lower, grad_bound)
        + widened(from_upper, grad_bound)
    )
    specimen_step = middle.swapaxes(1, 2).reshape(2, tile_rows, tile_cols)
    return (specimen_step, illumination_step)


def solution(mesh):
    return jax.shard_map(
        shards,
        mesh=mesh,
        in_specs=(
            P("col", "row", None, None),
            P(),
            P("row", "col", None, None),
            P(None, "row", "col"),
            P(),
        ),
        out_specs=(P(None, "row", "col"), P()),
        check_vma=False,
    )
```

```python
import math

import jax
import jax.numpy as jnp
import numpy as np
from jax import lax
from jax.experimental import pallas as pl
from jax.experimental.pallas import tpu as pltpu
from jax.sharding import PartitionSpec as P


LANES = 128
CHUNK = 32
BLOCK = 256
PIECE = 16
HALF_TOP = 65504.0


def passed_along(value, axis, steps):
    count = lax.axis_size(axis)
    pairs = [(source, (source + steps) % count) for source in range(count)]
    return lax.ppermute(value, axis, pairs)


def passed_both(value, row_steps, col_steps):
    rows, cols = lax.axis_size("row"), lax.axis_size("col")
    pairs = [
        (row * cols + col, (row + row_steps) % rows * cols + (col + col_steps) % cols)
        for row in range(rows)
        for col in range(cols)
    ]
    return lax.ppermute(value, ("row", "col"), pairs)


def dft_tables(size):
    index = np.arange(size, dtype=np.int64)
    wrapped = index[:, None] * index[None, :] % size
    angle = wrapped.astype(np.float32) * np.float32(2.0 * math.pi / size)
    norm = np.float32(1.0 / math.sqrt(size))
    cos_table = np.cos(angle.astype(np.float64)).astype(np.float32) * norm
    sin_table = -np.sin(angle.astype(np.float64)).astype(np.float32) * norm
    tables = (cos_table, sin_table, -sin_table)
    return tuple(jnp.asarray(table, jnp.bfloat16) for table in tables)


def narrowed(value, bound):
    return (value * (HALF_TOP / bound)).astype(jnp.float16)


def widened(value, bound):
    return value.astype(jnp.float32) * (bound / HALF_TOP)


def table_copies(tables, left, right, sems):
    cos_table, sin_table, negative = tables
    size = cos_table.shape[-1]
    low, high = pl.ds(0, size), pl.ds(size, size)
    moves = [
        (cos_table, left, low, low),
        (cos_table, left, high, high),
        (negative, left, low, high),
        (sin_table, left, high, low),
        (cos_table, right, low, low),
        (cos_table, right, high, high),
        (sin_table, right, low, high),
        (negative, right, high, low),
    ]
    return [
        pltpu.make_async_copy(source, table.at[rows, columns], sems.at[index])
        for index, (source, table, rows, columns) in enumerate(moves)
    ]


def region_copies(pieces, region, sems):
    middle, west, _ = pieces[:3]
    rows, cols, edge = middle.shape[1], middle.shape[2], west.shape[2]
    center, right = edge // LANES, (edge + cols) // LANES
    half = center + edge // LANES
    places = [(1, center), (1, 0), (1, right)]
    places += [(0, half), (2, half), (0, center), (2, center)]
    places += [(0, 0), (2, 0), (0, right), (2, right)]
    copies = []
    for piece, (target, first) in zip(pieces, places):
        for block in range(piece.shape[2] // LANES):
            copies.append(
                pltpu.make_async_copy(
                    piece.at[:, :, pl.ds(block * LANES, LANES)],
                    region.at[:, first + block, pl.ds(target * rows, rows)],
                    sems.at[len(copies)],
                )
            )
    return copies


def forward_kernel(offs, *refs):
    pieces, tables, refs = refs[:11], refs[11:14], refs[14:]
    ill, far, patch, region, left, right, wave, half, region_sems, table_sems = refs
    slot = pl.program_id(0)
    size = ill.shape[-1]
    row = offs[slot, 0]
    lane_shift = offs[slot, 1] % LANES
    lane = lax.broadcasted_iota(jnp.int32, (CHUNK, LANES), 1)
    blocks = size // LANES

    @pl.when(slot == 0)
    def _():
        region_moves = region_copies(pieces, region, region_sems)
        table_moves = table_copies(tables, left, right, table_sems)
        for move in region_moves:
            move.start()
        for move in region_moves:
            move.wait()
        for move in table_moves:
            move.start()

    def extract(step, carry):
        at = pl.multiple_of(step * CHUNK, CHUNK)
        last = [None, None]
        for block in range(blocks + 1):
            now = [
                pltpu.roll(
                    region[plane, slot + block, pl.ds(row + at, CHUNK), :],
                    (LANES - lane_shift) % LANES,
                    axis=1,
                )
                for plane in range(2)
            ]
            if block > 0:
                to = slice((block - 1) * LANES, block * LANES)
                spec_real, spec_imag = (
                    jnp.where(lane < LANES - lane_shift, last[plane], now[plane])
                    for plane in range(2)
                )
                patch[0, 0, pl.ds(at, CHUNK), to] = spec_real
                patch[0, 1, pl.ds(at, CHUNK), to] = spec_imag
                ill_real = ill[0, pl.ds(at, CHUNK), to]
                ill_imag = ill[1, pl.ds(at, CHUNK), to]
                wave[pl.ds(at, CHUNK), to] = (
                    ill_real * spec_real - ill_imag * spec_imag
                ).astype(jnp.bfloat16)
                wave[pl.ds(size + at, CHUNK), to] = (
                    ill_real * spec_imag + ill_imag * spec_real
                ).astype(jnp.bfloat16)
            last = now
        return carry

    lax.fori_loop(0, size // CHUNK, extract, 0, unroll=8)

    @pl.when(slot == 0)
    def _():
        for move in table_copies(tables, left, right, table_sems):
            move.wait()

    for block in range(size // BLOCK):
        to = slice(block * BLOCK, (block + 1) * BLOCK)
        also = slice(size + block * BLOCK, size + (block + 1) * BLOCK)
        product = jnp.dot(left[...], wave[:, to], preferred_element_type=jnp.float32)
        half[:, to] = product[:size].astype(jnp.bfloat16)
        half[:, also] = product[size:].astype(jnp.bfloat16)
    for plane in range(2):
        for block in range(size // BLOCK):
            to = slice(block * BLOCK, (block + 1) * BLOCK)
            of = slice(plane * size + block * BLOCK, plane * size + (block + 1) * BLOCK)
            far[0, plane, :, to] = jnp.dot(
                half[...], right[:, of], preferred_element_type=jnp.float32
            )


def backward_kernel(
    offs,
    order,
    far,
    patch,
    amp,
    ill,
    cos_table,
    sin_table,
    negative,
    accum,
    sums,
    corr,
    back,
    change,
    left,
    right,
    inverse,
    table_sems,
):
    slot = pl.program_id(0)
    size = ill.shape[-1]
    modules = size // amp.shape[3]
    senders = amp.shape[0]
    row = offs[slot, 0]
    lane_shift = offs[slot, 1] % LANES
    tables = (cos_table, sin_table, negative)
    blocks = size // LANES
    height = amp.shape[3]
    per = amp.shape[2]

    @pl.when(slot == 0)
    def _():
        for move in table_copies(tables, left, right, table_sems):
            move.start()
        sums[...] = jnp.zeros_like(sums)

        def clear(step, carry):
            at = pl.multiple_of(step * CHUNK, CHUNK)
            accum[:, :, pl.ds(at, CHUNK), :] = jnp.zeros(
                (2, accum.shape[1], CHUNK, LANES), jnp.float32
            )
            return carry

        lax.fori_loop(0, accum.shape[2] // CHUNK, clear, 0)

        def invert(module, carry):
            inverse[order[module]] = module
            return carry

        lax.fori_loop(0, modules, invert, 0)

    def correct(band, carry):
        at = pl.multiple_of(band * height, height)
        module = inverse[band]
        rows = pl.ds(at, height)
        far_real = far[0, 0, rows, :]
        far_imag = far[0, 1, rows, :]
        sender = (module // per + senders - 1) % senders
        level = amp[sender, 0, module % per].astype(jnp.float32)
        inverse_size = lax.rsqrt(far_real * far_real + far_imag * far_imag)
        factor = level * jnp.minimum(inverse_size, 4.0) - 1.0
        corr[rows, :] = (factor * far_real).astype(jnp.bfloat16)
        corr[pl.ds(size + at, height), :] = (factor * far_imag).astype(jnp.bfloat16)
        return carry

    lax.fori_loop(0, modules, correct, 0, unroll=8)

    @pl.when(slot == 0)
    def _():
        for move in table_copies(tables, left, right, table_sems):
            move.wait()

    for block in range(size // BLOCK):
        to = slice(block * BLOCK, (block + 1) * BLOCK)
        also = slice(size + block * BLOCK, size + (block + 1) * BLOCK)
        product = jnp.dot(right[...], corr[:, to], preferred_element_type=jnp.float32)
        back[:, to] = product[:size].astype(jnp.bfloat16)
        back[:, also] = product[size:].astype(jnp.bfloat16)
    for plane in range(2):
        for block in range(size // BLOCK):
            to = slice(block * BLOCK, (block + 1) * BLOCK)
            of = slice(plane * size + block * BLOCK, plane * size + (block + 1) * BLOCK)
            change[plane, :, to] = jnp.dot(
                back[...], left[:, of], preferred_element_type=jnp.float32
            )

    lane = lax.broadcasted_iota(jnp.int32, (CHUNK, LANES), 1)

    def spread(step, carry):
        at = pl.multiple_of(step * CHUNK, CHUNK)
        rows = pl.ds(at, CHUNK)
        last = [jnp.zeros((CHUNK, LANES), jnp.float32)] * 2
        for block in range(blocks + 1):
            if block < blocks:
                to = slice(block * LANES, (block + 1) * LANES)
                chg_real = change[0, rows, to]
                chg_imag = change[1, rows, to]
                spec_real = patch[0, 0, rows, to]
                spec_imag = patch[0, 1, rows, to]
                ill_real = ill[0, rows, to]
                ill_imag = ill[1, rows, to]
                places = pl.ds(step * (CHUNK // PIECE), CHUNK // PIECE)
                pieces = (CHUNK // PIECE, PIECE, LANES)
                sums[block, places, 0] += (spec_real * chg_real + spec_imag * chg_imag).reshape(
                    pieces
                )
                sums[block, places, 1] += (spec_real * chg_imag - spec_imag * chg_real).reshape(
                    pieces
                )
                sums[block, places, 2] += (spec_real * spec_real + spec_imag * spec_imag).reshape(
                    pieces
                )
                grads = (
                    ill_real * chg_real + ill_imag * chg_imag,
                    ill_real * chg_imag - ill_imag * chg_real,
                )
                now = [pltpu.roll(grad, lane_shift, axis=1) for grad in grads]
            else:
                now = [jnp.zeros((CHUNK, LANES), jnp.float32)] * 2
            for plane in range(2):
                placed = jnp.where(lane < lane_shift, last[plane], now[plane])
                accum[plane, slot + block, pl.ds(row + at, CHUNK), :] += placed
            last = now
        return carry

    lax.fori_loop(0, size // CHUNK, spread, 0, unroll=8)


def whole(shape):
    return pl.BlockSpec(shape, lambda slot, *refs: (0,) * len(shape))


def once(shape):
    return pl.BlockSpec(
        shape, lambda slot, *refs: (0,) * len(shape), pipeline_mode=pl.Buffered(1)
    )


def one_slot(shape):
    return pl.BlockSpec((1,) + shape, lambda slot, *refs: (slot,) + (0,) * len(shape))


def run_forward(offs, pieces, tables, ill):
    slots = offs.shape[0]
    size = ill.shape[-1]
    rows, cols, edge = pieces[0].shape[1], pieces[0].shape[2], pieces[1].shape[2]
    planes = jax.ShapeDtypeStruct((slots, 2, size, size), jnp.float32)
    return pl.pallas_call(
        forward_kernel,
        grid_spec=pltpu.PrefetchScalarGridSpec(
            num_scalar_prefetch=1,
            grid=(slots,),
            in_specs=[pl.BlockSpec(memory_space=pltpu.HBM)] * (len(pieces) + len(tables))
            + [once(ill.shape)],
            out_specs=[
                one_slot((2, size, size)),
                one_slot((2, size, size)),
            ],
            scratch_shapes=[
                pltpu.VMEM((2, (cols + 2 * edge) // LANES, 3 * rows, LANES), jnp.float32),
                pltpu.VMEM((2 * size, 2 * size), jnp.bfloat16),
                pltpu.VMEM((2 * size, 2 * size), jnp.bfloat16),
                pltpu.VMEM((2 * size, size), jnp.bfloat16),
                pltpu.VMEM((size, 2 * size), jnp.bfloat16),
                pltpu.SemaphoreType.DMA((24,)),
                pltpu.SemaphoreType.DMA((8,)),
            ],
        ),
        out_shape=[planes, planes],
        cost_estimate=pl.CostEstimate(
            flops=slots * 16 * size**3, bytes_accessed=30_000_000, transcendentals=0
        ),
        compiler_params=pltpu.CompilerParams(vmem_limit_bytes=67_000_000),
        name="forward",
    )(offs, *pieces, *tables, ill)


def run_backward(offs, order, far, patch, amp, ill, tables, region_shape):
    slots = offs.shape[0]
    size = ill.shape[-1]
    senders, _, per, height, _ = amp.shape
    sums_shape = (size // LANES, size // PIECE, 3, PIECE, LANES)
    return pl.pallas_call(
        backward_kernel,
        grid_spec=pltpu.PrefetchScalarGridSpec(
            num_scalar_prefetch=2,
            grid=(slots,),
            in_specs=[
                one_slot((2, size, size)),
                one_slot((2, size, size)),
                pl.BlockSpec(
                    (senders, 1, per, height, size), lambda slot, *refs: (0, slot, 0, 0, 0)
                ),
                once(ill.shape),
            ]
            + [pl.BlockSpec(memory_space=pltpu.HBM)] * len(tables),
            out_specs=[whole(region_shape), whole(sums_shape)],
            scratch_shapes=[
                pltpu.VMEM((2 * size, size), jnp.bfloat16),
                pltpu.VMEM((size, 2 * size), jnp.bfloat16),
                pltpu.VMEM((2, size, size), jnp.float32),
                pltpu.VMEM((2 * size, 2 * size), jnp.bfloat16),
                pltpu.VMEM((2 * size, 2 * size), jnp.bfloat16),
                pltpu.SMEM((senders * per,), jnp.int32),
                pltpu.SemaphoreType.DMA((8,)),
            ],
        ),
        out_shape=[
            jax.ShapeDtypeStruct(region_shape, jnp.float32),
            jax.ShapeDtypeStruct(sums_shape, jnp.float32),
        ],
        cost_estimate=pl.CostEstimate(
            flops=slots * 16 * size**3, bytes_accessed=30_000_000, transcendentals=0
        ),
        compiler_params=pltpu.CompilerParams(vmem_limit_bytes=67_000_000),
        name="backward",
    )(offs, order, far, patch, amp, ill, *tables)


def unpack_kernel(packed, out):
    size = out.shape[1]
    per = size // PIECE
    for column in range(size // LANES):
        for plane in range(2):
            part = packed[column * per : (column + 1) * per, plane * PIECE : (plane + 1) * PIECE]
            out[plane, :, column * LANES : (column + 1) * LANES] = part.reshape(size, LANES)


def unpacked(packed, size):
    return pl.pallas_call(
        unpack_kernel,
        in_specs=[pl.BlockSpec(memory_space=pltpu.VMEM)],
        out_specs=pl.BlockSpec(memory_space=pltpu.VMEM),
        out_shape=jax.ShapeDtypeStruct((2, size, size), jnp.float32),
        compiler_params=pltpu.CompilerParams(vmem_limit_bytes=16 * 1024 * 1024),
        name="unpack",
    )(packed)


def spread_out(value):
    return lax.all_to_all(value, ("row", "col"), split_axis=0, concat_axis=0, tiled=True)


def shards(measured, module_row, scan_offsets, specimen, illumination):
    slots = scan_offsets.shape[2]
    size = illumination.shape[-1]
    tile_rows = specimen.shape[1]
    tile_cols = specimen.shape[2]
    senders = lax.axis_size("row")
    devices = senders * lax.axis_size("col")
    per, height = measured.shape[1], measured.shape[2]
    late = slots // 2
    edge = tile_cols // 2
    grouped = measured.reshape(senders, slots, per, height, size)
    halves = {"left": specimen[:, :, :edge], "right": specimen[:, :, edge:]}
    rows = []
    for name in ("right", "left"):
        rows.append(passed_along(halves[name], "row", 1))
        rows.append(passed_along(halves[name], "row", -1))
    early_offs = passed_along(scan_offsets[0, 0, :late], "row", 1)
    late_offs = passed_both(scan_offsets[0, 0, late:], 1, 1)
    offs = jnp.concatenate([late_offs, early_offs], axis=0)
    moved = passed_along(grouped[:, late:], "col", 1)
    west = passed_along(halves["right"], "col", 1)
    east = passed_along(halves["left"], "col", -1)
    levels = jnp.concatenate([moved, grouped[:, :late]], axis=1)
    tables = dft_tables(size)
    lane = lax.broadcasted_iota(jnp.int32, (devices, 1, LANES), 2)
    stats = jnp.where(
        lane < LANES // 2, jnp.max(jnp.abs(specimen)), jnp.sum(specimen * specimen)
    )
    peaks = spread_out(stats)
    outers = []
    for index, (steps, name) in enumerate(((1, "west"), (1, "west"), (-1, "east"), (-1, "east"))):
        outers.append(passed_along(rows[index], "col", steps))
    levels, _ = lax.optimization_barrier((levels, tuple(rows)))
    arrived = lax.all_to_all(
        levels,
        "row",
        split_axis=0,
        concat_axis=0,
        tiled=True,
        axis_index_groups=[[(sender + 1) % senders for sender in range(senders)]],
    )
    pieces = (specimen, west, east, *rows, *outers)
    far, patch = run_forward(offs, pieces, tables, illumination)
    far, probe, peaks = lax.optimization_barrier((far, illumination, peaks))
    peak = jnp.maximum(jnp.max(peaks[:, :, : LANES // 2]), 1e-12)
    power = jnp.max(peaks[:, :, LANES // 2 :])
    ill_power = jnp.sum(probe * probe)
    ill_peak = jnp.maximum(jnp.max(jnp.abs(probe)), 1e-8)
    modulus = 1.5 * peak
    energy = jnp.minimum(
        modulus * jnp.sqrt(ill_power), 1.5 * ill_peak * jnp.sqrt(6.0 * power)
    )
    change_bound = 9.0 * jnp.maximum(energy, 1e-20)
    grad_bound = 24.0 * ill_peak * change_bound
    sum_bound = slots * modulus * change_bound
    density_bound = slots * modulus * modulus
    step_bound = math.sqrt(slots * devices) * change_bound
    bounds = (grad_bound, sum_bound, density_bound, step_bound)
    far, bounds = lax.optimization_barrier((far, bounds))
    grad_bound, sum_bound, density_bound, step_bound = bounds
    region_shape = (2, (tile_cols + 2 * edge) // LANES, 3 * tile_rows, LANES)
    accum, sums = run_backward(
        offs, module_row, far, patch, arrived, illumination, tables, region_shape
    )
    side = edge // LANES
    to_west = narrowed(accum[:, :side], grad_bound)
    to_east = narrowed(accum[:, -side:], grad_bound)
    from_east = passed_along(to_west, "col", -1)
    from_west = passed_along(to_east, "col", 1)
    sums = sums.reshape(devices, 3 * PIECE, LANES)
    line = lax.broadcasted_iota(jnp.int32, (1, 3 * PIECE, 1), 1)
    bounds = jnp.where(line < 2 * PIECE, sum_bound, density_bound)
    packed = narrowed(sums, bounds)
    parts = spread_out(packed)
    column = accum[:, side:-side] + jnp.concatenate(
        [widened(from_west, grad_bound), widened(from_east, grad_bound)], axis=1
    )
    to_upper = narrowed(column[:, :, :tile_rows], grad_bound)
    to_lower = narrowed(column[:, :, 2 * tile_rows :], grad_bound)
    from_lower = passed_along(to_upper, "row", -1)
    from_upper = passed_along(to_lower, "row", 1)
    total = jnp.sum(widened(parts, bounds), axis=0)
    mine = total[: 2 * PIECE].reshape(2, PIECE, LANES) / jnp.sqrt(total[2 * PIECE :] + 1e-06)
    mine = narrowed(mine, step_bound).reshape(1, 2 * PIECE, LANES)
    copies = jnp.broadcast_to(mine, (devices, 2 * PIECE, LANES))
    result = spread_out(copies)
    illumination_step = unpacked(widened(result, step_bound), size)
    middle = (
        column[:, :, tile_rows : 2 * tile_rows]
        + widened(from_lower, grad_bound)
        + widened(from_upper, grad_bound)
    )
    specimen_step = middle.swapaxes(1, 2).reshape(2, tile_rows, tile_cols)
    return (specimen_step, illumination_step)


def solution(mesh):
    return jax.shard_map(
        shards,
        mesh=mesh,
        in_specs=(
            P("col", "row", None, None),
            P(),
            P("row", "col", None, None),
            P(None, "row", "col"),
            P(),
        ),
        out_specs=(P(None, "row", "col"), P()),
        check_vma=False,
    )
```

```python
import math

import jax
import jax.numpy as jnp
import numpy as np
from jax import lax
from jax.experimental import pallas as pl
from jax.experimental.pallas import tpu as pltpu
from jax.sharding import PartitionSpec as P


LANES = 128
CHUNK = 32
BLOCK = 256
PIECE = 16
HALF_TOP = 65504.0


def passed_along(value, axis, steps):
    count = lax.axis_size(axis)
    pairs = [(source, (source + steps) % count) for source in range(count)]
    return lax.ppermute(value, axis, pairs)


def passed_both(value, row_steps, col_steps):
    rows, cols = lax.axis_size("row"), lax.axis_size("col")
    pairs = [
        (row * cols + col, (row + row_steps) % rows * cols + (col + col_steps) % cols)
        for row in range(rows)
        for col in range(cols)
    ]
    return lax.ppermute(value, ("row", "col"), pairs)


def dft_tables(size):
    index = np.arange(size, dtype=np.int64)
    wrapped = index[:, None] * index[None, :] % size
    angle = wrapped.astype(np.float32) * np.float32(2.0 * math.pi / size)
    norm = np.float32(1.0 / math.sqrt(size))
    cos_table = np.cos(angle.astype(np.float64)).astype(np.float32) * norm
    sin_table = -np.sin(angle.astype(np.float64)).astype(np.float32) * norm
    tables = (cos_table, sin_table, -sin_table)
    return tuple(jnp.asarray(table, jnp.bfloat16) for table in tables)


def narrowed(value, bound):
    return (value * (HALF_TOP / bound)).astype(jnp.float16)


def widened(value, bound):
    return value.astype(jnp.float32) * (bound / HALF_TOP)


def table_copies(tables, left, right, sems):
    cos_table, sin_table, negative = tables
    size = cos_table.shape[-1]
    low, high = pl.ds(0, size), pl.ds(size, size)
    moves = [
        (cos_table, left, low, low),
        (cos_table, left, high, high),
        (negative, left, low, high),
        (sin_table, left, high, low),
        (cos_table, right, low, low),
        (cos_table, right, high, high),
        (sin_table, right, low, high),
        (negative, right, high, low),
    ]
    return [
        pltpu.make_async_copy(source, table.at[rows, columns], sems.at[index])
        for index, (source, table, rows, columns) in enumerate(moves)
    ]


def region_copies(pieces, region, sems):
    middle, west, _ = pieces[:3]
    rows, cols, edge = middle.shape[1], middle.shape[2], west.shape[2]
    center, right = edge // LANES, (edge + cols) // LANES
    half = center + edge // LANES
    places = [(1, center), (1, 0), (1, right)]
    places += [(0, half), (2, half), (0, center), (2, center)]
    places += [(0, 0), (2, 0), (0, right), (2, right)]
    copies = []
    for piece, (target, first) in zip(pieces, places):
        for block in range(piece.shape[2] // LANES):
            copies.append(
                pltpu.make_async_copy(
                    piece.at[:, :, pl.ds(block * LANES, LANES)],
                    region.at[:, first + block, pl.ds(target * rows, rows)],
                    sems.at[len(copies)],
                )
            )
    return copies


def forward_kernel(offs, *refs):
    pieces, tables, refs = refs[:11], refs[11:14], refs[14:]
    ill, far, patch, region, left, right, wave, half, region_sems, table_sems = refs
    slot = pl.program_id(0)
    size = ill.shape[-1]
    row = offs[slot, 0]
    lane_shift = offs[slot, 1] % LANES
    lane = lax.broadcasted_iota(jnp.int32, (CHUNK, LANES), 1)
    blocks = size // LANES

    @pl.when(slot == 0)
    def _():
        region_moves = region_copies(pieces, region, region_sems)
        table_moves = table_copies(tables, left, right, table_sems)
        for move in region_moves:
            move.start()
        for move in region_moves:
            move.wait()
        for move in table_moves:
            move.start()

    def extract(step, carry):
        at = pl.multiple_of(step * CHUNK, CHUNK)
        last = [None, None]
        for block in range(blocks + 1):
            now = [
                pltpu.roll(
                    region[plane, slot + block, pl.ds(row + at, CHUNK), :],
                    (LANES - lane_shift) % LANES,
                    axis=1,
                )
                for plane in range(2)
            ]
            if block > 0:
                to = slice((block - 1) * LANES, block * LANES)
                spec_real, spec_imag = (
                    jnp.where(lane < LANES - lane_shift, last[plane], now[plane])
                    for plane in range(2)
                )
                patch[0, 0, pl.ds(at, CHUNK), to] = spec_real
                patch[0, 1, pl.ds(at, CHUNK), to] = spec_imag
                ill_real = ill[0, pl.ds(at, CHUNK), to]
                ill_imag = ill[1, pl.ds(at, CHUNK), to]
                wave[pl.ds(at, CHUNK), to] = (
                    ill_real * spec_real - ill_imag * spec_imag
                ).astype(jnp.bfloat16)
                wave[pl.ds(size + at, CHUNK), to] = (
                    ill_real * spec_imag + ill_imag * spec_real
                ).astype(jnp.bfloat16)
            last = now
        return carry

    lax.fori_loop(0, size // CHUNK, extract, 0, unroll=8)

    @pl.when(slot == 0)
    def _():
        for move in table_copies(tables, left, right, table_sems):
            move.wait()

    for block in range(size // BLOCK):
        to = slice(block * BLOCK, (block + 1) * BLOCK)
        also = slice(size + block * BLOCK, size + (block + 1) * BLOCK)
        product = jnp.dot(left[...], wave[:, to], preferred_element_type=jnp.float32)
        half[:, to] = product[:size].astype(jnp.bfloat16)
        half[:, also] = product[size:].astype(jnp.bfloat16)
    for plane in range(2):
        for block in range(size // BLOCK):
            to = slice(block * BLOCK, (block + 1) * BLOCK)
            of = slice(plane * size + block * BLOCK, plane * size + (block + 1) * BLOCK)
            far[0, plane, :, to] = jnp.dot(
                half[...], right[:, of], preferred_element_type=jnp.float32
            )


def backward_kernel(
    offs,
    order,
    far,
    patch,
    amp,
    ill,
    cos_table,
    sin_table,
    negative,
    accum,
    sums,
    corr,
    back,
    change,
    left,
    right,
    inverse,
    table_sems,
):
    slot = pl.program_id(0)
    size = ill.shape[-1]
    modules = size // amp.shape[3]
    senders = amp.shape[0]
    row = offs[slot, 0]
    lane_shift = offs[slot, 1] % LANES
    tables = (cos_table, sin_table, negative)
    blocks = size // LANES
    height = amp.shape[3]
    per = amp.shape[2]

    @pl.when(slot == 0)
    def _():
        for move in table_copies(tables, left, right, table_sems):
            move.start()
        sums[...] = jnp.zeros_like(sums)

        def clear(step, carry):
            at = pl.multiple_of(step * CHUNK, CHUNK)
            accum[:, :, pl.ds(at, CHUNK), :] = jnp.zeros(
                (2, accum.shape[1], CHUNK, LANES), jnp.float32
            )
            return carry

        lax.fori_loop(0, accum.shape[2] // CHUNK, clear, 0)

        def invert(module, carry):
            inverse[order[module]] = module
            return carry

        lax.fori_loop(0, modules, invert, 0)

    def correct(band, carry):
        at = pl.multiple_of(band * height, height)
        module = inverse[band]
        rows = pl.ds(at, height)
        far_real = far[0, 0, rows, :]
        far_imag = far[0, 1, rows, :]
        sender = (module // per + senders - 1) % senders
        level = amp[sender, 0, module % per].astype(jnp.float32)
        inverse_size = lax.rsqrt(far_real * far_real + far_imag * far_imag)
        factor = level * jnp.minimum(inverse_size, 4.0) - 1.0
        corr[rows, :] = (factor * far_real).astype(jnp.bfloat16)
        corr[pl.ds(size + at, height), :] = (factor * far_imag).astype(jnp.bfloat16)
        return carry

    lax.fori_loop(0, modules, correct, 0, unroll=8)

    @pl.when(slot == 0)
    def _():
        for move in table_copies(tables, left, right, table_sems):
            move.wait()

    for block in range(size // BLOCK):
        to = slice(block * BLOCK, (block + 1) * BLOCK)
        also = slice(size + block * BLOCK, size + (block + 1) * BLOCK)
        product = jnp.dot(right[...], corr[:, to], preferred_element_type=jnp.float32)
        back[:, to] = product[:size].astype(jnp.bfloat16)
        back[:, also] = product[size:].astype(jnp.bfloat16)
    for plane in range(2):
        for block in range(size // BLOCK):
            to = slice(block * BLOCK, (block + 1) * BLOCK)
            of = slice(plane * size + block * BLOCK, plane * size + (block + 1) * BLOCK)
            change[plane, :, to] = jnp.dot(
                back[...], left[:, of], preferred_element_type=jnp.float32
            )

    lane = lax.broadcasted_iota(jnp.int32, (CHUNK, LANES), 1)

    def spread(step, carry):
        at = pl.multiple_of(step * CHUNK, CHUNK)
        rows = pl.ds(at, CHUNK)
        last = [jnp.zeros((CHUNK, LANES), jnp.float32)] * 2
        for block in range(blocks + 1):
            if block < blocks:
                to = slice(block * LANES, (block + 1) * LANES)
                chg_real = change[0, rows, to]
                chg_imag = change[1, rows, to]
                spec_real = patch[0, 0, rows, to]
                spec_imag = patch[0, 1, rows, to]
                ill_real = ill[0, rows, to]
                ill_imag = ill[1, rows, to]
                places = pl.ds(step * (CHUNK // PIECE), CHUNK // PIECE)
                pieces = (CHUNK // PIECE, PIECE, LANES)
                sums[block, places, 0] += (spec_real * chg_real + spec_imag * chg_imag).reshape(
                    pieces
                )
                sums[block, places, 1] += (spec_real * chg_imag - spec_imag * chg_real).reshape(
                    pieces
                )
                sums[block, places, 2] += (spec_real * spec_real + spec_imag * spec_imag).reshape(
                    pieces
                )
                grads = (
                    ill_real * chg_real + ill_imag * chg_imag,
                    ill_real * chg_imag - ill_imag * chg_real,
                )
                now = [pltpu.roll(grad, lane_shift, axis=1) for grad in grads]
            else:
                now = [jnp.zeros((CHUNK, LANES), jnp.float32)] * 2
            for plane in range(2):
                placed = jnp.where(lane < lane_shift, last[plane], now[plane])
                accum[plane, slot + block, pl.ds(row + at, CHUNK), :] += placed
            last = now
        return carry

    lax.fori_loop(0, size // CHUNK, spread, 0, unroll=8)


def whole(shape):
    return pl.BlockSpec(shape, lambda slot, *refs: (0,) * len(shape))


def once(shape):
    return pl.BlockSpec(
        shape, lambda slot, *refs: (0,) * len(shape), pipeline_mode=pl.Buffered(1)
    )


def one_slot(shape):
    return pl.BlockSpec((1,) + shape, lambda slot, *refs: (slot,) + (0,) * len(shape))


def run_forward(offs, pieces, tables, ill):
    slots = offs.shape[0]
    size = ill.shape[-1]
    rows, cols, edge = pieces[0].shape[1], pieces[0].shape[2], pieces[1].shape[2]
    planes = jax.ShapeDtypeStruct((slots, 2, size, size), jnp.float32)
    return pl.pallas_call(
        forward_kernel,
        grid_spec=pltpu.PrefetchScalarGridSpec(
            num_scalar_prefetch=1,
            grid=(slots,),
            in_specs=[pl.BlockSpec(memory_space=pltpu.HBM)] * (len(pieces) + len(tables))
            + [once(ill.shape)],
            out_specs=[
                one_slot((2, size, size)),
                one_slot((2, size, size)),
            ],
            scratch_shapes=[
                pltpu.VMEM((2, (cols + 2 * edge) // LANES, 3 * rows, LANES), jnp.float32),
                pltpu.VMEM((2 * size, 2 * size), jnp.bfloat16),
                pltpu.VMEM((2 * size, 2 * size), jnp.bfloat16),
                pltpu.VMEM((2 * size, size), jnp.bfloat16),
                pltpu.VMEM((size, 2 * size), jnp.bfloat16),
                pltpu.SemaphoreType.DMA((24,)),
                pltpu.SemaphoreType.DMA((8,)),
            ],
        ),
        out_shape=[planes, planes],
        cost_estimate=pl.CostEstimate(
            flops=slots * 16 * size**3, bytes_accessed=30_000_000, transcendentals=0
        ),
        compiler_params=pltpu.CompilerParams(vmem_limit_bytes=67_000_000),
        name="forward",
    )(offs, *pieces, *tables, ill)


def run_backward(offs, order, far, patch, amp, ill, tables, region_shape):
    slots = offs.shape[0]
    size = ill.shape[-1]
    senders, _, per, height, _ = amp.shape
    sums_shape = (size // LANES, size // PIECE, 3, PIECE, LANES)
    return pl.pallas_call(
        backward_kernel,
        grid_spec=pltpu.PrefetchScalarGridSpec(
            num_scalar_prefetch=2,
            grid=(slots,),
            in_specs=[
                one_slot((2, size, size)),
                one_slot((2, size, size)),
                pl.BlockSpec(
                    (senders, 1, per, height, size), lambda slot, *refs: (0, slot, 0, 0, 0)
                ),
                once(ill.shape),
            ]
            + [pl.BlockSpec(memory_space=pltpu.HBM)] * len(tables),
            out_specs=[whole(region_shape), whole(sums_shape)],
            scratch_shapes=[
                pltpu.VMEM((2 * size, size), jnp.bfloat16),
                pltpu.VMEM((size, 2 * size), jnp.bfloat16),
                pltpu.VMEM((2, size, size), jnp.float32),
                pltpu.VMEM((2 * size, 2 * size), jnp.bfloat16),
                pltpu.VMEM((2 * size, 2 * size), jnp.bfloat16),
                pltpu.SMEM((senders * per,), jnp.int32),
                pltpu.SemaphoreType.DMA((8,)),
            ],
        ),
        out_shape=[
            jax.ShapeDtypeStruct(region_shape, jnp.float32),
            jax.ShapeDtypeStruct(sums_shape, jnp.float32),
        ],
        cost_estimate=pl.CostEstimate(
            flops=slots * 16 * size**3, bytes_accessed=30_000_000, transcendentals=0
        ),
        compiler_params=pltpu.CompilerParams(vmem_limit_bytes=67_000_000),
        name="backward",
    )(offs, order, far, patch, amp, ill, *tables)


def unpack_kernel(packed, out):
    size = out.shape[1]
    per = size // PIECE
    for column in range(size // LANES):
        for plane in range(2):
            part = packed[column * per : (column + 1) * per, plane * PIECE : (plane + 1) * PIECE]
            out[plane, :, column * LANES : (column + 1) * LANES] = part.reshape(size, LANES)


def unpacked(packed, size):
    return pl.pallas_call(
        unpack_kernel,
        in_specs=[pl.BlockSpec(memory_space=pltpu.VMEM)],
        out_specs=pl.BlockSpec(memory_space=pltpu.VMEM),
        out_shape=jax.ShapeDtypeStruct((2, size, size), jnp.float32),
        compiler_params=pltpu.CompilerParams(vmem_limit_bytes=16 * 1024 * 1024),
        name="unpack",
    )(packed)


def spread_out(value):
    return lax.all_to_all(value, ("row", "col"), split_axis=0, concat_axis=0, tiled=True)


def shards(measured, module_row, scan_offsets, specimen, illumination):
    slots = scan_offsets.shape[2]
    size = illumination.shape[-1]
    tile_rows = specimen.shape[1]
    tile_cols = specimen.shape[2]
    senders = lax.axis_size("row")
    devices = senders * lax.axis_size("col")
    per, height = measured.shape[1], measured.shape[2]
    late = slots // 2
    edge = tile_cols // 2
    grouped = measured.reshape(senders, slots, per, height, size)
    right_half = specimen[:, :, edge:]
    again, _ = lax.optimization_barrier((specimen, right_half))
    halves = {"left": again[:, :, :edge], "right": right_half}
    rows = []
    for name in ("right", "left"):
        rows.append(passed_along(halves[name], "row", 1))
        rows.append(passed_along(halves[name], "row", -1))
    early_offs = passed_along(scan_offsets[0, 0, :late], "row", 1)
    late_offs = passed_both(scan_offsets[0, 0, late:], 1, 1)
    offs = jnp.concatenate([late_offs, early_offs], axis=0)
    moved = passed_along(grouped[:, late:], "col", 1)
    west = passed_along(halves["right"], "col", 1)
    east = passed_along(halves["left"], "col", -1)
    levels = jnp.concatenate([moved, grouped[:, :late]], axis=1)
    tables = dft_tables(size)
    lane = lax.broadcasted_iota(jnp.int32, (devices, 1, LANES), 2)
    stats = jnp.where(
        lane < LANES // 2, jnp.max(jnp.abs(specimen)), jnp.sum(specimen * specimen)
    )
    peaks = spread_out(stats)
    outers = []
    for index, (steps, name) in enumerate(((1, "west"), (1, "west"), (-1, "east"), (-1, "east"))):
        outers.append(passed_along(rows[index], "col", steps))
    levels, probe, _ = lax.optimization_barrier((levels, illumination, tuple(rows)))
    ill_power = jnp.sum(probe * probe)
    ill_peak = jnp.maximum(jnp.max(jnp.abs(probe)), 1e-8)
    arrived = lax.all_to_all(
        levels,
        "row",
        split_axis=0,
        concat_axis=0,
        tiled=True,
        axis_index_groups=[[(sender + 1) % senders for sender in range(senders)]],
    )
    peak = jnp.maximum(jnp.max(peaks[:, :, : LANES // 2]), 1e-12)
    power = jnp.max(peaks[:, :, LANES // 2 :])
    modulus = 1.5 * peak
    energy = jnp.minimum(
        modulus * jnp.sqrt(ill_power), 1.5 * ill_peak * jnp.sqrt(6.0 * power)
    )
    change_bound = 9.0 * jnp.maximum(energy, 1e-20)
    grad_bound = 24.0 * ill_peak * change_bound
    sum_bound = slots * modulus * change_bound
    density_bound = slots * modulus * modulus
    step_bound = math.sqrt(slots * devices) * change_bound
    bounds = (grad_bound, sum_bound, density_bound, step_bound)
    offs, bounds = lax.optimization_barrier((offs, bounds))
    grad_bound, sum_bound, density_bound, step_bound = bounds
    pieces = (specimen, west, east, *rows, *outers)
    far, patch = run_forward(offs, pieces, tables, illumination)
    region_shape = (2, (tile_cols + 2 * edge) // LANES, 3 * tile_rows, LANES)
    accum, sums = run_backward(
        offs, module_row, far, patch, arrived, illumination, tables, region_shape
    )
    side = edge // LANES
    to_west = narrowed(accum[:, :side], grad_bound)
    to_east = narrowed(accum[:, -side:], grad_bound)
    from_east = passed_along(to_west, "col", -1)
    from_west = passed_along(to_east, "col", 1)
    sums = sums.reshape(devices, 3 * PIECE, LANES)
    line = lax.broadcasted_iota(jnp.int32, (1, 3 * PIECE, 1), 1)
    bounds = jnp.where(line < 2 * PIECE, sum_bound, density_bound)
    packed = narrowed(sums, bounds)
    parts = spread_out(packed)
    column = accum[:, side:-side] + jnp.concatenate(
        [widened(from_west, grad_bound), widened(from_east, grad_bound)], axis=1
    )
    to_upper = narrowed(column[:, :, :tile_rows], grad_bound)
    to_lower = narrowed(column[:, :, 2 * tile_rows :], grad_bound)
    from_lower = passed_along(to_upper, "row", -1)
    from_upper = passed_along(to_lower, "row", 1)
    total = jnp.sum(widened(parts, bounds), axis=0)
    mine = total[: 2 * PIECE].reshape(2, PIECE, LANES) / jnp.sqrt(total[2 * PIECE :] + 1e-06)
    mine = narrowed(mine, step_bound).reshape(1, 2 * PIECE, LANES)
    copies = jnp.broadcast_to(mine, (devices, 2 * PIECE, LANES))
    result = spread_out(copies)
    illumination_step = unpacked(widened(result, step_bound), size)
    middle = (
        column[:, :, tile_rows : 2 * tile_rows]
        + widened(from_lower, grad_bound)
        + widened(from_upper, grad_bound)
    )
    specimen_step = middle.swapaxes(1, 2).reshape(2, tile_rows, tile_cols)
    return (specimen_step, illumination_step)


def solution(mesh):
    return jax.shard_map(
        shards,
        mesh=mesh,
        in_specs=(
            P("col", "row", None, None),
            P(),
            P("row", "col", None, None),
            P(None, "row", "col"),
            P(),
        ),
        out_specs=(P(None, "row", "col"), P()),
        check_vma=False,
    )
```

```python
import math

import jax
import jax.numpy as jnp
import numpy as np
from jax import lax
from jax.experimental import pallas as pl
from jax.experimental.pallas import tpu as pltpu
from jax.sharding import PartitionSpec as P


LANES = 128
CHUNK = 32
BLOCK = 256
PIECE = 16
HALF_TOP = 65504.0


def passed_along(value, axis, steps):
    count = lax.axis_size(axis)
    pairs = [(source, (source + steps) % count) for source in range(count)]
    return lax.ppermute(value, axis, pairs)


def dft_tables(size):
    index = np.arange(size, dtype=np.int64)
    wrapped = index[:, None] * index[None, :] % size
    angle = wrapped.astype(np.float32) * np.float32(2.0 * math.pi / size)
    norm = np.float32(1.0 / math.sqrt(size))
    cos_table = np.cos(angle.astype(np.float64)).astype(np.float32) * norm
    sin_table = -np.sin(angle.astype(np.float64)).astype(np.float32) * norm
    tables = (cos_table, sin_table, -sin_table)
    return tuple(jnp.asarray(table, jnp.bfloat16) for table in tables)


def narrowed(value, bound):
    return (value * (HALF_TOP / bound)).astype(jnp.float16)


def widened(value, bound):
    return value.astype(jnp.float32) * (bound / HALF_TOP)


def table_copies(tables, left, right, sems):
    cos_table, sin_table, negative = tables
    size = cos_table.shape[-1]
    low, high = pl.ds(0, size), pl.ds(size, size)
    moves = [
        (cos_table, left, low, low),
        (cos_table, left, high, high),
        (negative, left, low, high),
        (sin_table, left, high, low),
        (cos_table, right, low, low),
        (cos_table, right, high, high),
        (sin_table, right, low, high),
        (negative, right, high, low),
    ]
    return [
        pltpu.make_async_copy(source, table.at[rows, columns], sems.at[index])
        for index, (source, table, rows, columns) in enumerate(moves)
    ]


def region_copies(pieces, region, sems):
    middle, west, _ = pieces[:3]
    rows, cols, edge = middle.shape[1], middle.shape[2], west.shape[2]
    center, right = edge // LANES, (edge + cols) // LANES
    half = center + edge // LANES
    places = [(1, center), (1, 0), (1, right)]
    places += [(0, half), (2, half), (0, center), (2, center)]
    places += [(0, 0), (2, 0), (0, right), (2, right)]
    copies = []
    for piece, (target, first) in zip(pieces, places):
        for block in range(piece.shape[2] // LANES):
            copies.append(
                pltpu.make_async_copy(
                    piece.at[:, :, pl.ds(block * LANES, LANES)],
                    region.at[:, first + block, pl.ds(target * rows, rows)],
                    sems.at[len(copies)],
                )
            )
    return copies


def forward_kernel(offs, *refs):
    pieces, tables, refs = refs[:11], refs[11:14], refs[14:]
    ill, far, patch, region, left, right, wave, half, region_sems, table_sems = refs
    slot = pl.program_id(0)
    size = ill.shape[-1]
    row = offs[slot, 0]
    lane_shift = offs[slot, 1] % LANES
    lane = lax.broadcasted_iota(jnp.int32, (CHUNK, LANES), 1)
    blocks = size // LANES

    @pl.when(slot == 0)
    def _():
        region_moves = region_copies(pieces, region, region_sems)
        table_moves = table_copies(tables, left, right, table_sems)
        for move in region_moves:
            move.start()
        for move in region_moves:
            move.wait()
        for move in table_moves:
            move.start()

    def extract(step, carry):
        at = pl.multiple_of(step * CHUNK, CHUNK)
        last = [None, None]
        for block in range(blocks + 1):
            now = [
                pltpu.roll(
                    region[plane, slot + block, pl.ds(row + at, CHUNK), :],
                    (LANES - lane_shift) % LANES,
                    axis=1,
                )
                for plane in range(2)
            ]
            if block > 0:
                to = slice((block - 1) * LANES, block * LANES)
                spec_real, spec_imag = (
                    jnp.where(lane < LANES - lane_shift, last[plane], now[plane])
                    for plane in range(2)
                )
                patch[0, 0, pl.ds(at, CHUNK), to] = spec_real
                patch[0, 1, pl.ds(at, CHUNK), to] = spec_imag
                ill_real = ill[0, pl.ds(at, CHUNK), to]
                ill_imag = ill[1, pl.ds(at, CHUNK), to]
                wave[pl.ds(at, CHUNK), to] = (
                    ill_real * spec_real - ill_imag * spec_imag
                ).astype(jnp.bfloat16)
                wave[pl.ds(size + at, CHUNK), to] = (
                    ill_real * spec_imag + ill_imag * spec_real
                ).astype(jnp.bfloat16)
            last = now
        return carry

    lax.fori_loop(0, size // CHUNK, extract, 0, unroll=8)

    @pl.when(slot == 0)
    def _():
        for move in table_copies(tables, left, right, table_sems):
            move.wait()

    for block in range(size // BLOCK):
        to = slice(block * BLOCK, (block + 1) * BLOCK)
        also = slice(size + block * BLOCK, size + (block + 1) * BLOCK)
        product = jnp.dot(left[...], wave[:, to], preferred_element_type=jnp.float32)
        half[:, to] = product[:size].astype(jnp.bfloat16)
        half[:, also] = product[size:].astype(jnp.bfloat16)
    for plane in range(2):
        for block in range(size // BLOCK):
            to = slice(block * BLOCK, (block + 1) * BLOCK)
            of = slice(plane * size + block * BLOCK, plane * size + (block + 1) * BLOCK)
            far[0, plane, :, to] = jnp.dot(
                half[...], right[:, of], preferred_element_type=jnp.float32
            )


def backward_kernel(
    offs,
    order,
    far,
    patch,
    amp,
    ill,
    cos_table,
    sin_table,
    negative,
    accum,
    sums,
    corr,
    back,
    change,
    left,
    right,
    inverse,
    table_sems,
):
    slot = pl.program_id(0)
    size = ill.shape[-1]
    modules = size // amp.shape[3]
    senders = amp.shape[0]
    row = offs[slot, 0]
    lane_shift = offs[slot, 1] % LANES
    tables = (cos_table, sin_table, negative)
    blocks = size // LANES
    height = amp.shape[3]
    per = amp.shape[2]

    @pl.when(slot == 0)
    def _():
        for move in table_copies(tables, left, right, table_sems):
            move.start()
        sums[...] = jnp.zeros_like(sums)

        def clear(step, carry):
            at = pl.multiple_of(step * CHUNK, CHUNK)
            accum[:, :, pl.ds(at, CHUNK), :] = jnp.zeros(
                (2, accum.shape[1], CHUNK, LANES), jnp.float32
            )
            return carry

        lax.fori_loop(0, accum.shape[2] // CHUNK, clear, 0)

        def invert(module, carry):
            inverse[order[module]] = module
            return carry

        lax.fori_loop(0, modules, invert, 0)

    def correct(band, carry):
        at = pl.multiple_of(band * height, height)
        module = inverse[band]
        rows = pl.ds(at, height)
        far_real = far[0, 0, rows, :]
        far_imag = far[0, 1, rows, :]
        sender = (module // per + senders - 1) % senders
        level = amp[sender, 0, module % per].astype(jnp.float32)
        inverse_size = lax.rsqrt(far_real * far_real + far_imag * far_imag)
        factor = level * jnp.minimum(inverse_size, 4.0) - 1.0
        corr[rows, :] = (factor * far_real).astype(jnp.bfloat16)
        corr[pl.ds(size + at, height), :] = (factor * far_imag).astype(jnp.bfloat16)
        return carry

    lax.fori_loop(0, modules, correct, 0, unroll=8)

    @pl.when(slot == 0)
    def _():
        for move in table_copies(tables, left, right, table_sems):
            move.wait()

    for block in range(size // BLOCK):
        to = slice(block * BLOCK, (block + 1) * BLOCK)
        also = slice(size + block * BLOCK, size + (block + 1) * BLOCK)
        product = jnp.dot(right[...], corr[:, to], preferred_element_type=jnp.float32)
        back[:, to] = product[:size].astype(jnp.bfloat16)
        back[:, also] = product[size:].astype(jnp.bfloat16)
    for plane in range(2):
        for block in range(size // BLOCK):
            to = slice(block * BLOCK, (block + 1) * BLOCK)
            of = slice(plane * size + block * BLOCK, plane * size + (block + 1) * BLOCK)
            change[plane, :, to] = jnp.dot(
                back[...], left[:, of], preferred_element_type=jnp.float32
            )

    lane = lax.broadcasted_iota(jnp.int32, (CHUNK, LANES), 1)

    def spread(step, carry):
        at = pl.multiple_of(step * CHUNK, CHUNK)
        rows = pl.ds(at, CHUNK)
        last = [jnp.zeros((CHUNK, LANES), jnp.float32)] * 2
        for block in range(blocks + 1):
            if block < blocks:
                to = slice(block * LANES, (block + 1) * LANES)
                chg_real = change[0, rows, to]
                chg_imag = change[1, rows, to]
                spec_real = patch[0, 0, rows, to]
                spec_imag = patch[0, 1, rows, to]
                ill_real = ill[0, rows, to]
                ill_imag = ill[1, rows, to]
                places = pl.ds(step * (CHUNK // PIECE), CHUNK // PIECE)
                pieces = (CHUNK // PIECE, PIECE, LANES)
                sums[block, places, 0] += (spec_real * chg_real + spec_imag * chg_imag).reshape(
                    pieces
                )
                sums[block, places, 1] += (spec_real * chg_imag - spec_imag * chg_real).reshape(
                    pieces
                )
                sums[block, places, 2] += (spec_real * spec_real + spec_imag * spec_imag).reshape(
                    pieces
                )
                grads = (
                    ill_real * chg_real + ill_imag * chg_imag,
                    ill_real * chg_imag - ill_imag * chg_real,
                )
                now = [pltpu.roll(grad, lane_shift, axis=1) for grad in grads]
            else:
                now = [jnp.zeros((CHUNK, LANES), jnp.float32)] * 2
            for plane in range(2):
                placed = jnp.where(lane < lane_shift, last[plane], now[plane])
                accum[plane, slot + block, pl.ds(row + at, CHUNK), :] += placed
            last = now
        return carry

    lax.fori_loop(0, size // CHUNK, spread, 0, unroll=8)


def whole(shape):
    return pl.BlockSpec(shape, lambda slot, *refs: (0,) * len(shape))


def once(shape):
    return pl.BlockSpec(
        shape, lambda slot, *refs: (0,) * len(shape), pipeline_mode=pl.Buffered(1)
    )


def one_slot(shape):
    return pl.BlockSpec((1,) + shape, lambda slot, *refs: (slot,) + (0,) * len(shape))


def run_forward(offs, pieces, tables, ill):
    slots = offs.shape[0]
    size = ill.shape[-1]
    rows, cols, edge = pieces[0].shape[1], pieces[0].shape[2], pieces[1].shape[2]
    planes = jax.ShapeDtypeStruct((slots, 2, size, size), jnp.float32)
    return pl.pallas_call(
        forward_kernel,
        grid_spec=pltpu.PrefetchScalarGridSpec(
            num_scalar_prefetch=1,
            grid=(slots,),
            in_specs=[pl.BlockSpec(memory_space=pltpu.HBM)] * (len(pieces) + len(tables))
            + [once(ill.shape)],
            out_specs=[
                one_slot((2, size, size)),
                one_slot((2, size, size)),
            ],
            scratch_shapes=[
                pltpu.VMEM((2, (cols + 2 * edge) // LANES, 3 * rows, LANES), jnp.float32),
                pltpu.VMEM((2 * size, 2 * size), jnp.bfloat16),
                pltpu.VMEM((2 * size, 2 * size), jnp.bfloat16),
                pltpu.VMEM((2 * size, size), jnp.bfloat16),
                pltpu.VMEM((size, 2 * size), jnp.bfloat16),
                pltpu.SemaphoreType.DMA((24,)),
                pltpu.SemaphoreType.DMA((8,)),
            ],
        ),
        out_shape=[planes, planes],
        cost_estimate=pl.CostEstimate(
            flops=slots * 16 * size**3, bytes_accessed=30_000_000, transcendentals=0
        ),
        compiler_params=pltpu.CompilerParams(vmem_limit_bytes=67_000_000),
        name="forward",
    )(offs, *pieces, *tables, ill)


def run_backward(offs, order, far, patch, amp, ill, tables, region_shape):
    slots = offs.shape[0]
    size = ill.shape[-1]
    senders, _, per, height, _ = amp.shape
    sums_shape = (size // LANES, size // PIECE, 3, PIECE, LANES)
    return pl.pallas_call(
        backward_kernel,
        grid_spec=pltpu.PrefetchScalarGridSpec(
            num_scalar_prefetch=2,
            grid=(slots,),
            in_specs=[
                one_slot((2, size, size)),
                one_slot((2, size, size)),
                pl.BlockSpec(
                    (senders, 1, per, height, size), lambda slot, *refs: (0, slot, 0, 0, 0)
                ),
                once(ill.shape),
            ]
            + [pl.BlockSpec(memory_space=pltpu.HBM)] * len(tables),
            out_specs=[whole(region_shape), whole(sums_shape)],
            scratch_shapes=[
                pltpu.VMEM((2 * size, size), jnp.bfloat16),
                pltpu.VMEM((size, 2 * size), jnp.bfloat16),
                pltpu.VMEM((2, size, size), jnp.float32),
                pltpu.VMEM((2 * size, 2 * size), jnp.bfloat16),
                pltpu.VMEM((2 * size, 2 * size), jnp.bfloat16),
                pltpu.SMEM((senders * per,), jnp.int32),
                pltpu.SemaphoreType.DMA((8,)),
            ],
        ),
        out_shape=[
            jax.ShapeDtypeStruct(region_shape, jnp.float32),
            jax.ShapeDtypeStruct(sums_shape, jnp.float32),
        ],
        cost_estimate=pl.CostEstimate(
            flops=slots * 16 * size**3, bytes_accessed=30_000_000, transcendentals=0
        ),
        compiler_params=pltpu.CompilerParams(vmem_limit_bytes=67_000_000),
        name="backward",
    )(offs, order, far, patch, amp, ill, *tables)


def unpack_kernel(packed, out):
    size = out.shape[1]
    per = size // PIECE
    for column in range(size // LANES):
        for plane in range(2):
            part = packed[column * per : (column + 1) * per, plane * PIECE : (plane + 1) * PIECE]
            out[plane, :, column * LANES : (column + 1) * LANES] = part.reshape(size, LANES)


def unpacked(packed, size):
    return pl.pallas_call(
        unpack_kernel,
        in_specs=[pl.BlockSpec(memory_space=pltpu.VMEM)],
        out_specs=pl.BlockSpec(memory_space=pltpu.VMEM),
        out_shape=jax.ShapeDtypeStruct((2, size, size), jnp.float32),
        compiler_params=pltpu.CompilerParams(vmem_limit_bytes=16 * 1024 * 1024),
        name="unpack",
    )(packed)


def spread_out(value):
    return lax.all_to_all(value, ("row", "col"), split_axis=0, concat_axis=0, tiled=True)


def shards(measured, module_row, scan_offsets, specimen, illumination):
    slots = scan_offsets.shape[2]
    size = illumination.shape[-1]
    tile_rows = specimen.shape[1]
    tile_cols = specimen.shape[2]
    senders = lax.axis_size("row")
    devices = senders * lax.axis_size("col")
    per, height = measured.shape[1], measured.shape[2]
    late = slots // 2
    edge = tile_cols // 2
    grouped = measured.reshape(senders, slots, per, height, size)
    right_half = specimen[:, :, edge:]
    again, _ = lax.optimization_barrier((specimen, right_half))
    halves = {"left": again[:, :, :edge], "right": right_half}
    rows = []
    for name in ("right", "left"):
        rows.append(passed_along(halves[name], "row", 1))
        rows.append(passed_along(halves[name], "row", -1))
    moved = passed_along(grouped[:, late:], "col", 1)
    west = passed_along(halves["right"], "col", 1)
    east = passed_along(halves["left"], "col", -1)
    levels = jnp.concatenate([moved, grouped[:, :late]], axis=1)
    tables = dft_tables(size)
    lane = lax.broadcasted_iota(jnp.int32, (1, 1, LANES), 2)
    count = 2 * slots
    own_offs = scan_offsets[0, 0].reshape(1, 1, count).astype(jnp.float32)
    stats = jnp.pad(own_offs, ((0, 0), (0, 0), (0, LANES - count)))
    stats = jnp.where(lane == count, jnp.max(jnp.abs(specimen)), stats)
    stats = jnp.where(lane == count + 1, jnp.sum(specimen * specimen), stats)
    peaks = spread_out(jnp.broadcast_to(stats, (devices, 1, LANES)))
    outers = []
    for index, (steps, name) in enumerate(((1, "west"), (1, "west"), (-1, "east"), (-1, "east"))):
        outers.append(passed_along(rows[index], "col", steps))
    levels, probe, _ = lax.optimization_barrier((levels, illumination, tuple(rows)))
    ill_power = jnp.sum(probe * probe)
    ill_peak = jnp.maximum(jnp.max(jnp.abs(probe)), 1e-8)
    arrived = lax.all_to_all(
        levels,
        "row",
        split_axis=0,
        concat_axis=0,
        tiled=True,
        axis_index_groups=[[(sender + 1) % senders for sender in range(senders)]],
    )
    most = jnp.max(peaks, axis=0)
    peak = jnp.maximum(most[0, count], 1e-12)
    power = most[0, count + 1]
    cols = lax.axis_size("col")
    col_index = lax.axis_index("col")
    above = (lax.axis_index("row") + senders - 1) % senders * cols
    near = lax.dynamic_slice(peaks, (above + col_index, 0, 0), (1, 1, LANES))
    far_off = above + (col_index + cols - 1) % cols
    far_off = lax.dynamic_slice(peaks, (far_off, 0, 0), (1, 1, LANES))
    offs = jnp.concatenate(
        [far_off[0, 0, 2 * late : count], near[0, 0, : 2 * late]]
    ).astype(jnp.int32).reshape(slots, 2)
    modulus = 1.5 * peak
    energy = jnp.minimum(
        modulus * jnp.sqrt(ill_power), 1.5 * ill_peak * jnp.sqrt(6.0 * power)
    )
    change_bound = 9.0 * jnp.maximum(energy, 1e-20)
    grad_bound = 24.0 * ill_peak * change_bound
    sum_bound = slots * modulus * change_bound
    density_bound = slots * modulus * modulus
    step_bound = math.sqrt(slots * devices) * change_bound
    bounds = (grad_bound, sum_bound, density_bound, step_bound)
    offs, bounds = lax.optimization_barrier((offs, bounds))
    grad_bound, sum_bound, density_bound, step_bound = bounds
    pieces = (specimen, west, east, *rows, *outers)
    far, patch = run_forward(offs, pieces, tables, illumination)
    region_shape = (2, (tile_cols + 2 * edge) // LANES, 3 * tile_rows, LANES)
    accum, sums = run_backward(
        offs, module_row, far, patch, arrived, illumination, tables, region_shape
    )
    side = edge // LANES
    to_west = narrowed(accum[:, :side], grad_bound)
    to_east = narrowed(accum[:, -side:], grad_bound)
    from_east = passed_along(to_west, "col", -1)
    from_west = passed_along(to_east, "col", 1)
    sums = sums.reshape(devices, 3 * PIECE, LANES)
    line = lax.broadcasted_iota(jnp.int32, (1, 3 * PIECE, 1), 1)
    bounds = jnp.where(line < 2 * PIECE, sum_bound, density_bound)
    packed = narrowed(sums, bounds)
    parts = spread_out(packed)
    column = accum[:, side:-side] + jnp.concatenate(
        [widened(from_west, grad_bound), widened(from_east, grad_bound)], axis=1
    )
    to_upper = narrowed(column[:, :, :tile_rows], grad_bound)
    to_lower = narrowed(column[:, :, 2 * tile_rows :], grad_bound)
    from_lower = passed_along(to_upper, "row", -1)
    from_upper = passed_along(to_lower, "row", 1)
    total = jnp.sum(widened(parts, bounds), axis=0)
    mine = total[: 2 * PIECE].reshape(2, PIECE, LANES) / jnp.sqrt(total[2 * PIECE :] + 1e-06)
    mine = narrowed(mine, step_bound).reshape(1, 2 * PIECE, LANES)
    copies = jnp.broadcast_to(mine, (devices, 2 * PIECE, LANES))
    result = spread_out(copies)
    illumination_step = unpacked(widened(result, step_bound), size)
    middle = (
        column[:, :, tile_rows : 2 * tile_rows]
        + widened(from_lower, grad_bound)
        + widened(from_upper, grad_bound)
    )
    specimen_step = middle.swapaxes(1, 2).reshape(2, tile_rows, tile_cols)
    return (specimen_step, illumination_step)


def solution(mesh):
    return jax.shard_map(
        shards,
        mesh=mesh,
        in_specs=(
            P("col", "row", None, None),
            P(),
            P("row", "col", None, None),
            P(None, "row", "col"),
            P(),
        ),
        out_specs=(P(None, "row", "col"), P()),
        check_vma=False,
    )
```
